256 devices in a mesh: ctx: 32 (over x_hi, z, core), tp: 8 (over y, x_lo).
Axes of the slice: x: 4 (x_hi: 2, x_lo: 2; x = x_hi * 2 + x_lo), y: 4, z: 8, core: 2. Of those that a mesh axis runs over, the one named last changes fastest.
Arguments:
- queries: bfloat16 [4096, 4096], P('ctx', 'tp'), may hold values from -6 to 6
- keys: bfloat16 [4096, 8192], P('ctx', 'tp'), may hold values from -6 to 6
- values: bfloat16 [4096, 8192], P('ctx', 'tp'), may hold values from -6 to 6
- beta_logit: float32 [32, 8192], P('tp', 'ctx'), may hold values from -8 to 8
- out_weight: bfloat16 [4096, 4096], P('ctx', 'tp'), may hold values from -0.1875 to 0.1875
- out_grad: bfloat16 [4096, 4096], P('ctx', 'tp'), may hold values from -6 to 6
Outputs:
- mixed: bfloat16 [4096, 4096], P('ctx', 'tp')
- query_grad: bfloat16 [4096, 4096], P('ctx', 'tp')
- key_grad: bfloat16 [4096, 8192], P('ctx', 'tp')
- value_grad: bfloat16 [4096, 8192], P('ctx', 'tp')
- logit_grad: float32 [32, 8192], P('tp', 'ctx')
- weight_grad: float32 [4096, 4096], P('ctx', 'tp')
The draws below stay inside these ranges and needn't reach their ends.
All inputs are finite; a program needn't handle non-finite values.
Results may differ from the reference program's by a relative error of at most 0.023.
Values may be sent and summed in bfloat16 or wider, within the bound.
No kernel may reach another device: no remote copies, remote signals or barrier semaphores. Data moves between devices by JAX's collectives and lax.ppermute only.
A program may use at most 128 MiB of HBM per device.

```python
import math
import jax
import jax.numpy as jnp
from jax import lax

D = 4096
HEADS = 32
DK = 128
L_DEV = 128
HV = 4096
SEQ = 4096
N_CTX = 32


def draw_beta_logit(key, part):
    key_centre = jax.random.fold_in(key, 11)
    key_noise = jax.random.fold_in(key, 12)
    centre = jax.random.uniform(key_centre, (HEADS, 1), jnp.float32, -2.5, 2.5)
    noise = jax.random.normal(key_noise, (HEADS, 2 * SEQ), jnp.float32)
    return jnp.clip(centre + noise, -8.0, 8.0).astype(jnp.float32)


def strengthened(values, own_key, source, target, parts, factor):
    owner, partner = [(jnp.arange(values.shape[axis_at]) // (values.shape[axis_at] // parts)).reshape([-1 if axis == axis_at else 1 for axis in range(values.ndim)]) for axis_at in (source, target)]
    chosen = jax.random.permutation(own_key, parts)[partner]
    strong = (owner == chosen) | (owner == (partner + parts // 2) % parts)
    return jnp.where(strong, factor * values, values)


def levels(rng, extent, split, low, top_value):
    gain = 1.0
    for dim, parts in split:
        draws = jax.random.uniform(jax.random.fold_in(jax.random.fold_in(rng, 6), dim), (parts,), jnp.float32, low / len(split), top_value / len(split))
        gain = gain * jnp.repeat(jnp.exp(draws), extent[dim] // parts).reshape((-1,) + (1,) * (len(extent) - 1 - dim))
    return gain


def gaussian(stream_key, extent, scale, most, cuts=(), held_as=jnp.bfloat16):
    values = scale * jax.random.normal(stream_key, extent, jnp.float32)
    if cuts:
        values = values * levels(stream_key, extent, cuts, -0.22, 0.18)
    return jnp.clip(values, -most, most).astype(held_as)


def bell_draw_with(key, shape, scale, bound, cuts, heavy, held_as=jnp.bfloat16):
    array = scale * jax.random.normal(key, shape, jnp.float32)
    if cuts:
        array = array * levels(key, shape, cuts, -0.22, 0.18)
    return jnp.clip(strengthened(array, jax.random.fold_in(key, 3), *heavy), -bound, bound).astype(held_as)


def setup_inputs(seed: int = 0) -> dict:
    splits = jax.random.split(jax.random.key(seed), 7)
    queries = gaussian(splits[0], (SEQ, HV), 1.0, 6.0, ((0, 32), (1, 8)))
    keys = gaussian(splits[1], (SEQ, 2 * HV), 1.0, 6.0, ((0, 32), (1, 8)))
    values = gaussian(splits[2], (SEQ, 2 * HV), 1.0, 6.0, ((0, 32), (1, 8)))
    beta_logit = draw_beta_logit(jax.random.fold_in(splits[6], 71), 0)
    out_weight = bell_draw_with(splits[4], (D, HV), HV ** -0.5, 0.1875, ((0, 32), (1, 8)), (1, 0, 32, 2.75))
    out_grad = bell_draw_with(splits[5], (SEQ, D), 1.0, 6.0, ((0, 32), (1, 8)), (0, 1, 32, 2.75))
    return {"queries": queries, "keys": keys, "values": values, "beta_logit": beta_logit, "out_weight": out_weight, "out_grad": out_grad}


def normalize(matrix):
    return matrix * lax.rsqrt(lax.optimization_barrier(jnp.sum(matrix * matrix, axis=-1, keepdims=True)) + 1e-06)

def mix_blocks(memory, query_heads, key_heads, value_heads, strength):
    head_count, length, width = query_heads.shape
    blocks = length // 64
    query_blk = query_heads.reshape(head_count, blocks, 64, width).transpose(1, 0, 2, 3)
    key_blk = key_heads.reshape(head_count, blocks, 128, width).transpose(1, 0, 2, 3)
    value_blk = value_heads.reshape(head_count, blocks, 128, value_heads.shape[2]).transpose(1, 0, 2, 3)
    gate_blk = strength.reshape(head_count, blocks, 128).transpose(1, 0, 2)
    row_ids = lax.broadcasted_iota(jnp.int32, (128, 128), 0)
    col_ids = lax.broadcasted_iota(jnp.int32, (128, 128), 1)
    below_diag = col_ids < row_ids
    token_ids = lax.broadcasted_iota(jnp.int32, (64, 128), 0)
    refl_ids = lax.broadcasted_iota(jnp.int32, (64, 128), 1)
    visible = refl_ids <= 2 * token_ids + 1
    identity_map = jnp.eye(128, dtype=jnp.float32)
    highest = lax.Precision.HIGHEST

    def advance(current, pieces):
        query_x, key_x, value_x, gate_x = pieces
        key_gram = jnp.einsum('hid,hjd->hij', key_x, key_x, precision=highest)
        system = identity_map + jnp.where(below_diag, gate_x[:, :, None] * key_gram, 0.0)
        right_side = gate_x[:, :, None] * (value_x - jnp.einsum('hid,hde->hie', key_x, current, precision=highest))
        updates = lax.linalg.triangular_solve(system, right_side, left_side=True, lower=True, unit_diagonal=True)
        scores = jnp.where(visible, jnp.einsum('htd,hid->hti', query_x, key_x, precision=highest), 0.0)
        result = jnp.einsum('htd,hde->hte', query_x, current, precision=highest)
        result = result + jnp.einsum('hti,hie->hte', scores, updates, precision=highest)
        current = current + jnp.einsum('hid,hie->hde', key_x, updates, precision=highest)
        return (current, result)
    memory, block_out = lax.scan(advance, memory, (query_blk, key_blk, value_blk, gate_blk))
    block_out = block_out.transpose(1, 0, 2, 3).reshape(head_count, length, block_out.shape[3])
    return (block_out, memory)

def group_map(memory, query_f, key_f, value_f, logits):
    head_count = logits.shape[0]
    length = query_f.shape[0]
    width = query_f.shape[1] // head_count
    query_heads = normalize(query_f.reshape(length, head_count, width)).transpose(1, 0, 2)
    key_heads = normalize(key_f.reshape(length, head_count, 2, width)).transpose(1, 0, 2, 3).reshape(head_count, 2 * length, width)
    value_heads = value_f.reshape(length, head_count, 2, width).transpose(1, 0, 2, 3).reshape(head_count, 2 * length, width)
    strength = 2.0 * jax.nn.sigmoid(logits)
    block_out, memory = mix_blocks(memory, query_heads, key_heads, value_heads, strength)
    return (block_out.transpose(1, 0, 2).reshape(length, head_count * width), memory)

def reference(queries, keys, values, beta_logit, out_weight, out_grad):
    query_f = queries.astype(jnp.float32)
    key_f = keys.astype(jnp.float32)
    value_f = values.astype(jnp.float32)
    start_state = jnp.zeros((HEADS, DK, DK), jnp.float32)

    def forward(query_in, key_in, value_in, logit_in):
        return group_map(start_state, query_in, key_in, value_in, logit_in)[0]
    heads_f, pull = jax.vjp(forward, query_f, key_f, value_f, beta_logit)
    heads_out = heads_f.astype(jnp.bfloat16)
    mixed = jnp.dot(heads_out.astype(jnp.float32), out_weight.T.astype(jnp.float32), preferred_element_type=jnp.float32).astype(jnp.bfloat16)
    head_grad = jnp.dot(out_grad.astype(jnp.float32), out_weight.astype(jnp.float32), preferred_element_type=jnp.float32)
    query_grad, key_grad, value_grad, logit_grad = pull(head_grad)
    scale_factor = 1.0 / math.sqrt(SEQ)

    def accumulate(total, pieces):
        grad_blk, heads_blk = pieces
        partial_term = jnp.dot(grad_blk.T.astype(jnp.float32), heads_blk.astype(jnp.float32), preferred_element_type=jnp.float32) * scale_factor
        partial_term = lax.optimization_barrier(partial_term.astype(jnp.bfloat16)).astype(jnp.float32)
        return (total + partial_term, None)
    weight_grad, _ = lax.scan(accumulate, jnp.zeros((D, HV), jnp.float32), (out_grad.reshape(N_CTX, L_DEV, D), heads_out.reshape(N_CTX, L_DEV, HV)))
    return (mixed, query_grad.astype(jnp.bfloat16), key_grad.astype(jnp.bfloat16), value_grad.astype(jnp.bfloat16), logit_grad, weight_grad)
```

```python
import functools
import math

import jax
import jax.numpy as jnp
from jax import lax
from jax.experimental import pallas as pl
from jax.experimental.pallas import tpu as pltpu
from jax.sharding import PartitionSpec as P

F32 = jnp.float32
BF16 = jnp.bfloat16
WIDTH = 128
PAIRS = 2 * WIDTH


def send(block, distance):
    devices = range(lax.axis_size("ctx"))
    route = [(i - distance, i) for i in devices if i - distance in devices]
    return lax.ppermute(block, "ctx", route)


def exchange(block, bit):
    route = [(i, i ^ bit) for i in range(lax.axis_size("ctx"))]
    return lax.ppermute(block, "ctx", route)


def split(x):
    high = x.astype(BF16)
    return high, (x - high.astype(F32)).astype(BF16)


def dot(a, b, ca=1, cb=0, passes=3):
    dims = (((ca,), (cb,)), ((), ()))
    mul = functools.partial(lax.dot_general, dimension_numbers=dims, preferred_element_type=F32)
    a_high, a_low = split(a)
    b_high, b_low = split(b)
    if passes == 1:
        return mul(a_high, b_high)
    return mul(a_high, b_high) + (mul(a_low, b_high) + mul(a_high, b_low))


def inverse_norm(x):
    return lax.rsqrt(jnp.sum(x * x, axis=-1, keepdims=True) + 1e-06)


def order_of(shape, dim):
    p = lax.broadcasted_iota(jnp.int32, shape, dim)
    return 2 * (p & (WIDTH - 1)) + (p >> 7)


def column_of(row):
    shape = (PAIRS, PAIRS)
    time = lax.broadcasted_iota(jnp.int32, shape, 1)
    return jnp.sum(jnp.where(time == order_of(shape, 0), row, 0.0), axis=1, keepdims=True)


def row_of(column):
    shape = (PAIRS, PAIRS)
    time = lax.broadcasted_iota(jnp.int32, shape, 1)
    return jnp.sum(jnp.where(time == order_of(shape, 0), column, 0.0), axis=0, keepdims=True)


def visible_mask():
    shape = (WIDTH, PAIRS)
    token = lax.broadcasted_iota(jnp.int32, shape, 0)
    return (lax.broadcasted_iota(jnp.int32, shape, 1) & (WIDTH - 1)) <= token


def stacked(ref):
    return jnp.concatenate([ref[:, :WIDTH], ref[:, WIDTH:]], axis=0).astype(F32)


def prepare_kernel(place, q_ref, k_ref, v_ref, logit_ref, ab_ref, m_ref, wy_ref, qt_ref, local_ref):
    head = pl.program_id(0)
    query = q_ref[...].astype(F32)
    query = query * inverse_norm(query)
    key = stacked(k_ref)
    key = key * inverse_norm(key)
    value = stacked(v_ref)
    strength = 2.0 / (1.0 + jnp.exp(-column_of(logit_ref[pl.ds(head, 1), :])))
    shape = (PAIRS, PAIRS)
    row, col = order_of(shape, 0), order_of(shape, 1)
    coupling = jnp.where(col < row, strength * dot(key, key, 1, 1), 0.0)
    identity = jnp.where(row == col, 1.0, 0.0).astype(F32)
    inverse = identity - jnp.where((row >> 1) == (col >> 1), coupling, 0.0)
    for level in range(1, 8):
        join = ((row >> (level + 1)) == (col >> (level + 1))) & ((row >> level) != (col >> level))
        edge = jnp.where(join, coupling, 0.0)
        inverse = inverse - dot(dot(inverse, edge), inverse)
    scores = jnp.where(visible_mask(), dot(query, key, 1, 1), 0.0)
    scaled = strength * jnp.concatenate([key, value], axis=1)
    wy_ref[0] = dot(inverse, scaled)
    reads = jnp.concatenate([dot(scores, inverse), dot(key, inverse, 0, 0)], axis=0)
    m_ref[0] = reads
    product = dot(reads, scaled)
    qt_ref[0] = query - product[:WIDTH, :WIDTH]
    local_ref[0] = product[:WIDTH, WIDTH:]
    eye = jnp.where(
        lax.broadcasted_iota(jnp.int32, (WIDTH, WIDTH), 0)
        == lax.broadcasted_iota(jnp.int32, (WIDTH, WIDTH), 1),
        1.0,
        0.0,
    )
    ab_ref[0, :, :WIDTH] = (eye - product[WIDTH:, :WIDTH]).astype(BF16)
    ab_ref[0, :, WIDTH:] = product[WIDTH:, WIDTH:].astype(BF16)


def slot(head, place):
    return (head + 2 * place[0]) % 4


def by_head(*block):
    return pl.BlockSpec((1,) + block, lambda h, place: (h,) + (0,) * len(block))


def by_slot(*block):
    return pl.BlockSpec((1,) + block, lambda h, place: (slot(h, place),) + (0,) * len(block))


def by_columns(width):
    return pl.BlockSpec((WIDTH, width), lambda h, place: (0, h))


def whole(*shape):
    return pl.BlockSpec(shape, lambda i, place: (0,) * len(shape))


def call(kernel, steps, in_specs, out_specs, out_shape, flops, moved, scratch=()):
    return pl.pallas_call(
        kernel,
        grid_spec=pltpu.PrefetchScalarGridSpec(
            num_scalar_prefetch=1,
            grid=(steps,),
            in_specs=in_specs,
            out_specs=out_specs,
            scratch_shapes=list(scratch),
        ),
        out_shape=out_shape,
        compiler_params=pltpu.CompilerParams(vmem_limit_bytes=40 << 20),
        cost_estimate=pl.CostEstimate(flops=flops, bytes_accessed=moved, transcendentals=0),
    )


def arr(dtype, *shape):
    return jax.ShapeDtypeStruct(shape, dtype)


def prepare(place, queries, keys, values, logits):
    return call(
        prepare_kernel,
        4,
        [by_columns(WIDTH), by_columns(PAIRS), by_columns(PAIRS), whole(4, PAIRS)],
        [
            by_slot(WIDTH, PAIRS),
            by_head(PAIRS, PAIRS),
            by_head(PAIRS, PAIRS),
            by_head(WIDTH, WIDTH),
            by_head(WIDTH, WIDTH),
        ],
        [
            arr(BF16, 4, WIDTH, PAIRS),
            arr(F32, 4, PAIRS, PAIRS),
            arr(F32, 4, PAIRS, PAIRS),
            arr(F32, 4, WIDTH, WIDTH),
            arr(F32, 4, WIDTH, WIDTH),
        ],
        4 * 60 * 2 * PAIRS**3,
        4 << 20,
    )(place, queries, keys, values, logits)


def feature_block(grad_ref, place, z, row, core):
    owner = (row ^ place[1]) * 4 + z // 2
    column = pl.multiple_of((z % 2) * 256 + (core ^ place[0]) * 128, 128)
    return owner, pl.ds(column, 128)


def outputs_kernel(place, qt_ref, local_ref, state_ref, grad_ref, heads_ref, mine_ref, other_ref, held):
    z = pl.program_id(0)

    @pl.when(z == 0)
    def _():
        for head in range(4):
            state = state_ref[slot(head, place)].astype(F32)
            result = dot(qt_ref[head], state) + local_ref[head]
            held[:, head * WIDTH : (head + 1) * WIDTH] = result.astype(BF16)
        heads_ref[...] = held[...]

    for row in range(2):
        for core, out_ref in ((0, mine_ref), (1, other_ref)):
            owner, columns = feature_block(grad_ref, place, z, row, core)
            block = grad_ref[owner, :, columns]
            product = lax.dot_general(
                block, held[...], (((0,), (0,)), ((), ())), preferred_element_type=F32
            )
            out_ref[0, row] = (product * (1.0 / 64.0)).astype(BF16)


def outputs(place, qt, local, state, grad_full):
    heads = arr(BF16, WIDTH, 512)
    part = arr(BF16, 8, 2, WIDTH, 512)
    tile = pl.BlockSpec((1, 2, WIDTH, 512), lambda z, place: (z, 0, 0, 0))
    return call(
        outputs_kernel,
        8,
        [whole(4, WIDTH, WIDTH), whole(4, WIDTH, WIDTH), whole(4, WIDTH, WIDTH), whole(8, WIDTH, 512)],
        [whole(WIDTH, 512), tile, tile],
        [heads, part, part],
        2 * 128 * 512 * 4096,
        6 << 20,
        [pltpu.VMEM((WIDTH, 512), BF16)],
    )(place, qt, local, state, grad_full)


def mixed_kernel(place, heads_ref, mine_ref, other_ref, out_ref):
    z = pl.program_id(0)
    for row in range(2):
        for core, w_ref in ((0, mine_ref), (1, other_ref)):
            owner, columns = feature_block(out_ref, place, z, row, core)
            product = lax.dot_general(
                heads_ref[...], w_ref[0, row], (((1,), (1,)), ((), ())), preferred_element_type=F32
            )
            out_ref[owner, :, columns] = product.astype(BF16)


def mixed_parts(place, heads, mine, other):
    tile = pl.BlockSpec((1, 2, WIDTH, 512), lambda z, place: (z, 0, 0, 0))
    return call(
        mixed_kernel,
        8,
        [whole(WIDTH, 512), tile, tile],
        whole(8, WIDTH, 512),
        arr(BF16, 8, WIDTH, 512),
        2 * 128 * 512 * 4096,
        6 << 20,
    )(place, heads, mine, other)


def head_grad_kernel(place, grad_ref, mine_ref, other_ref, qt_ref, out_ref, own_ref):
    z = pl.program_id(0)
    total = jnp.zeros((WIDTH, 512), F32)
    for row in range(2):
        for core, w_ref in ((0, mine_ref), (1, other_ref)):
            owner, columns = feature_block(grad_ref, place, z, row, core)
            total += jnp.dot(
                grad_ref[owner, :, columns], w_ref[0, row], preferred_element_type=F32
            )

    @pl.when(z == 0)
    def _():
        out_ref[...] = total

    @pl.when(z > 0)
    def _():
        out_ref[...] += total

    @pl.when(z == 7)
    def _():
        for head in range(4):
            grad = out_ref[:, head * WIDTH : (head + 1) * WIDTH]
            own_ref[slot(head, place)] = dot(qt_ref[head], grad, 0, 0).astype(BF16)


def head_gradient(place, grad_full, mine, other, qt):
    tile = pl.BlockSpec((1, 2, WIDTH, 512), lambda z, place: (z, 0, 0, 0))
    return call(
        head_grad_kernel,
        8,
        [whole(8, WIDTH, 512), tile, tile, whole(4, WIDTH, WIDTH)],
        [whole(WIDTH, 512), whole(4, WIDTH, WIDTH)],
        [arr(F32, WIDTH, 512), arr(BF16, 4, WIDTH, WIDTH)],
        2 * 128 * 512 * 4096,
        6 << 20,
    )(place, grad_full, mine, other, qt)


def pull_kernel(
    place, q_ref, k_ref, logit_ref, m_ref, wy_ref, state_ref, end_ref, grad_ref,
    dq_ref, dk_ref, dv_ref, dlogit_ref,
):
    head = pl.program_id(0)
    query = q_ref[...].astype(F32)
    query_scale = inverse_norm(query)
    query = query * query_scale
    key = stacked(k_ref)
    key_scale = inverse_norm(key)
    key = key * key_scale
    logit = column_of(logit_ref[pl.ds(head, 1), :])
    strength = 2.0 / (1.0 + jnp.exp(-logit))
    state = state_ref[0].astype(F32)
    end = end_ref[0].astype(F32)
    grad = grad_ref[...]
    shape = (PAIRS, PAIRS)
    before = order_of(shape, 1) < order_of(shape, 0)
    updates = wy_ref[0, :, WIDTH:] - dot(wy_ref[0, :, :WIDTH], state)
    pulled = dot(m_ref[0], jnp.concatenate([grad, end], axis=0), 0, 0)
    value_grad = strength * pulled
    dv_ref[:, :WIDTH] = value_grad[:WIDTH].astype(BF16)
    dv_ref[:, WIDTH:] = value_grad[WIDTH:].astype(BF16)
    slope = jnp.sum(pulled * updates, axis=1, keepdims=True) / (1.0 + jnp.exp(logit))
    dlogit_ref[pl.ds(head, 1), :] = row_of(slope)
    cross = dot(jnp.concatenate([grad, value_grad], axis=0), updates, 1, 1)
    pairs = jnp.concatenate(
        [
            jnp.where(visible_mask(), cross[:WIDTH], 0.0),
            jnp.where(before, -cross[WIDTH:], 0.0),
        ],
        axis=0,
    )
    forward = dot(pairs, key)
    backward = dot(pairs, jnp.concatenate([query, key], axis=0), 0, 0)
    by_state = dot(jnp.concatenate([grad, -value_grad], axis=0), state, 1, 1)
    query_grad = forward[:WIDTH] + by_state[:WIDTH]
    key_grad = forward[WIDTH:] + backward + dot(updates, end, 1, 1) + by_state[WIDTH:]
    query_grad = query_scale * (
        query_grad - query * jnp.sum(query * query_grad, axis=1, keepdims=True)
    )
    key_grad = key_scale * (key_grad - key * jnp.sum(key * key_grad, axis=1, keepdims=True))
    dq_ref[...] = query_grad.astype(BF16)
    dk_ref[:, :WIDTH] = key_grad[:WIDTH].astype(BF16)
    dk_ref[:, WIDTH:] = key_grad[WIDTH:].astype(BF16)


def pull(place, queries, keys, logits, reads, wy, state, end, head_grad):
    return call(
        pull_kernel,
        4,
        [
            by_columns(WIDTH),
            by_columns(PAIRS),
            whole(4, PAIRS),
            by_head(PAIRS, PAIRS),
            by_head(PAIRS, PAIRS),
            by_slot(WIDTH, WIDTH),
            by_slot(WIDTH, WIDTH),
            by_columns(WIDTH),
        ],
        [by_columns(WIDTH), by_columns(PAIRS), by_columns(PAIRS), whole(4, PAIRS)],
        [
            arr(BF16, WIDTH, 512),
            arr(BF16, WIDTH, 1024),
            arr(BF16, WIDTH, 1024),
            arr(F32, 4, PAIRS),
        ],
        4 * 14 * 2 * PAIRS**3,
        5 << 20,
    )(place, queries, keys, logits, reads, wy, state, end, head_grad)


def mul(a, b):
    return jnp.einsum("hij,hjk->hik", a, b, preferred_element_type=F32)


def mul_t(a, b):
    return jnp.einsum("hji,hjk->hik", a, b, preferred_element_type=F32)


def halves(x):
    return x[:, :, :WIDTH], x[:, :, WIDTH:]


def forward_states(ab, core):
    mine, theirs = ab[:2], exchange(ab[2:], 1)
    even = jnp.where(core == 0, mine, theirs)
    odd = jnp.where(core == 0, theirs, mine)
    even_a, even_b = halves(even)
    odd_a, odd_b = halves(odd)
    joined = mul(odd_a, even)
    chip = jnp.concatenate(
        [joined[:, :, :WIDTH], joined[:, :, WIDTH:] + odd_b.astype(F32)], axis=2
    ).astype(BF16)
    one, two = send(chip, 2), send(chip, 4)
    window, state = halves(one)
    windows = [window]
    state = state.astype(F32)
    step = mul(window, two)
    state = state + step[:, :, WIDTH:]
    window = step[:, :, :WIDTH].astype(BF16)
    for distance in (4, 8):
        windows.append(window)
        came = send(jnp.concatenate([window, state.astype(BF16)], axis=2), distance)
        step = mul(window, came)
        state = state + step[:, :, WIDTH:]
        window = step[:, :, :WIDTH].astype(BF16)
    windows.append(window)
    state = state + mul(window, send(state.astype(BF16), 16))
    first = state.astype(BF16)
    second = (mul(even_a, first) + even_b.astype(F32)).astype(BF16)
    kept = jnp.where(core == 0, first, second)
    given = jnp.where(core == 0, second, first)
    return jnp.concatenate([kept, exchange(given, 1)], axis=0), (even_a, odd_a, windows)


def backward_states(own, core, saved):
    even_a, odd_a, windows = saved
    mine, theirs = own[:2], exchange(own[2:], 1)
    even = jnp.where(core == 0, mine, theirs)
    odd = jnp.where(core == 0, theirs, mine)
    total = even.astype(F32) + mul_t(even_a, odd)
    for window, distance in zip(windows, (2, 4, 8)):
        passed = mul_t(window, total.astype(BF16)).astype(BF16)
        total = total + send(passed, -distance).astype(F32)
    rounded = total.astype(BF16)
    far = mul_t(windows[3], rounded).astype(BF16)
    second = send(rounded, -2).astype(F32) + send(far, -18).astype(F32)
    second = second.astype(BF16)
    first = (odd.astype(F32) + mul_t(odd_a, second)).astype(BF16)
    kept = jnp.where(core == 0, first, second)
    given = jnp.where(core == 0, second, first)
    return jnp.concatenate([kept, exchange(given, 1)], axis=0)


def local(queries, keys, values, beta_logit, out_weight, out_grad):
    index = lax.axis_index("ctx")
    core = index & 1
    place = jnp.stack([core, index >> 4]).astype(jnp.int32)
    rings = [[(half * 8 + z) * 2 + c for z in range(8)] for half in range(2) for c in range(2)]
    weight_pair = jnp.stack([out_weight, exchange(out_weight, 16)])
    weight_mine = lax.all_gather(weight_pair, "ctx", axis=0, axis_index_groups=rings)
    weight_other = exchange(weight_mine, 1)
    grad_full = lax.all_to_all(
        jnp.broadcast_to(out_grad[None], (8, WIDTH, 512)), "tp", 0, 0, tiled=True
    )
    ab, reads, wy, qt, local_out = prepare(place, queries, keys, values, beta_logit)
    state, saved = forward_states(ab, core)
    heads, part_mine, part_other = outputs(place, qt, local_out, state, grad_full)
    part = part_mine.astype(F32) + exchange(part_other, 1).astype(F32)
    ring_sum = lax.psum_scatter(
        part.astype(BF16).reshape(8, PAIRS, 512),
        "ctx",
        scatter_dimension=0,
        axis_index_groups=rings,
    )
    weight_grad = ring_sum[:WIDTH].astype(F32) + exchange(ring_sum[WIDTH:], 16).astype(F32)
    mixed = lax.all_to_all(
        mixed_parts(place, heads, weight_mine, weight_other), "tp", 0, 0, tiled=True
    )
    mixed = jnp.sum(mixed.astype(F32), axis=0).astype(BF16)
    head_grad, own = head_gradient(place, grad_full, weight_mine, weight_other, qt)
    end = backward_states(own, core, saved)
    query_grad, key_grad, value_grad, logit_grad = pull(
        place, queries, keys, beta_logit, reads, wy, state, end, head_grad
    )
    return mixed, query_grad, key_grad, value_grad, logit_grad, weight_grad


def solution(mesh):
    placed = P("ctx", "tp")
    return jax.shard_map(
        local,
        mesh=mesh,
        in_specs=(placed, placed, placed, P("tp", "ctx"), placed, placed),
        out_specs=(placed, placed, placed, placed, P("tp", "ctx"), placed),
        check_vma=False,
    )
```

```python
import functools
import math

import jax
import jax.numpy as jnp
from jax import lax
from jax.experimental import pallas as pl
from jax.experimental.pallas import tpu as pltpu
from jax.sharding import PartitionSpec as P

F32 = jnp.float32
BF16 = jnp.bfloat16
WIDTH = 128
VMEM = 56 << 20
PAIRS = 2 * WIDTH


def send(block, distance):
    devices = range(lax.axis_size("ctx"))
    route = [(i - distance, i) for i in devices if i - distance in devices]
    return lax.ppermute(block, "ctx", route)


def exchange(block, bit):
    route = [(i, i ^ bit) for i in range(lax.axis_size("ctx"))]
    return lax.ppermute(block, "ctx", route)


def split(x):
    high = x.astype(BF16)
    return high, (x - high.astype(F32)).astype(BF16)


def dot(a, b, ca=1, cb=0, passes=3):
    dims = (((ca,), (cb,)), ((), ()))
    mul = functools.partial(lax.dot_general, dimension_numbers=dims, preferred_element_type=F32)
    a_high, a_low = split(a)
    b_high, b_low = split(b)
    if passes == 1:
        return mul(a_high, b_high)
    return mul(a_high, b_high) + (mul(a_low, b_high) + mul(a_high, b_low))


def inverse_norm(x):
    return lax.rsqrt(jnp.sum(x * x, axis=-1, keepdims=True) + 1e-06)


def order_of(shape, dim):
    p = lax.broadcasted_iota(jnp.int32, shape, dim)
    return 2 * (p & (WIDTH - 1)) + (p >> 7)


def column_of(row):
    shape = (PAIRS, PAIRS)
    time = lax.broadcasted_iota(jnp.int32, shape, 1)
    return jnp.sum(jnp.where(time == order_of(shape, 0), row, 0.0), axis=1, keepdims=True)


def row_of(column):
    shape = (PAIRS, PAIRS)
    time = lax.broadcasted_iota(jnp.int32, shape, 1)
    return jnp.sum(jnp.where(time == order_of(shape, 0), column, 0.0), axis=0, keepdims=True)


def visible_mask():
    shape = (WIDTH, PAIRS)
    token = lax.broadcasted_iota(jnp.int32, shape, 0)
    return (lax.broadcasted_iota(jnp.int32, shape, 1) & (WIDTH - 1)) <= token


def stacked(ref, i):
    start = i * PAIRS
    parts = [ref[:, start : start + WIDTH], ref[:, start + WIDTH : start + PAIRS]]
    return jnp.concatenate(parts, axis=0).astype(F32)


def prepare_kernel(*refs):
    q_ref, k_ref, v_ref, logit_ref = refs[1:5]
    ab_ref, m_ref, wy_ref, qt_ref, local_ref = refs[-5:]
    two = range(2)
    shape = (PAIRS, PAIRS)
    row, col = order_of(shape, 0), order_of(shape, 1)
    identity = jnp.where(row == col, 1.0, 0.0).astype(F32)
    query = [q_ref[:, i * WIDTH : (i + 1) * WIDTH].astype(F32) for i in two]
    query = [x * inverse_norm(x) for x in query]
    key = [stacked(k_ref, i) for i in two]
    key = [x * inverse_norm(x) for x in key]
    strength = [2.0 / (1.0 + jnp.exp(-column_of(logit_ref[0, i : i + 1, :]))) for i in two]
    coupling = [jnp.where(col < row, strength[i] * dot(key[i], key[i], 1, 1), 0.0) for i in two]
    inverse = [identity - jnp.where((row >> 1) == (col >> 1), coupling[i], 0.0) for i in two]
    for level in range(1, 8):
        join = ((row >> (level + 1)) == (col >> (level + 1))) & ((row >> level) != (col >> level))
        edge = [jnp.where(join, coupling[i], 0.0) for i in two]
        step = [dot(inverse[i], edge[i], passes=1) for i in two]
        inverse = [inverse[i] - dot(step[i], inverse[i], passes=1) for i in two]
    rest = [identity - inverse[i] - dot(coupling[i], inverse[i]) for i in two]
    inverse = [inverse[i] + dot(inverse[i], rest[i], passes=1) for i in two]
    scores = [jnp.where(visible_mask(), dot(query[i], key[i], 1, 1), 0.0) for i in two]
    scaled = [strength[i] * jnp.concatenate([key[i], stacked(v_ref, i)], axis=1) for i in two]
    reads = [
        jnp.concatenate([dot(scores[i], inverse[i]), dot(key[i], inverse[i], 0, 0)], axis=0)
        for i in two
    ]
    product = [dot(reads[i], scaled[i]) for i in two]
    eye = identity[:WIDTH, :WIDTH]
    for i in two:
        ab_ref[i, :, :WIDTH] = (eye - product[i][WIDTH:, :WIDTH]).astype(BF16)
        ab_ref[i, :, WIDTH:] = product[i][WIDTH:, WIDTH:].astype(BF16)
        qt_ref[i] = query[i] - product[i][:WIDTH, :WIDTH]
        local_ref[i] = product[i][:WIDTH, WIDTH:]
        m_ref[i] = reads[i]
        wy_ref[i] = dot(inverse[i], scaled[i])


def slot(head, place):
    return (head + 2 * place[0]) % 4


def by_pair(*block):
    return pl.BlockSpec((2,) + block, lambda i, place: (i,) + (0,) * len(block))


def by_slot(*block):
    return pl.BlockSpec((2,) + block, lambda i, place: (i ^ place[0],) + (0,) * len(block))


def by_columns(width):
    return pl.BlockSpec((WIDTH, 2 * width), lambda i, place: (0, i))


def whole(*shape):
    return pl.BlockSpec(shape, lambda i, place: (0,) * len(shape))


def call(kernel, steps, in_specs, out_specs, out_shape, flops, moved, scratch=()):
    return pl.pallas_call(
        kernel,
        grid_spec=pltpu.PrefetchScalarGridSpec(
            num_scalar_prefetch=1,
            grid=(steps,),
            in_specs=in_specs,
            out_specs=out_specs,
            scratch_shapes=list(scratch),
        ),
        out_shape=out_shape,
        compiler_params=pltpu.CompilerParams(vmem_limit_bytes=VMEM),
        cost_estimate=pl.CostEstimate(flops=flops, bytes_accessed=moved, transcendentals=0),
    )


def arr(dtype, *shape):
    return jax.ShapeDtypeStruct(shape, dtype)


def prepare(place, queries, keys, values, logits, mine, filled=()):
    def pair(place):
        return place[0] if mine else 1 - place[0]

    def columns(width):
        return pl.BlockSpec((WIDTH, 2 * width), lambda i, place: (0, pair(place)))

    def heads(*block):
        return pl.BlockSpec((2,) + block, lambda i, place: (pair(place),) + (0,) * len(block))

    def stored(n):
        return arr(F32, 4, n, n)

    return pl.pallas_call(
        prepare_kernel,
        grid_spec=pltpu.PrefetchScalarGridSpec(
            num_scalar_prefetch=1,
            grid=(1,),
            in_specs=[
                columns(WIDTH),
                columns(PAIRS),
                columns(PAIRS),
                pl.BlockSpec((1, 2, PAIRS), lambda i, place: (pair(place), 0, 0)),
            ]
            + [pl.BlockSpec(memory_space=pl.ANY)] * len(filled),
            out_specs=[
                pl.BlockSpec((2, WIDTH, PAIRS), lambda i, place: (0, 0, 0)),
                heads(PAIRS, PAIRS),
                heads(PAIRS, PAIRS),
                heads(WIDTH, WIDTH),
                heads(WIDTH, WIDTH),
            ],
        ),
        out_shape=[
            arr(BF16, 2, WIDTH, PAIRS),
            stored(PAIRS),
            stored(PAIRS),
            stored(WIDTH),
            stored(WIDTH),
        ],
        input_output_aliases={5 + i: 1 + i for i in range(len(filled))},
        compiler_params=pltpu.CompilerParams(vmem_limit_bytes=VMEM),
        cost_estimate=pl.CostEstimate(
            flops=(1 if mine else 100) << 20, bytes_accessed=1 << (16 if mine else 24), transcendentals=0
        ),
    )(place, queries, keys, values, logits.reshape(2, 2, PAIRS), *filled)


def feature_block(grad_ref, place, z, row, core):
    owner = (row ^ place[1]) * 4 + z // 2
    column = pl.multiple_of((z % 2) * 256 + (core ^ place[0]) * 128, 128)
    return owner, pl.ds(column, 128)


def grad_block(grad_ref, place, z, row, core):
    owner, columns = feature_block(grad_ref, place, z, row, core)
    return grad_ref[owner, :, columns]


def weight_rows(mine_ref, other_ref):
    return jnp.concatenate([mine_ref[0, 0], mine_ref[0, 1], other_ref[0, 0], other_ref[0, 1]], axis=0)


def outputs_kernel(place, qt_ref, local_ref, state_ref, grad_ref, heads_ref, mine_ref, other_ref, held):
    z = pl.program_id(0)

    @pl.when(z == 0)
    def _():
        for head in range(4):
            state = state_ref[slot(head, place)].astype(F32)
            result = dot(qt_ref[head], state) + local_ref[head]
            held[:, head * WIDTH : (head + 1) * WIDTH] = result.astype(BF16)
        heads_ref[...] = held[...]

    blocks = jnp.concatenate(
        [grad_block(grad_ref, place, z, row, core) for core in range(2) for row in range(2)], axis=1
    )
    product = lax.dot_general(
        blocks, held[...], (((0,), (0,)), ((), ())), preferred_element_type=F32
    )
    product = (product * (1.0 / 64.0)).astype(BF16)
    for row in range(2):
        mine_ref[0, row] = product[row * WIDTH : (row + 1) * WIDTH]
        other_ref[0, row] = product[(2 + row) * WIDTH : (3 + row) * WIDTH]


def outputs(place, qt, local, state, grad_full):
    heads = arr(BF16, WIDTH, 512)
    part = arr(BF16, 8, 2, WIDTH, 512)
    tile = pl.BlockSpec((1, 2, WIDTH, 512), lambda z, place: (z, 0, 0, 0))
    return call(
        outputs_kernel,
        8,
        [whole(4, WIDTH, WIDTH), whole(4, WIDTH, WIDTH), whole(4, WIDTH, WIDTH), whole(8, WIDTH, 512)],
        [whole(WIDTH, 512), tile, tile],
        [heads, part, part],
        2 * 128 * 512 * 4096,
        6 << 20,
        [pltpu.VMEM((WIDTH, 512), BF16)],
    )(place, qt, local, state, grad_full)


def mixed_kernel(place, heads_ref, mine_ref, other_ref, out_ref):
    z = pl.program_id(0)
    product = lax.dot_general(
        heads_ref[...],
        weight_rows(mine_ref, other_ref),
        (((1,), (1,)), ((), ())),
        preferred_element_type=F32,
    ).astype(BF16)
    for core in range(2):
        for row in range(2):
            owner, columns = feature_block(out_ref, place, z, row, core)
            start = (2 * core + row) * WIDTH
            out_ref[owner, :, columns] = product[:, start : start + WIDTH]


def mixed_parts(place, heads, mine, other):
    tile = pl.BlockSpec((1, 2, WIDTH, 512), lambda z, place: (z, 0, 0, 0))
    return call(
        mixed_kernel,
        8,
        [whole(WIDTH, 512), tile, tile],
        whole(8, WIDTH, 512),
        arr(BF16, 8, WIDTH, 512),
        2 * 128 * 512 * 4096,
        6 << 20,
    )(place, heads, mine, other)


def head_grad_kernel(place, grad_ref, mine_ref, other_ref, qt_ref, out_ref, own_ref):
    z = pl.program_id(0)
    blocks = jnp.concatenate(
        [grad_block(grad_ref, place, z, row, core) for core in range(2) for row in range(2)], axis=1
    )
    total = jnp.dot(blocks, weight_rows(mine_ref, other_ref), preferred_element_type=F32)

    @pl.when(z == 0)
    def _():
        out_ref[...] = total

    @pl.when(z > 0)
    def _():
        out_ref[...] += total

    @pl.when(z == 7)
    def _():
        for head in range(4):
            grad = out_ref[:, head * WIDTH : (head + 1) * WIDTH]
            own_ref[slot(head, place)] = dot(qt_ref[head], grad, 0, 0).astype(BF16)


def head_gradient(place, grad_full, mine, other, qt):
    tile = pl.BlockSpec((1, 2, WIDTH, 512), lambda z, place: (z, 0, 0, 0))
    return call(
        head_grad_kernel,
        8,
        [whole(8, WIDTH, 512), tile, tile, whole(4, WIDTH, WIDTH)],
        [whole(WIDTH, 512), whole(4, WIDTH, WIDTH)],
        [arr(F32, WIDTH, 512), arr(BF16, 4, WIDTH, WIDTH)],
        2 * 128 * 512 * 4096,
        6 << 20,
    )(place, grad_full, mine, other, qt)


def pull_kernel(
    place, q_ref, k_ref, logit_ref, m_ref, wy_ref, state_ref, end_ref, grad_ref,
    dq_ref, dk_ref, dv_ref, dlogit_ref,
):
    two = range(2)
    shape = (PAIRS, PAIRS)
    before = order_of(shape, 1) < order_of(shape, 0)
    query = [q_ref[:, i * WIDTH : (i + 1) * WIDTH].astype(F32) for i in two]
    query_scale = [inverse_norm(x) for x in query]
    query = [query[i] * query_scale[i] for i in two]
    key = [stacked(k_ref, i) for i in two]
    key_scale = [inverse_norm(x) for x in key]
    key = [key[i] * key_scale[i] for i in two]
    logit = [column_of(logit_ref[0, i : i + 1, :]) for i in two]
    state = [state_ref[i].astype(F32) for i in two]
    end = [end_ref[i].astype(F32) for i in two]
    grad = [grad_ref[:, i * WIDTH : (i + 1) * WIDTH] for i in two]
    updates = [wy_ref[i, :, WIDTH:] - dot(wy_ref[i, :, :WIDTH], state[i]) for i in two]
    pulled = [dot(m_ref[i], jnp.concatenate([grad[i], end[i]], axis=0), 0, 0) for i in two]
    value_grad = [2.0 / (1.0 + jnp.exp(-logit[i])) * pulled[i] for i in two]
    cross = [
        dot(jnp.concatenate([grad[i], value_grad[i]], axis=0), updates[i], 1, 1) for i in two
    ]
    pairs = [
        jnp.concatenate(
            [
                jnp.where(visible_mask(), cross[i][:WIDTH], 0.0),
                jnp.where(before, -cross[i][WIDTH:], 0.0),
            ],
            axis=0,
        )
        for i in two
    ]
    forward = [dot(pairs[i], key[i]) for i in two]
    backward = [dot(pairs[i], jnp.concatenate([query[i], key[i]], axis=0), 0, 0) for i in two]
    by_state = [
        dot(jnp.concatenate([grad[i], -value_grad[i]], axis=0), state[i], 1, 1) for i in two
    ]
    by_end = [dot(updates[i], end[i], 1, 1) for i in two]
    for i in two:
        start = i * PAIRS
        dv_ref[:, start : start + WIDTH] = value_grad[i][:WIDTH].astype(BF16)
        dv_ref[:, start + WIDTH : start + PAIRS] = value_grad[i][WIDTH:].astype(BF16)
        slope = jnp.sum(pulled[i] * updates[i], axis=1, keepdims=True) / (1.0 + jnp.exp(logit[i]))
        dlogit_ref[0, i : i + 1, :] = row_of(slope)
        query_grad = forward[i][:WIDTH] + by_state[i][:WIDTH]
        query_grad = query_scale[i] * (
            query_grad - query[i] * jnp.sum(query[i] * query_grad, axis=1, keepdims=True)
        )
        dq_ref[:, i * WIDTH : (i + 1) * WIDTH] = query_grad.astype(BF16)
        key_grad = forward[i][WIDTH:] + backward[i] + by_end[i] + by_state[i][WIDTH:]
        key_grad = key_scale[i] * (
            key_grad - key[i] * jnp.sum(key[i] * key_grad, axis=1, keepdims=True)
        )
        dk_ref[:, start : start + WIDTH] = key_grad[:WIDTH].astype(BF16)
        dk_ref[:, start + WIDTH : start + PAIRS] = key_grad[WIDTH:].astype(BF16)


def pull(place, queries, keys, logits, reads, wy, state, end, head_grad):
    logit_spec = pl.BlockSpec((1, 2, PAIRS), lambda i, place: (i, 0, 0))
    *grads, logit_grad = call(
        pull_kernel,
        2,
        [
            by_columns(WIDTH),
            by_columns(PAIRS),
            logit_spec,
            by_pair(PAIRS, PAIRS),
            by_pair(PAIRS, PAIRS),
            by_slot(WIDTH, WIDTH),
            by_slot(WIDTH, WIDTH),
            by_columns(WIDTH),
        ],
        [by_columns(WIDTH), by_columns(PAIRS), by_columns(PAIRS), logit_spec],
        [
            arr(BF16, WIDTH, 512),
            arr(BF16, WIDTH, 1024),
            arr(BF16, WIDTH, 1024),
            arr(F32, 2, 2, PAIRS),
        ],
        4 * 14 * 2 * PAIRS**3,
        5 << 20,
    )(place, queries, keys, logits.reshape(2, 2, PAIRS), reads, wy, state, end, head_grad)
    return (*grads, logit_grad.reshape(4, PAIRS))


def mul(a, b):
    return jnp.einsum("hij,hjk->hik", a, b, preferred_element_type=F32)


def mul_t(a, b):
    return jnp.einsum("hji,hjk->hik", a, b, preferred_element_type=F32)


def halves(x):
    return x[:, :, :WIDTH], x[:, :, WIDTH:]


def forward_states(mine, theirs, core, gate):
    theirs = exchange(theirs, 1)
    even = jnp.where(core == 0, mine, theirs)
    odd = jnp.where(core == 0, theirs, mine)
    even_a, even_b = halves(even)
    odd_a, odd_b = halves(odd)
    joined = mul(odd_a, even)
    chip = jnp.concatenate(
        [joined[:, :, :WIDTH], joined[:, :, WIDTH:] + odd_b.astype(F32)], axis=2
    ).astype(BF16)
    one, two = send(chip, 2), send(chip, 4)
    window1, state = halves(one)
    step = mul(window1, two)
    state = state.astype(F32) + step[:, :, WIDTH:]
    window2 = step[:, :, :WIDTH].astype(BF16)
    step = mul(window2, send(jnp.concatenate([window2, state.astype(BF16)], axis=2), 4))
    state = state + step[:, :, WIDTH:]
    window4 = step[:, :, :WIDTH].astype(BF16)
    rounded = state.astype(BF16)
    both = jnp.concatenate([window4, rounded], axis=2)
    near_a, near_b = halves(send(both, 8))
    mid_a, mid_b = halves(send(both, 16))
    far_b = send(rounded, 24)
    inner = (mid_b.astype(F32) + mul(mid_a, far_b)).astype(BF16)
    inner = (near_b.astype(F32) + mul(near_a, inner)).astype(BF16)
    first = (state + mul(window4, inner)).astype(BF16)
    window8 = mul(window4, near_a).astype(BF16)
    window12 = mul(window8, mid_a).astype(BF16)
    second = (mul(even_a, first) + even_b.astype(F32)).astype(BF16)
    kept = jnp.where(core == 0, first, second)
    given = jnp.where(core == 0, second, first)
    gate, given = lax.optimization_barrier((gate, given))
    state_in = jnp.concatenate([kept, exchange(given, 1)], axis=0)
    return gate, state_in, (even_a, odd_a, window1, window2, window4, window8, window12)


def backward_states(own, core, saved):
    even_a, odd_a, window1, window2, window4, window8, window12 = saved
    mine, theirs = own[:2], exchange(own[2:], 1)
    even = jnp.where(core == 0, mine, theirs)
    odd = jnp.where(core == 0, theirs, mine)
    total = even.astype(F32) + mul_t(even_a, odd)
    for window, distance in ((window1, 2), (window2, 4)):
        passed = mul_t(window, total.astype(BF16)).astype(BF16)
        total = total + send(passed, -distance).astype(F32)
    rounded = total.astype(BF16)
    second = send(rounded, -2).astype(F32)
    for window, distance in ((window4, 10), (window8, 18), (window12, 26)):
        second += send(mul_t(window, rounded).astype(BF16), -distance).astype(F32)
    second = second.astype(BF16)
    first = (odd.astype(F32) + mul_t(odd_a, second)).astype(BF16)
    kept = jnp.where(core == 0, first, second)
    given = jnp.where(core == 0, second, first)
    return jnp.concatenate([kept, exchange(given, 1)], axis=0)


def local(queries, keys, values, beta_logit, out_weight, out_grad):
    index = lax.axis_index("ctx")
    core = index & 1
    place = jnp.stack([core, index >> 4]).astype(jnp.int32)
    rings = [[(half * 8 + z) * 2 + c for z in range(8)] for half in range(2) for c in range(2)]
    operands = (queries, keys, values, beta_logit)
    theirs, *filled = prepare(place, *operands, False)
    weight_pair = jnp.stack([out_weight, exchange(out_weight, 16)])
    weight_pair, *operands = lax.optimization_barrier((weight_pair, *operands))
    mine, reads, wy, qt, local_out = prepare(place, *operands, True, filled)
    weight_mine = lax.all_gather(weight_pair, "ctx", axis=0, axis_index_groups=rings)
    grad_full = lax.all_to_all(
        jnp.broadcast_to(out_grad[None], (8, WIDTH, 512)), "tp", 0, 0, tiled=True
    )
    weight_mine, state, saved = forward_states(mine, theirs, core, weight_mine)
    weight_other = exchange(weight_mine, 1)
    heads, part_mine, part_other = outputs(place, qt, local_out, state, grad_full)
    part = part_mine.astype(F32) + exchange(part_other, 1).astype(F32)
    ring_sum = lax.psum_scatter(
        part.astype(BF16).reshape(8, PAIRS, 512),
        "ctx",
        scatter_dimension=0,
        axis_index_groups=rings,
    )
    weight_grad = ring_sum[:WIDTH].astype(F32) + exchange(ring_sum[WIDTH:], 16).astype(F32)
    mixed = lax.all_to_all(
        mixed_parts(place, heads, weight_mine, weight_other), "tp", 0, 0, tiled=True
    )
    mixed = jnp.sum(mixed.astype(F32), axis=0).astype(BF16)
    head_grad, own = head_gradient(place, grad_full, weight_mine, weight_other, qt)
    end = backward_states(own, core, saved)
    query_grad, key_grad, value_grad, logit_grad = pull(
        place, queries, keys, beta_logit, reads, wy, state, end, head_grad
    )
    return mixed, query_grad, key_grad, value_grad, logit_grad, weight_grad


def solution(mesh):
    placed = P("ctx", "tp")
    return jax.shard_map(
        local,
        mesh=mesh,
        in_specs=(placed, placed, placed, P("tp", "ctx"), placed, placed),
        out_specs=(placed, placed, placed, placed, P("tp", "ctx"), placed),
        check_vma=False,
    )
```

```python
import functools
import math

import jax
import jax.numpy as jnp
from jax import lax
from jax.experimental import pallas as pl
from jax.experimental.pallas import tpu as pltpu
from jax.sharding import PartitionSpec as P

F32 = jnp.float32
BF16 = jnp.bfloat16
WIDTH = 128
VMEM = 56 << 20
PAIRS = 2 * WIDTH


def send(block, distance):
    devices = range(lax.axis_size("ctx"))
    route = [(i - distance, i) for i in devices if i - distance in devices]
    return lax.ppermute(block, "ctx", route)


def exchange(block, bit):
    route = [(i, i ^ bit) for i in range(lax.axis_size("ctx"))]
    return lax.ppermute(block, "ctx", route)


def split(x):
    high = x.astype(BF16)
    return high, (x - high.astype(F32)).astype(BF16)


def dot(a, b, ca=1, cb=0, passes=3):
    dims = (((ca,), (cb,)), ((), ()))
    mul = functools.partial(lax.dot_general, dimension_numbers=dims, preferred_element_type=F32)
    if passes == 1:
        return mul(a.astype(BF16), b.astype(BF16))
    if b.dtype == BF16:
        a_high, a_low = split(a)
        return mul(a_high, b) + mul(a_low, b)
    a_high, a_low = split(a)
    b_high, b_low = split(b)
    return mul(a_high, b_high) + (mul(a_low, b_high) + mul(a_high, b_low))


def inverse_norm(x):
    return lax.rsqrt(jnp.sum(x * x, axis=-1, keepdims=True) + 1e-06)


def order_of(shape, dim):
    p = lax.broadcasted_iota(jnp.int32, shape, dim)
    return 2 * (p & (WIDTH - 1)) + (p >> 7)


def column_of(row):
    shape = (PAIRS, PAIRS)
    time = lax.broadcasted_iota(jnp.int32, shape, 1)
    return jnp.sum(jnp.where(time == order_of(shape, 0), row, 0.0), axis=1, keepdims=True)


def row_of(column):
    shape = (PAIRS, PAIRS)
    time = lax.broadcasted_iota(jnp.int32, shape, 1)
    return jnp.sum(jnp.where(time == order_of(shape, 0), column, 0.0), axis=0, keepdims=True)


def visible_mask():
    shape = (WIDTH, PAIRS)
    token = lax.broadcasted_iota(jnp.int32, shape, 0)
    return (lax.broadcasted_iota(jnp.int32, shape, 1) & (WIDTH - 1)) <= token


def stacked(ref, i):
    start = i * PAIRS
    parts = [ref[:, start : start + WIDTH], ref[:, start + WIDTH : start + PAIRS]]
    return jnp.concatenate(parts, axis=0).astype(F32)


def prepare_kernel(mine, *refs):
    place, q_ref, k_ref, v_ref, logit_ref = refs[:5]
    first = 2 * (place[0] if mine else 1 - place[0])
    ab_ref, m_ref, wy_ref, qt_ref, local_ref = refs[-5:]
    two = range(2)
    shape = (PAIRS, PAIRS)
    row, col = order_of(shape, 0), order_of(shape, 1)
    identity = jnp.where(row == col, 1.0, 0.0).astype(F32)
    query = [q_ref[:, i * WIDTH : (i + 1) * WIDTH].astype(F32) for i in two]
    query = [x * inverse_norm(x) for x in query]
    key = [stacked(k_ref, i) for i in two]
    key = [x * inverse_norm(x) for x in key]
    strength = [2.0 / (1.0 + jnp.exp(-column_of(logit_ref[pl.ds(first + i, 1), :]))) for i in two]
    coupling = [jnp.where(col < row, strength[i] * dot(key[i], key[i], 1, 1), 0.0) for i in two]
    inverse = [identity - jnp.where((row >> 1) == (col >> 1), coupling[i], 0.0) for i in two]
    for level in range(1, 8):
        join = ((row >> (level + 1)) == (col >> (level + 1))) & ((row >> level) != (col >> level))
        edge = [jnp.where(join, coupling[i], 0.0) for i in two]
        step = [dot(inverse[i], edge[i], passes=1) for i in two]
        inverse = [inverse[i] - dot(step[i], inverse[i], passes=1) for i in two]
    rest = [identity - inverse[i] - dot(coupling[i], inverse[i]) for i in two]
    inverse = [inverse[i] + dot(inverse[i], rest[i], passes=1) for i in two]
    scores = [jnp.where(visible_mask(), dot(query[i], key[i], 1, 1), 0.0) for i in two]
    scaled = [strength[i] * jnp.concatenate([key[i], stacked(v_ref, i)], axis=1) for i in two]
    reads = [
        jnp.concatenate([dot(scores[i], inverse[i]), dot(key[i], inverse[i], 0, 0)], axis=0)
        for i in two
    ]
    product = [dot(reads[i], scaled[i]) for i in two]
    eye = identity[:WIDTH, :WIDTH]
    for i in two:
        ab_ref[i, :, :WIDTH] = (eye - product[i][WIDTH:, :WIDTH]).astype(BF16)
        ab_ref[i, :, WIDTH:] = product[i][WIDTH:, WIDTH:].astype(BF16)
        qt_ref[i] = query[i] - product[i][:WIDTH, :WIDTH]
        local_ref[i] = product[i][:WIDTH, WIDTH:]
        m_ref[i] = reads[i]
        wy_ref[i] = dot(inverse[i], scaled[i])


def slot(head, place):
    return (head + 2 * place[0]) % 4


def by_pair(*block):
    return pl.BlockSpec((2,) + block, lambda i, place: (i,) + (0,) * len(block))


def by_slot(*block):
    return pl.BlockSpec((2,) + block, lambda i, place: (i ^ place[0],) + (0,) * len(block))


def by_columns(width):
    return pl.BlockSpec((WIDTH, 2 * width), lambda i, place: (0, i))


def whole(*shape):
    return pl.BlockSpec(shape, lambda i, place: (0,) * len(shape))


def call(kernel, steps, in_specs, out_specs, out_shape, flops, moved, scratch=()):
    return pl.pallas_call(
        kernel,
        grid_spec=pltpu.PrefetchScalarGridSpec(
            num_scalar_prefetch=1,
            grid=(steps,),
            in_specs=in_specs,
            out_specs=out_specs,
            scratch_shapes=list(scratch),
        ),
        out_shape=out_shape,
        compiler_params=pltpu.CompilerParams(vmem_limit_bytes=VMEM),
        cost_estimate=pl.CostEstimate(flops=flops, bytes_accessed=moved, transcendentals=0),
    )


def arr(dtype, *shape):
    return jax.ShapeDtypeStruct(shape, dtype)


def prepare(place, queries, keys, values, logits, mine, filled=()):
    def pair(place):
        return place[0] if mine else 1 - place[0]

    def columns(width):
        return pl.BlockSpec((WIDTH, 2 * width), lambda i, place: (0, pair(place)))

    def heads(*block):
        return pl.BlockSpec((2,) + block, lambda i, place: (pair(place),) + (0,) * len(block))

    def stored(n):
        return arr(F32, 4, n, n)

    return pl.pallas_call(
        functools.partial(prepare_kernel, mine),
        grid_spec=pltpu.PrefetchScalarGridSpec(
            num_scalar_prefetch=1,
            grid=(1,),
            in_specs=[
                columns(WIDTH),
                columns(PAIRS),
                columns(PAIRS),
                whole(4, PAIRS),
            ]
            + [pl.BlockSpec(memory_space=pl.ANY)] * len(filled),
            out_specs=[
                pl.BlockSpec((2, WIDTH, PAIRS), lambda i, place: (0, 0, 0)),
                heads(PAIRS, PAIRS),
                heads(PAIRS, PAIRS),
                heads(WIDTH, WIDTH),
                heads(WIDTH, WIDTH),
            ],
        ),
        out_shape=[
            arr(BF16, 2, WIDTH, PAIRS),
            stored(PAIRS),
            stored(PAIRS),
            stored(WIDTH),
            stored(WIDTH),
        ],
        input_output_aliases={5 + i: 1 + i for i in range(len(filled))},
        compiler_params=pltpu.CompilerParams(vmem_limit_bytes=VMEM),
        cost_estimate=pl.CostEstimate(
            flops=(1 if mine else 100) << 20, bytes_accessed=1 << (16 if mine else 24), transcendentals=0
        ),
    )(place, queries, keys, values, logits, *filled)


STEPS = 4
BLOCKS = [(z, core, row) for z in range(2) for core in range(2) for row in range(2)]


def grad_block(place, step, z, core, row):
    column = pl.multiple_of(z * 256 + (core ^ place[0]) * 128, 128)
    return (row ^ place[1]) * 4 + step, slice(None), pl.ds(column, 128)


def weight_rows(mine_ref, other_ref):
    return jnp.concatenate([(mine_ref, other_ref)[core][z, row] for z, core, row in BLOCKS], axis=0)


def weight_tile():
    return pl.BlockSpec((2, 2, WIDTH, 512), lambda step, place: (step, 0, 0, 0))


def outputs_kernel(place, qt_ref, local_ref, state_ref, grad_ref, heads_ref, out_ref, held):
    step = pl.program_id(0)

    @pl.when(step == 0)
    def _():
        for head in range(4):
            result = dot(qt_ref[head], state_ref[slot(head, place)]) + local_ref[head]
            held[:, head * WIDTH : (head + 1) * WIDTH] = result.astype(BF16)
        heads_ref[...] = held[...]

    for z in range(2):
        rows = [grad_ref[grad_block(place, step, *block)] for block in BLOCKS[4 * z : 4 * z + 4]]
        product = lax.dot_general(
            jnp.concatenate(rows, axis=1),
            held[...],
            (((0,), (0,)), ((), ())),
            preferred_element_type=F32,
        )
        out_ref[z] = (product * (1.0 / 64.0)).astype(BF16)


def outputs(place, qt, local, state, grad_full):
    return call(
        outputs_kernel,
        STEPS,
        [whole(4, WIDTH, WIDTH), whole(4, WIDTH, WIDTH), whole(4, WIDTH, WIDTH), whole(8, WIDTH, 512)],
        [whole(WIDTH, 512), pl.BlockSpec((2, 512, 512), lambda step, place: (step, 0, 0))],
        [arr(BF16, WIDTH, 512), arr(BF16, 8, 512, 512)],
        2 * 128 * 512 * 4096,
        6 << 20,
        [pltpu.VMEM((WIDTH, 512), BF16)],
    )(place, qt, local, state, grad_full)


def mixed_kernel(place, heads_ref, mine_ref, other_ref, out_ref):
    step = pl.program_id(0)
    product = lax.dot_general(
        heads_ref[...],
        weight_rows(mine_ref, other_ref),
        (((1,), (1,)), ((), ())),
        preferred_element_type=F32,
    ).astype(BF16)
    for i, block in enumerate(BLOCKS):
        out_ref[grad_block(place, step, *block)] = product[:, i * WIDTH : (i + 1) * WIDTH]


def mixed_parts(place, heads, mine, other):
    return call(
        mixed_kernel,
        STEPS,
        [whole(WIDTH, 512), weight_tile(), weight_tile()],
        whole(8, WIDTH, 512),
        arr(BF16, 8, WIDTH, 512),
        2 * 128 * 512 * 4096,
        6 << 20,
    )(place, heads, mine, other)


def head_grad_kernel(place, grad_ref, mine_ref, other_ref, qt_ref, out_ref, own_ref):
    step = pl.program_id(0)
    blocks = [grad_ref[grad_block(place, step, *block)] for block in BLOCKS]
    total = jnp.dot(
        jnp.concatenate(blocks, axis=1),
        weight_rows(mine_ref, other_ref),
        preferred_element_type=F32,
    )

    @pl.when(step == 0)
    def _():
        out_ref[...] = total

    @pl.when(step > 0)
    def _():
        out_ref[...] += total

    @pl.when(step == STEPS - 1)
    def _():
        for head in range(4):
            grad = out_ref[:, head * WIDTH : (head + 1) * WIDTH]
            own_ref[slot(head, place)] = dot(qt_ref[head], grad, 0, 0).astype(BF16)


def head_gradient(place, grad_full, mine, other, qt):
    return call(
        head_grad_kernel,
        STEPS,
        [whole(8, WIDTH, 512), weight_tile(), weight_tile(), whole(4, WIDTH, WIDTH)],
        [whole(WIDTH, 512), whole(4, WIDTH, WIDTH)],
        [arr(F32, WIDTH, 512), arr(BF16, 4, WIDTH, WIDTH)],
        2 * 128 * 512 * 4096,
        6 << 20,
    )(place, grad_full, mine, other, qt)


def pull_kernel(
    place, q_ref, k_ref, logit_ref, m_ref, wy_ref, state_ref, end_ref, grad_ref,
    dq_ref, dk_ref, dv_ref, dlogit_ref,
):
    two = range(2)
    shape = (PAIRS, PAIRS)
    before = order_of(shape, 1) < order_of(shape, 0)
    query = [q_ref[:, i * WIDTH : (i + 1) * WIDTH].astype(F32) for i in two]
    query_scale = [inverse_norm(x) for x in query]
    query = [query[i] * query_scale[i] for i in two]
    key = [stacked(k_ref, i) for i in two]
    key_scale = [inverse_norm(x) for x in key]
    key = [key[i] * key_scale[i] for i in two]
    first = 2 * pl.program_id(0)
    logit = [column_of(logit_ref[pl.ds(first + i, 1), :]) for i in two]
    state = [state_ref[i] for i in two]
    end = [end_ref[i] for i in two]
    grad = [grad_ref[:, i * WIDTH : (i + 1) * WIDTH] for i in two]
    updates = [wy_ref[i, :, WIDTH:] - dot(wy_ref[i, :, :WIDTH], state[i]) for i in two]
    pulled = [dot(m_ref[i], jnp.concatenate([grad[i], end[i].astype(F32)], axis=0), 0, 0) for i in two]
    value_grad = [2.0 / (1.0 + jnp.exp(-logit[i])) * pulled[i] for i in two]
    cross = [
        dot(jnp.concatenate([grad[i], value_grad[i]], axis=0), updates[i], 1, 1) for i in two
    ]
    pairs = [
        jnp.concatenate(
            [
                jnp.where(visible_mask(), cross[i][:WIDTH], 0.0),
                jnp.where(before, -cross[i][WIDTH:], 0.0),
            ],
            axis=0,
        )
        for i in two
    ]
    forward = [dot(pairs[i], key[i]) for i in two]
    backward = [dot(pairs[i], jnp.concatenate([query[i], key[i]], axis=0), 0, 0) for i in two]
    by_state = [
        dot(jnp.concatenate([grad[i], -value_grad[i]], axis=0), state[i], 1, 1, passes=1)
        for i in two
    ]
    by_end = [dot(updates[i], end[i], 1, 1, passes=1) for i in two]
    for i in two:
        start = i * PAIRS
        dv_ref[:, start : start + WIDTH] = value_grad[i][:WIDTH].astype(BF16)
        dv_ref[:, start + WIDTH : start + PAIRS] = value_grad[i][WIDTH:].astype(BF16)
        slope = jnp.sum(pulled[i] * updates[i], axis=1, keepdims=True) / (1.0 + jnp.exp(logit[i]))
        dlogit_ref[pl.ds(first + i, 1), :] = row_of(slope)
        query_grad = forward[i][:WIDTH] + by_state[i][:WIDTH]
        query_grad = query_scale[i] * (
            query_grad - query[i] * jnp.sum(query[i] * query_grad, axis=1, keepdims=True)
        )
        dq_ref[:, i * WIDTH : (i + 1) * WIDTH] = query_grad.astype(BF16)
        key_grad = forward[i][WIDTH:] + backward[i] + by_end[i] + by_state[i][WIDTH:]
        key_grad = key_scale[i] * (
            key_grad - key[i] * jnp.sum(key[i] * key_grad, axis=1, keepdims=True)
        )
        dk_ref[:, start : start + WIDTH] = key_grad[:WIDTH].astype(BF16)
        dk_ref[:, start + WIDTH : start + PAIRS] = key_grad[WIDTH:].astype(BF16)


def pull(place, queries, keys, logits, reads, wy, state, end, head_grad):
    return call(
        pull_kernel,
        2,
        [
            by_columns(WIDTH),
            by_columns(PAIRS),
            whole(4, PAIRS),
            by_pair(PAIRS, PAIRS),
            by_pair(PAIRS, PAIRS),
            by_slot(WIDTH, WIDTH),
            by_slot(WIDTH, WIDTH),
            by_columns(WIDTH),
        ],
        [by_columns(WIDTH), by_columns(PAIRS), by_columns(PAIRS), whole(4, PAIRS)],
        [
            arr(BF16, WIDTH, 512),
            arr(BF16, WIDTH, 1024),
            arr(BF16, WIDTH, 1024),
            arr(F32, 4, PAIRS),
        ],
        4 * 14 * 2 * PAIRS**3,
        5 << 20,
    )(place, queries, keys, logits, reads, wy, state, end, head_grad)


def mul(a, b):
    return jnp.einsum("hij,hjk->hik", a, b, preferred_element_type=F32)


def mul_t(a, b):
    return jnp.einsum("hji,hjk->hik", a, b, preferred_element_type=F32)


def halves(x):
    return x[:, :, :WIDTH], x[:, :, WIDTH:]


def forward_states(mine, theirs, core, grad_full, gate):
    theirs = exchange(theirs, 1)
    even = jnp.where(core == 0, mine, theirs)
    odd = jnp.where(core == 0, theirs, mine)
    even_a, even_b = halves(even)
    odd_a, odd_b = halves(odd)
    joined = mul(odd_a, even)
    chip = jnp.concatenate(
        [joined[:, :, :WIDTH], joined[:, :, WIDTH:] + odd_b.astype(F32)], axis=2
    ).astype(BF16)
    one, two = send(chip, 2), send(chip, 4)
    window1, state = halves(one)
    step = mul(window1, two)
    state = state.astype(F32) + step[:, :, WIDTH:]
    window2 = step[:, :, :WIDTH].astype(BF16)
    step = mul(window2, send(jnp.concatenate([window2, state.astype(BF16)], axis=2), 4))
    state = state + step[:, :, WIDTH:]
    window4 = step[:, :, :WIDTH].astype(BF16)
    rounded = state.astype(BF16)
    both = jnp.concatenate([window4, rounded], axis=2)
    grad_full, both = lax.optimization_barrier((grad_full, both))
    near_a, near_b = halves(send(both, 8))
    mid_a, mid_b = halves(send(both, 16))
    far_b = send(rounded, 24)
    inner = (mid_b.astype(F32) + mul(mid_a, far_b)).astype(BF16)
    inner = (near_b.astype(F32) + mul(near_a, inner)).astype(BF16)
    first = (state + mul(window4, inner)).astype(BF16)
    window8 = mul(window4, near_a).astype(BF16)
    window12 = mul(window8, mid_a).astype(BF16)
    second = (mul(even_a, first) + even_b.astype(F32)).astype(BF16)
    kept = jnp.where(core == 0, first, second)
    given = jnp.where(core == 0, second, first)
    gate, given = lax.optimization_barrier((gate, given))
    state_in = jnp.concatenate([kept, exchange(given, 1)], axis=0)
    return grad_full, gate, state_in, (even_a, odd_a, window1, window2, window4, window8, window12)


def backward_states(own, core, saved):
    even_a, odd_a, window1, window2, window4, window8, window12 = saved
    mine, theirs = own[:2], exchange(own[2:], 1)
    even = jnp.where(core == 0, mine, theirs)
    odd = jnp.where(core == 0, theirs, mine)
    total = even.astype(F32) + mul_t(even_a, odd)
    for window, distance in ((window1, 2), (window2, 4)):
        passed = mul_t(window, total.astype(BF16)).astype(BF16)
        total = total + send(passed, -distance).astype(F32)
    rounded = total.astype(BF16)
    second = send(rounded, -2).astype(F32)
    for window, distance in ((window4, 10), (window8, 18), (window12, 26)):
        second += send(mul_t(window, rounded).astype(BF16), -distance).astype(F32)
    second = second.astype(BF16)
    first = (odd.astype(F32) + mul_t(odd_a, second)).astype(BF16)
    kept = jnp.where(core == 0, first, second)
    given = jnp.where(core == 0, second, first)
    return jnp.concatenate([kept, exchange(given, 1)], axis=0)


def local(queries, keys, values, beta_logit, out_weight, out_grad):
    index = lax.axis_index("ctx")
    core = index & 1
    place = jnp.stack([core, index >> 4]).astype(jnp.int32)
    rings = [[(half * 8 + z) * 2 + c for z in range(8)] for half in range(2) for c in range(2)]
    operands = (queries, keys, values, beta_logit)
    across = exchange(out_weight, 16)
    theirs, *filled = prepare(place, *operands, False)
    across, theirs = lax.optimization_barrier((across, theirs))
    weight_pair = jnp.stack([out_weight, across])
    weight_pair, *operands = lax.optimization_barrier((weight_pair, *operands))
    mine, reads, wy, qt, local_out = prepare(place, *operands, True, filled)
    weight_mine = lax.all_gather(weight_pair, "ctx", axis=0, axis_index_groups=rings)
    grad_full = lax.all_to_all(
        jnp.broadcast_to(out_grad[None], (8, WIDTH, 512)), "tp", 0, 0, tiled=True
    )
    grad_full, weight_mine, state, saved = forward_states(
        mine, theirs, core, grad_full, weight_mine
    )
    weight_other = exchange(weight_mine, 1)
    heads, part = outputs(place, qt, local_out, state, grad_full)
    ring_sum = lax.psum_scatter(
        part, "ctx", scatter_dimension=0, axis_index_groups=rings
    ).reshape(2, 2, WIDTH, 512)
    weight_grad = ring_sum[0, 0].astype(F32) + exchange(ring_sum[1, 0], 1).astype(F32)
    weight_grad += exchange(ring_sum[0, 1], 16).astype(F32)
    weight_grad += exchange(ring_sum[1, 1], 17).astype(F32)
    mixed = lax.all_to_all(
        mixed_parts(place, heads, weight_mine, weight_other), "tp", 0, 0, tiled=True
    )
    mixed = jnp.sum(mixed.astype(F32), axis=0).astype(BF16)
    head_grad, own = head_gradient(place, grad_full, weight_mine, weight_other, qt)
    end = backward_states(own, core, saved)
    query_grad, key_grad, value_grad, logit_grad = pull(
        place, queries, keys, beta_logit, reads, wy, state, end, head_grad
    )
    return mixed, query_grad, key_grad, value_grad, logit_grad, weight_grad


def solution(mesh):
    placed = P("ctx", "tp")
    return jax.shard_map(
        local,
        mesh=mesh,
        in_specs=(placed, placed, placed, P("tp", "ctx"), placed, placed),
        out_specs=(placed, placed, placed, placed, P("tp", "ctx"), placed),
        check_vma=False,
    )
```

```python
import functools
import math

import jax
import jax.numpy as jnp
from jax import lax
from jax.experimental import pallas as pl
from jax.experimental.pallas import tpu as pltpu
from jax.sharding import PartitionSpec as P

F32 = jnp.float32
BF16 = jnp.bfloat16
WIDTH = 128
VMEM = 62 << 20
PAIRS = 2 * WIDTH


def send(block, distance):
    devices = range(lax.axis_size("ctx"))
    route = [(i - distance, i) for i in devices if i - distance in devices]
    return lax.ppermute(block, "ctx", route)


def exchange(block, bit):
    route = [(i, i ^ bit) for i in range(lax.axis_size("ctx"))]
    return lax.ppermute(block, "ctx", route)


def split(x):
    high = x.astype(BF16)
    return high, (x - high.astype(F32)).astype(BF16)


def dot(a, b, ca=1, cb=0, passes=3):
    dims = (((ca,), (cb,)), ((), ()))
    mul = functools.partial(lax.dot_general, dimension_numbers=dims, preferred_element_type=F32)
    if passes == 1:
        return mul(a.astype(BF16), b.astype(BF16))
    if b.dtype == BF16:
        a_high, a_low = split(a)
        return mul(a_high, b) + mul(a_low, b)
    a_high, a_low = split(a)
    b_high, b_low = split(b)
    return mul(a_high, b_high) + (mul(a_low, b_high) + mul(a_high, b_low))


def inverse_norm(x):
    return lax.rsqrt(jnp.sum(x * x, axis=-1, keepdims=True) + 1e-06)


def order_of(shape, dim):
    p = lax.broadcasted_iota(jnp.int32, shape, dim)
    return 2 * (p & (WIDTH - 1)) + (p >> 7)


def column_of(row):
    shape = (PAIRS, PAIRS)
    time = lax.broadcasted_iota(jnp.int32, shape, 1)
    return jnp.sum(jnp.where(time == order_of(shape, 0), row, 0.0), axis=1, keepdims=True)


def row_of(column):
    shape = (PAIRS, PAIRS)
    time = lax.broadcasted_iota(jnp.int32, shape, 1)
    return jnp.sum(jnp.where(time == order_of(shape, 0), column, 0.0), axis=0, keepdims=True)


def visible_mask():
    shape = (WIDTH, PAIRS)
    token = lax.broadcasted_iota(jnp.int32, shape, 0)
    return (lax.broadcasted_iota(jnp.int32, shape, 1) & (WIDTH - 1)) <= token


def stacked(ref, i):
    start = i * PAIRS
    parts = [ref[:, start : start + WIDTH], ref[:, start + WIDTH : start + PAIRS]]
    return jnp.concatenate(parts, axis=0).astype(F32)


def prepare_kernel(mine, *refs):
    place, q_ref, k_ref, v_ref, logit_ref = refs[:5]
    first = 2 * (place[0] if mine else 1 - place[0])
    ab_ref, m_ref, wy_ref, qt_ref, local_ref = refs[-5:]
    two = range(2)
    shape = (PAIRS, PAIRS)
    row, col = order_of(shape, 0), order_of(shape, 1)
    identity = jnp.where(row == col, 1.0, 0.0).astype(F32)
    query = [q_ref[:, i * WIDTH : (i + 1) * WIDTH].astype(F32) for i in two]
    query = [x * inverse_norm(x) for x in query]
    key = [stacked(k_ref, i) for i in two]
    key = [x * inverse_norm(x) for x in key]
    strength = [2.0 / (1.0 + jnp.exp(-column_of(logit_ref[pl.ds(first + i, 1), :]))) for i in two]
    coupling = [jnp.where(col < row, strength[i] * dot(key[i], key[i], 1, 1), 0.0) for i in two]
    inverse = [identity - jnp.where((row >> 1) == (col >> 1), coupling[i], 0.0) for i in two]
    for level in range(1, 8):
        join = ((row >> (level + 1)) == (col >> (level + 1))) & ((row >> level) != (col >> level))
        edge = [jnp.where(join, coupling[i], 0.0) for i in two]
        step = [dot(inverse[i], edge[i], passes=1) for i in two]
        inverse = [inverse[i] - dot(step[i], inverse[i], passes=1) for i in two]
    rest = [identity - inverse[i] - dot(coupling[i], inverse[i]) for i in two]
    inverse = [inverse[i] + dot(inverse[i], rest[i], passes=1) for i in two]
    scores = [jnp.where(visible_mask(), dot(query[i], key[i], 1, 1), 0.0) for i in two]
    scaled = [strength[i] * jnp.concatenate([key[i], stacked(v_ref, i)], axis=1) for i in two]
    reads = [
        jnp.concatenate([dot(scores[i], inverse[i]), dot(key[i], inverse[i], 0, 0)], axis=0)
        for i in two
    ]
    product = [dot(reads[i], scaled[i]) for i in two]
    eye = identity[:WIDTH, :WIDTH]
    for i in two:
        ab_ref[i, :, :WIDTH] = (eye - product[i][WIDTH:, :WIDTH]).astype(BF16)
        ab_ref[i, :, WIDTH:] = product[i][WIDTH:, WIDTH:].astype(BF16)
        qt_ref[i] = query[i] - product[i][:WIDTH, :WIDTH]
        local_ref[i] = product[i][:WIDTH, WIDTH:]
        m_ref[i] = reads[i]
        wy_ref[i] = dot(inverse[i], scaled[i])


def slot(head, place):
    return (head + 2 * place[0]) % 4


def by_pair(*block):
    return pl.BlockSpec((2,) + block, lambda i, place: (i,) + (0,) * len(block))


def by_slot(*block):
    return pl.BlockSpec((2,) + block, lambda i, place: (i ^ place[0],) + (0,) * len(block))


def by_columns(width):
    return pl.BlockSpec((WIDTH, 2 * width), lambda i, place: (0, i))


def whole(*shape):
    return pl.BlockSpec(shape, lambda i, place: (0,) * len(shape))


def call(kernel, steps, in_specs, out_specs, out_shape, flops, moved, scratch=()):
    return pl.pallas_call(
        kernel,
        grid_spec=pltpu.PrefetchScalarGridSpec(
            num_scalar_prefetch=1,
            grid=(steps,),
            in_specs=in_specs,
            out_specs=out_specs,
            scratch_shapes=list(scratch),
        ),
        out_shape=out_shape,
        compiler_params=pltpu.CompilerParams(vmem_limit_bytes=VMEM),
        cost_estimate=pl.CostEstimate(flops=flops, bytes_accessed=moved, transcendentals=0),
    )


def arr(dtype, *shape):
    return jax.ShapeDtypeStruct(shape, dtype)


def prepare(place, queries, keys, values, logits, mine, filled=()):
    def pair(place):
        return place[0] if mine else 1 - place[0]

    def columns(width):
        return pl.BlockSpec((WIDTH, 2 * width), lambda i, place: (0, pair(place)))

    def heads(*block):
        return pl.BlockSpec((2,) + block, lambda i, place: (pair(place),) + (0,) * len(block))

    def stored(n):
        return arr(F32, 4, n, n)

    return pl.pallas_call(
        functools.partial(prepare_kernel, mine),
        grid_spec=pltpu.PrefetchScalarGridSpec(
            num_scalar_prefetch=1,
            grid=(1,),
            in_specs=[
                columns(WIDTH),
                columns(PAIRS),
                columns(PAIRS),
                whole(4, PAIRS),
            ]
            + [pl.BlockSpec(memory_space=pl.ANY)] * len(filled),
            out_specs=[
                pl.BlockSpec((2, WIDTH, PAIRS), lambda i, place: (0, 0, 0)),
                heads(PAIRS, PAIRS),
                heads(PAIRS, PAIRS),
                heads(WIDTH, WIDTH),
                heads(WIDTH, WIDTH),
            ],
        ),
        out_shape=[
            arr(BF16, 2, WIDTH, PAIRS),
            stored(PAIRS),
            stored(PAIRS),
            stored(WIDTH),
            stored(WIDTH),
        ],
        input_output_aliases={5 + i: 1 + i for i in range(len(filled))},
        compiler_params=pltpu.CompilerParams(vmem_limit_bytes=VMEM),
        cost_estimate=pl.CostEstimate(
            flops=(1 if mine else 100) << 20, bytes_accessed=1 << (16 if mine else 24), transcendentals=0
        ),
    )(place, queries, keys, values, logits, *filled)


STEPS = 4
BLOCKS = [(z, row) for z in range(2) for row in range(2)]


def grad_rows(place, step, own_ref, other_ref):
    def block(ref, z, row):
        column = pl.multiple_of(z * 256 + place[0] * 128, 128)
        return ref[(row ^ place[1]) * 4 + step, :, pl.ds(column, 128)]

    rows = [
        jnp.concatenate([block(ref, *place_of) for place_of in BLOCKS], axis=1)
        for ref in (own_ref, other_ref)
    ]
    return jnp.concatenate(rows, axis=0)


def weight_rows(ref):
    return jnp.concatenate([ref[z, row] for z, row in BLOCKS], axis=0)


def weight_tile():
    return pl.BlockSpec((2, 2, WIDTH, 512), lambda step, place: (step, 0, 0, 0))


def heads_kernel(place, qt_ref, local_ref, state_ref, heads_ref):
    for head in range(4):
        result = dot(qt_ref[head], state_ref[slot(head, place)]) + local_ref[head]
        heads_ref[:, head * WIDTH : (head + 1) * WIDTH] = result.astype(BF16)


def head_outputs(place, qt, local, state):
    square = whole(4, WIDTH, WIDTH)
    return call(
        heads_kernel,
        1,
        [square, square, square],
        whole(WIDTH, 512),
        arr(BF16, WIDTH, 512),
        2 * 4 * 128**3,
        1 << 20,
    )(place, qt, local, state)


def weight_terms_kernel(place, own_ref, other_ref, heads_ref, heads_other_ref, out_ref):
    product = lax.dot_general(
        grad_rows(place, pl.program_id(0), own_ref, other_ref),
        jnp.concatenate([heads_ref[...], heads_other_ref[...]], axis=0),
        (((0,), (0,)), ((), ())),
        preferred_element_type=F32,
    )
    product = (product * (1.0 / 64.0)).astype(BF16)
    for z in range(2):
        out_ref[z] = product[z * 256 : z * 256 + 256]


def weight_terms(place, grad_full, grad_other, heads, heads_other):
    return call(
        weight_terms_kernel,
        STEPS,
        [whole(8, WIDTH, 512), whole(8, WIDTH, 512), whole(WIDTH, 512), whole(WIDTH, 512)],
        pl.BlockSpec((2, 256, 512), lambda step, place: (step, 0, 0)),
        arr(BF16, 8, 256, 512),
        2 * 128 * 512 * 4096,
        5 << 20,
    )(place, grad_full, grad_other, heads, heads_other)


def mixed_kernel(place, heads_ref, heads_other_ref, weight_ref, out_ref):
    step = pl.program_id(0)
    product = lax.dot_general(
        jnp.concatenate([heads_ref[...], heads_other_ref[...]], axis=0),
        weight_rows(weight_ref),
        (((1,), (1,)), ((), ())),
        preferred_element_type=F32,
    ).astype(BF16)
    for i, (z, row) in enumerate(BLOCKS):
        owner = (row ^ place[1]) * 4 + step
        out_ref[owner, :, z * 128 : z * 128 + 128] = product[:, i * WIDTH : (i + 1) * WIDTH]


def mixed_parts(place, heads, heads_other, weight):
    return call(
        mixed_kernel,
        STEPS,
        [whole(WIDTH, 512), whole(WIDTH, 512), weight_tile()],
        whole(8, 256, 256),
        arr(BF16, 8, 256, 256),
        2 * 128 * 512 * 4096,
        3 << 20,
    )(place, heads, heads_other, weight)


def head_grad_kernel(place, own_ref, other_ref, weight_ref, kept_ref, given_ref):
    step = pl.program_id(0)
    total = jnp.dot(
        grad_rows(place, step, own_ref, other_ref),
        weight_rows(weight_ref),
        preferred_element_type=F32,
    )

    @pl.when(step == 0)
    def _():
        kept_ref[...] = total[:WIDTH]
        given_ref[...] = total[WIDTH:]

    @pl.when(step > 0)
    def _():
        kept_ref[...] += total[:WIDTH]
        given_ref[...] += total[WIDTH:]


def head_gradient(place, grad_full, grad_other, weight):
    part = arr(F32, WIDTH, 512)
    return call(
        head_grad_kernel,
        STEPS,
        [whole(8, WIDTH, 512), whole(8, WIDTH, 512), weight_tile()],
        [whole(WIDTH, 512), whole(WIDTH, 512)],
        [part, part],
        2 * 128 * 512 * 4096,
        5 << 20,
    )(place, grad_full, grad_other, weight)


def own_kernel(place, kept_ref, came_ref, qt_ref, grad_ref, mine_ref, theirs_ref):
    grad_ref[...] = kept_ref[...] + came_ref[...]
    for head in range(4):
        grad = grad_ref[:, head * WIDTH : (head + 1) * WIDTH]
        own = dot(qt_ref[head], grad, 0, 0).astype(BF16)

        @pl.when(place[0] == head // 2)
        def _():
            mine_ref[head % 2] = own

        @pl.when(place[0] != head // 2)
        def _():
            theirs_ref[head % 2] = own


def own_cotangent(place, kept, came, qt):
    pair = arr(BF16, 2, WIDTH, WIDTH)
    return call(
        own_kernel,
        1,
        [whole(WIDTH, 512), whole(WIDTH, 512), whole(4, WIDTH, WIDTH)],
        [whole(WIDTH, 512), whole(2, WIDTH, WIDTH), whole(2, WIDTH, WIDTH)],
        [arr(F32, WIDTH, 512), pair, pair],
        2 * 4 * 128**3,
        1 << 20,
    )(place, kept, came, qt)


def pull_kernel(
    place, q_ref, k_ref, logit_ref, m_ref, wy_ref, state_ref, end_ref, grad_ref,
    dq_ref, dk_ref, dv_ref, dlogit_ref,
):
    two = range(2)
    shape = (PAIRS, PAIRS)
    before = order_of(shape, 1) < order_of(shape, 0)
    query = [q_ref[:, i * WIDTH : (i + 1) * WIDTH].astype(F32) for i in two]
    query_scale = [inverse_norm(x) for x in query]
    query = [query[i] * query_scale[i] for i in two]
    key = [stacked(k_ref, i) for i in two]
    key_scale = [inverse_norm(x) for x in key]
    key = [key[i] * key_scale[i] for i in two]
    first = 2 * pl.program_id(0)
    logit = [column_of(logit_ref[pl.ds(first + i, 1), :]) for i in two]
    state = [state_ref[i] for i in two]
    end = [end_ref[i] for i in two]
    grad = [grad_ref[:, i * WIDTH : (i + 1) * WIDTH] for i in two]
    updates = [wy_ref[i, :, WIDTH:] - dot(wy_ref[i, :, :WIDTH], state[i]) for i in two]
    pulled = [dot(m_ref[i], jnp.concatenate([grad[i], end[i].astype(F32)], axis=0), 0, 0) for i in two]
    value_grad = [2.0 / (1.0 + jnp.exp(-logit[i])) * pulled[i] for i in two]
    cross = [
        dot(jnp.concatenate([grad[i], value_grad[i]], axis=0), updates[i], 1, 1) for i in two
    ]
    pairs = [
        jnp.concatenate(
            [
                jnp.where(visible_mask(), cross[i][:WIDTH], 0.0),
                jnp.where(before, -cross[i][WIDTH:], 0.0),
            ],
            axis=0,
        )
        for i in two
    ]
    forward = [dot(pairs[i], key[i]) for i in two]
    backward = [dot(pairs[i], jnp.concatenate([query[i], key[i]], axis=0), 0, 0) for i in two]
    by_state = [
        dot(jnp.concatenate([grad[i], -value_grad[i]], axis=0), state[i], 1, 1, passes=1)
        for i in two
    ]
    by_end = [dot(updates[i], end[i], 1, 1, passes=1) for i in two]
    for i in two:
        start = i * PAIRS
        dv_ref[:, start : start + WIDTH] = value_grad[i][:WIDTH].astype(BF16)
        dv_ref[:, start + WIDTH : start + PAIRS] = value_grad[i][WIDTH:].astype(BF16)
        slope = jnp.sum(pulled[i] * updates[i], axis=1, keepdims=True) / (1.0 + jnp.exp(logit[i]))
        dlogit_ref[pl.ds(first + i, 1), :] = row_of(slope)
        query_grad = forward[i][:WIDTH] + by_state[i][:WIDTH]
        query_grad = query_scale[i] * (
            query_grad - query[i] * jnp.sum(query[i] * query_grad, axis=1, keepdims=True)
        )
        dq_ref[:, i * WIDTH : (i + 1) * WIDTH] = query_grad.astype(BF16)
        key_grad = forward[i][WIDTH:] + backward[i] + by_end[i] + by_state[i][WIDTH:]
        key_grad = key_scale[i] * (
            key_grad - key[i] * jnp.sum(key[i] * key_grad, axis=1, keepdims=True)
        )
        dk_ref[:, start : start + WIDTH] = key_grad[:WIDTH].astype(BF16)
        dk_ref[:, start + WIDTH : start + PAIRS] = key_grad[WIDTH:].astype(BF16)


def pull(place, queries, keys, logits, reads, wy, state, end, head_grad):
    return call(
        pull_kernel,
        2,
        [
            by_columns(WIDTH),
            by_columns(PAIRS),
            whole(4, PAIRS),
            by_pair(PAIRS, PAIRS),
            by_pair(PAIRS, PAIRS),
            by_slot(WIDTH, WIDTH),
            by_slot(WIDTH, WIDTH),
            by_columns(WIDTH),
        ],
        [by_columns(WIDTH), by_columns(PAIRS), by_columns(PAIRS), whole(4, PAIRS)],
        [
            arr(BF16, WIDTH, 512),
            arr(BF16, WIDTH, 1024),
            arr(BF16, WIDTH, 1024),
            arr(F32, 4, PAIRS),
        ],
        4 * 14 * 2 * PAIRS**3,
        5 << 20,
    )(place, queries, keys, logits, reads, wy, state, end, head_grad)


def mul(a, b):
    return jnp.einsum("hij,hjk->hik", a, b, preferred_element_type=F32)


def mul_t(a, b):
    return jnp.einsum("hji,hjk->hik", a, b, preferred_element_type=F32)


def halves(x):
    return x[:, :, :WIDTH], x[:, :, WIDTH:]


def forward_states(mine, theirs, core, grad_full, gate):
    theirs = exchange(theirs, 1)
    even = jnp.where(core == 0, mine, theirs)
    odd = jnp.where(core == 0, theirs, mine)
    even_a, even_b = halves(even)
    odd_a, odd_b = halves(odd)
    joined = mul(odd_a, even)
    chip = jnp.concatenate(
        [joined[:, :, :WIDTH], joined[:, :, WIDTH:] + odd_b.astype(F32)], axis=2
    ).astype(BF16)
    one, two = send(chip, 2), send(chip, 4)
    window1, state = halves(one)
    step = mul(window1, two)
    state = state.astype(F32) + step[:, :, WIDTH:]
    window2 = step[:, :, :WIDTH].astype(BF16)
    step = mul(window2, send(jnp.concatenate([window2, state.astype(BF16)], axis=2), 4))
    state = state + step[:, :, WIDTH:]
    window4 = step[:, :, :WIDTH].astype(BF16)
    rounded = state.astype(BF16)
    both = jnp.concatenate([window4, rounded], axis=2)
    grad_full, both = lax.optimization_barrier((grad_full, both))
    near_a, near_b = halves(send(both, 8))
    mid_a, mid_b = halves(send(both, 16))
    far_b = send(rounded, 24)
    inner = (mid_b.astype(F32) + mul(mid_a, far_b)).astype(BF16)
    inner = (near_b.astype(F32) + mul(near_a, inner)).astype(BF16)
    first = (state + mul(window4, inner)).astype(BF16)
    window8 = mul(window4, near_a).astype(BF16)
    window12 = mul(window8, mid_a).astype(BF16)
    second = (mul(even_a, first) + even_b.astype(F32)).astype(BF16)
    kept = jnp.where(core == 0, first, second)
    given = jnp.where(core == 0, second, first)
    gate, given = lax.optimization_barrier((gate, given))
    state_in = jnp.concatenate([kept, exchange(given, 1)], axis=0)
    return grad_full, gate, state_in, (even_a, odd_a, window1, window2, window4, window8, window12)


def backward_states(mine, theirs, core, saved, gate):
    even_a, odd_a, window1, window2, window4, window8, window12 = saved
    theirs = exchange(theirs, 1)
    even = jnp.where(core == 0, mine, theirs)
    odd = jnp.where(core == 0, theirs, mine)
    total = even.astype(F32) + mul_t(even_a, odd)
    for window, distance in ((window1, 2), (window2, 4)):
        passed = mul_t(window, total.astype(BF16)).astype(BF16)
        if distance == 4:
            gate, passed = lax.optimization_barrier((gate, passed))
        total = total + send(passed, -distance).astype(F32)
    rounded = total.astype(BF16)
    second = send(rounded, -2).astype(F32)
    for window, distance in ((window4, 10), (window8, 18), (window12, 26)):
        second += send(mul_t(window, rounded).astype(BF16), -distance).astype(F32)
    second = second.astype(BF16)
    first = (odd.astype(F32) + mul_t(odd_a, second)).astype(BF16)
    kept = jnp.where(core == 0, first, second)
    given = jnp.where(core == 0, second, first)
    return gate, jnp.concatenate([kept, exchange(given, 1)], axis=0)


def local(queries, keys, values, beta_logit, out_weight, out_grad):
    index = lax.axis_index("ctx")
    core = index & 1
    place = jnp.stack([core, index >> 4]).astype(jnp.int32)
    rings = [[(half * 8 + z) * 2 + c for z in range(8)] for half in range(2) for c in range(2)]
    operands = (queries, keys, values, beta_logit)
    across = exchange(out_weight, 16)
    theirs, *filled = prepare(place, *operands, False)
    across, theirs = lax.optimization_barrier((across, theirs))
    weight_pair = jnp.stack([out_weight, across])
    weight_pair, *operands = lax.optimization_barrier((weight_pair, *operands))
    mine, reads, wy, qt, local_out = prepare(place, *operands, True, filled)
    weight_mine = lax.all_gather(weight_pair, "ctx", axis=0, axis_index_groups=rings)
    grad_full = lax.all_to_all(
        jnp.broadcast_to(out_grad[None], (8, WIDTH, 512)), "tp", 0, 0, tiled=True
    )
    grad_full, weight_mine, state, saved = forward_states(
        mine, theirs, core, grad_full, weight_mine
    )
    grad_other = exchange(grad_full, 1)
    heads = head_outputs(place, qt, local_out, state)
    heads_other = exchange(heads, 1)
    terms = weight_terms(place, grad_full, grad_other, heads, heads_other)
    ring_sum = lax.psum_scatter(
        terms, "ctx", scatter_dimension=0, axis_index_groups=rings
    ).reshape(2, WIDTH, 512)
    weight_grad = ring_sum[0].astype(F32) + exchange(ring_sum[1], 16).astype(F32)
    kept, given = head_gradient(place, grad_full, grad_other, weight_mine)
    head_grad, own, own_theirs = own_cotangent(place, kept, exchange(given, 1), qt)
    parts = mixed_parts(place, heads, heads_other, weight_mine)
    parts, end = backward_states(own, own_theirs, core, saved, parts)
    parts = lax.all_to_all(parts, "tp", 0, 0, tiled=True)
    sums = jnp.sum(parts.astype(F32), axis=0).astype(BF16)
    kept, came = sums[:WIDTH], exchange(sums[WIDTH:], 1)
    first, second = jnp.where(core == 0, kept, came), jnp.where(core == 0, came, kept)
    mixed = jnp.concatenate(
        [first[:, :WIDTH], second[:, :WIDTH], first[:, WIDTH:], second[:, WIDTH:]], axis=1
    )
    query_grad, key_grad, value_grad, logit_grad = pull(
        place, queries, keys, beta_logit, reads, wy, state, end, head_grad
    )
    return mixed, query_grad, key_grad, value_grad, logit_grad, weight_grad


def solution(mesh):
    placed = P("ctx", "tp")
    return jax.shard_map(
        local,
        mesh=mesh,
        in_specs=(placed, placed, placed, P("tp", "ctx"), placed, placed),
        out_specs=(placed, placed, placed, placed, P("tp", "ctx"), placed),
        check_vma=False,
    )
```

```python
import functools
import math

import jax
import jax.numpy as jnp
from jax import lax
from jax.experimental import pallas as pl
from jax.experimental.pallas import tpu as pltpu
from jax.sharding import PartitionSpec as P

F32 = jnp.float32
BF16 = jnp.bfloat16
WIDTH = 128
VMEM = 62 << 20
PAIRS = 2 * WIDTH


def send(block, distance):
    devices = range(lax.axis_size("ctx"))
    route = [(i - distance, i) for i in devices if i - distance in devices]
    return lax.ppermute(block, "ctx", route)


def exchange(block, bit):
    route = [(i, i ^ bit) for i in range(lax.axis_size("ctx"))]
    return lax.ppermute(block, "ctx", route)


def split(x):
    high = x.astype(BF16)
    return high, (x - high.astype(F32)).astype(BF16)


def dot(a, b, ca=1, cb=0, passes=3):
    dims = (((ca,), (cb,)), ((), ()))
    mul = functools.partial(lax.dot_general, dimension_numbers=dims, preferred_element_type=F32)
    if passes == 1:
        return mul(a.astype(BF16), b.astype(BF16))
    if b.dtype == BF16:
        a_high, a_low = split(a)
        return mul(a_high, b) + mul(a_low, b)
    a_high, a_low = split(a)
    b_high, b_low = split(b)
    return mul(a_high, b_high) + (mul(a_low, b_high) + mul(a_high, b_low))


def inverse_norm(x):
    return lax.rsqrt(jnp.sum(x * x, axis=-1, keepdims=True) + 1e-06)


def order_of(shape, dim):
    p = lax.broadcasted_iota(jnp.int32, shape, dim)
    return 2 * (p & (WIDTH - 1)) + (p >> 7)


def column_of(row):
    shape = (PAIRS, PAIRS)
    time = lax.broadcasted_iota(jnp.int32, shape, 1)
    return jnp.sum(jnp.where(time == order_of(shape, 0), row, 0.0), axis=1, keepdims=True)


def row_of(column):
    shape = (PAIRS, PAIRS)
    time = lax.broadcasted_iota(jnp.int32, shape, 1)
    return jnp.sum(jnp.where(time == order_of(shape, 0), column, 0.0), axis=0, keepdims=True)


def visible_mask():
    shape = (WIDTH, PAIRS)
    token = lax.broadcasted_iota(jnp.int32, shape, 0)
    return (lax.broadcasted_iota(jnp.int32, shape, 1) & (WIDTH - 1)) <= token


def stacked(ref, i):
    start = i * PAIRS
    parts = [ref[:, start : start + WIDTH], ref[:, start + WIDTH : start + PAIRS]]
    return jnp.concatenate(parts, axis=0).astype(F32)


def prepare_kernel(mine, *refs):
    place, q_ref, k_ref, v_ref, logit_ref = refs[:5]
    first = 2 * (place[0] if mine else 1 - place[0])
    ab_ref, m_ref, wy_ref, qt_ref, local_ref = refs[-5:]
    two = range(2)
    shape = (PAIRS, PAIRS)
    row, col = order_of(shape, 0), order_of(shape, 1)
    identity = jnp.where(row == col, 1.0, 0.0).astype(F32)
    query = [q_ref[:, i * WIDTH : (i + 1) * WIDTH].astype(F32) for i in two]
    query = [x * inverse_norm(x) for x in query]
    key = [stacked(k_ref, i) for i in two]
    key = [x * inverse_norm(x) for x in key]
    strength = [2.0 / (1.0 + jnp.exp(-column_of(logit_ref[pl.ds(first + i, 1), :]))) for i in two]
    coupling = [jnp.where(col < row, strength[i] * dot(key[i], key[i], 1, 1), 0.0) for i in two]
    inverse = [identity - jnp.where((row >> 1) == (col >> 1), coupling[i], 0.0) for i in two]
    for level in range(1, 8):
        join = ((row >> (level + 1)) == (col >> (level + 1))) & ((row >> level) != (col >> level))
        edge = [jnp.where(join, coupling[i], 0.0) for i in two]
        step = [dot(inverse[i], edge[i], passes=1) for i in two]
        inverse = [inverse[i] - dot(step[i], inverse[i], passes=1) for i in two]
    rest = [identity - inverse[i] - dot(coupling[i], inverse[i]) for i in two]
    inverse = [inverse[i] + dot(inverse[i], rest[i], passes=1) for i in two]
    scores = [jnp.where(visible_mask(), dot(query[i], key[i], 1, 1), 0.0) for i in two]
    scaled = [strength[i] * jnp.concatenate([key[i], stacked(v_ref, i)], axis=1) for i in two]
    reads = [
        jnp.concatenate([dot(scores[i], inverse[i]), dot(key[i], inverse[i], 0, 0)], axis=0)
        for i in two
    ]
    product = [dot(reads[i], scaled[i]) for i in two]
    eye = identity[:WIDTH, :WIDTH]
    for i in two:
        ab_ref[i, :, :WIDTH] = (eye - product[i][WIDTH:, :WIDTH]).astype(BF16)
        ab_ref[i, :, WIDTH:] = product[i][WIDTH:, WIDTH:].astype(BF16)
        qt_ref[i] = query[i] - product[i][:WIDTH, :WIDTH]
        local_ref[i] = product[i][:WIDTH, WIDTH:]
        m_ref[i] = reads[i]
        wy_ref[i] = dot(inverse[i], scaled[i])


def slot(head, place):
    return (head + 2 * place[0]) % 4


def by_pair(*block):
    return pl.BlockSpec((2,) + block, lambda i, place: (i,) + (0,) * len(block))


def by_slot(*block):
    return pl.BlockSpec((2,) + block, lambda i, place: (i ^ place[0],) + (0,) * len(block))


def by_columns(width):
    return pl.BlockSpec((WIDTH, 2 * width), lambda i, place: (0, i))


def whole(*shape):
    return pl.BlockSpec(shape, lambda i, place: (0,) * len(shape))


def call(kernel, steps, in_specs, out_specs, out_shape, flops, moved, scratch=()):
    return pl.pallas_call(
        kernel,
        grid_spec=pltpu.PrefetchScalarGridSpec(
            num_scalar_prefetch=1,
            grid=(steps,),
            in_specs=in_specs,
            out_specs=out_specs,
            scratch_shapes=list(scratch),
        ),
        out_shape=out_shape,
        compiler_params=pltpu.CompilerParams(vmem_limit_bytes=VMEM),
        cost_estimate=pl.CostEstimate(flops=flops, bytes_accessed=moved, transcendentals=0),
    )


def arr(dtype, *shape):
    return jax.ShapeDtypeStruct(shape, dtype)


def prepare(place, queries, keys, values, logits, mine, filled=()):
    def pair(place):
        return place[0] if mine else 1 - place[0]

    def columns(width):
        return pl.BlockSpec((WIDTH, 2 * width), lambda i, place: (0, pair(place)))

    def heads(*block):
        return pl.BlockSpec((2,) + block, lambda i, place: (pair(place),) + (0,) * len(block))

    def stored(n):
        return arr(F32, 4, n, n)

    return pl.pallas_call(
        functools.partial(prepare_kernel, mine),
        grid_spec=pltpu.PrefetchScalarGridSpec(
            num_scalar_prefetch=1,
            grid=(1,),
            in_specs=[
                columns(WIDTH),
                columns(PAIRS),
                columns(PAIRS),
                whole(4, PAIRS),
            ]
            + [pl.BlockSpec(memory_space=pl.ANY)] * len(filled),
            out_specs=[
                pl.BlockSpec((2, WIDTH, PAIRS), lambda i, place: (0, 0, 0)),
                heads(PAIRS, PAIRS),
                heads(PAIRS, PAIRS),
                heads(WIDTH, WIDTH),
                heads(WIDTH, WIDTH),
            ],
        ),
        out_shape=[
            arr(BF16, 2, WIDTH, PAIRS),
            stored(PAIRS),
            stored(PAIRS),
            stored(WIDTH),
            stored(WIDTH),
        ],
        input_output_aliases={5 + i: 1 + i for i in range(len(filled))},
        compiler_params=pltpu.CompilerParams(vmem_limit_bytes=VMEM),
        cost_estimate=pl.CostEstimate(
            flops=(1 if mine else 100) << 20, bytes_accessed=1 << (16 if mine else 24), transcendentals=0
        ),
    )(place, queries, keys, values, logits, *filled)


STEPS = 4
BLOCKS = [(z, row) for z in range(2) for row in range(2)]


def grad_rows(place, step, own_ref, other_ref):
    def block(ref, z, row):
        column = pl.multiple_of(z * 256 + place[0] * 128, 128)
        return ref[(row ^ place[1]) * 4 + step, :, pl.ds(column, 128)]

    rows = [
        jnp.concatenate([block(ref, *place_of) for place_of in BLOCKS], axis=1)
        for ref in (own_ref, other_ref)
    ]
    return jnp.concatenate(rows, axis=0)


def weight_rows(ref):
    return jnp.concatenate([ref[z, row] for z, row in BLOCKS], axis=0)


def weight_tile():
    return pl.BlockSpec((2, 2, WIDTH, 512), lambda step, place: (step, 0, 0, 0))


def heads_kernel(place, qt_ref, local_ref, state_ref, heads_ref):
    for head in range(4):
        result = dot(qt_ref[head], state_ref[slot(head, place)]) + local_ref[head]
        heads_ref[:, head * WIDTH : (head + 1) * WIDTH] = result.astype(BF16)


def head_outputs(place, qt, local, state):
    square = whole(4, WIDTH, WIDTH)
    return call(
        heads_kernel,
        1,
        [square, square, square],
        whole(WIDTH, 512),
        arr(BF16, WIDTH, 512),
        2 * 4 * 128**3,
        1 << 20,
    )(place, qt, local, state)


def weight_terms_kernel(place, own_ref, other_ref, heads_ref, heads_other_ref, out_ref):
    product = lax.dot_general(
        grad_rows(place, pl.program_id(0), own_ref, other_ref),
        jnp.concatenate([heads_ref[...], heads_other_ref[...]], axis=0),
        (((0,), (0,)), ((), ())),
        preferred_element_type=F32,
    )
    product = (product * (1.0 / 64.0)).astype(BF16)
    for z in range(2):
        out_ref[z] = product[z * 256 : z * 256 + 256]


def weight_terms(place, grad_full, grad_other, heads, heads_other):
    return call(
        weight_terms_kernel,
        STEPS,
        [whole(8, WIDTH, 512), whole(8, WIDTH, 512), whole(WIDTH, 512), whole(WIDTH, 512)],
        pl.BlockSpec((2, 256, 512), lambda step, place: (step, 0, 0)),
        arr(BF16, 8, 256, 512),
        2 * 128 * 512 * 4096,
        5 << 20,
    )(place, grad_full, grad_other, heads, heads_other)


def mixed_kernel(place, heads_ref, heads_other_ref, weight_ref, out_ref):
    step = pl.program_id(0)
    product = lax.dot_general(
        jnp.concatenate([heads_ref[...], heads_other_ref[...]], axis=0),
        weight_rows(weight_ref),
        (((1,), (1,)), ((), ())),
        preferred_element_type=F32,
    ).astype(BF16)
    for i, (z, row) in enumerate(BLOCKS):
        owner = (row ^ place[1]) * 4 + step
        out_ref[owner, :, z * 128 : z * 128 + 128] = product[:, i * WIDTH : (i + 1) * WIDTH]


def mixed_parts(place, heads, heads_other, weight):
    return call(
        mixed_kernel,
        STEPS,
        [whole(WIDTH, 512), whole(WIDTH, 512), weight_tile()],
        whole(8, 256, 256),
        arr(BF16, 8, 256, 256),
        2 * 128 * 512 * 4096,
        3 << 20,
    )(place, heads, heads_other, weight)


def head_grad_kernel(place, own_ref, other_ref, weight_ref, kept_ref, given_ref):
    step = pl.program_id(0)
    total = jnp.dot(
        grad_rows(place, step, own_ref, other_ref),
        weight_rows(weight_ref),
        preferred_element_type=F32,
    )

    @pl.when(step == 0)
    def _():
        kept_ref[...] = total[:WIDTH]
        given_ref[...] = total[WIDTH:]

    @pl.when(step > 0)
    def _():
        kept_ref[...] += total[:WIDTH]
        given_ref[...] += total[WIDTH:]


def head_gradient(place, grad_full, grad_other, weight):
    part = arr(F32, WIDTH, 512)
    return call(
        head_grad_kernel,
        STEPS,
        [whole(8, WIDTH, 512), whole(8, WIDTH, 512), weight_tile()],
        [whole(WIDTH, 512), whole(WIDTH, 512)],
        [part, part],
        2 * 128 * 512 * 4096,
        5 << 20,
    )(place, grad_full, grad_other, weight)


def own_kernel(place, kept_ref, came_ref, qt_ref, grad_ref, mine_ref, theirs_ref):
    grad_ref[...] = kept_ref[...] + came_ref[...]
    for head in range(4):
        grad = grad_ref[:, head * WIDTH : (head + 1) * WIDTH]
        own = dot(qt_ref[head], grad, 0, 0).astype(BF16)

        @pl.when(place[0] == head // 2)
        def _():
            mine_ref[head % 2] = own

        @pl.when(place[0] != head // 2)
        def _():
            theirs_ref[head % 2] = own


def own_cotangent(place, kept, came, qt):
    pair = arr(BF16, 2, WIDTH, WIDTH)
    return call(
        own_kernel,
        1,
        [whole(WIDTH, 512), whole(WIDTH, 512), whole(4, WIDTH, WIDTH)],
        [whole(WIDTH, 512), whole(2, WIDTH, WIDTH), whole(2, WIDTH, WIDTH)],
        [arr(F32, WIDTH, 512), pair, pair],
        2 * 4 * 128**3,
        1 << 20,
    )(place, kept, came, qt)


def pull_kernel(
    place, q_ref, k_ref, logit_ref, m_ref, wy_ref, state_ref, end_ref, grad_ref,
    dq_ref, dk_ref, dv_ref, dlogit_ref,
):
    two = range(2)
    shape = (PAIRS, PAIRS)
    before = order_of(shape, 1) < order_of(shape, 0)
    query = [q_ref[:, i * WIDTH : (i + 1) * WIDTH].astype(F32) for i in two]
    query_scale = [inverse_norm(x) for x in query]
    query = [query[i] * query_scale[i] for i in two]
    key = [stacked(k_ref, i) for i in two]
    key_scale = [inverse_norm(x) for x in key]
    key = [key[i] * key_scale[i] for i in two]
    first = 2 * pl.program_id(0)
    logit = [column_of(logit_ref[pl.ds(first + i, 1), :]) for i in two]
    state = [state_ref[i] for i in two]
    end = [end_ref[i] for i in two]
    grad = [grad_ref[:, i * WIDTH : (i + 1) * WIDTH] for i in two]
    updates = [wy_ref[i, :, WIDTH:] - dot(wy_ref[i, :, :WIDTH], state[i]) for i in two]
    pulled = [dot(m_ref[i], jnp.concatenate([grad[i], end[i].astype(F32)], axis=0), 0, 0) for i in two]
    value_grad = [2.0 / (1.0 + jnp.exp(-logit[i])) * pulled[i] for i in two]
    cross = [
        dot(jnp.concatenate([grad[i], value_grad[i]], axis=0), updates[i], 1, 1) for i in two
    ]
    pairs = [
        jnp.concatenate(
            [
                jnp.where(visible_mask(), cross[i][:WIDTH], 0.0),
                jnp.where(before, -cross[i][WIDTH:], 0.0),
            ],
            axis=0,
        )
        for i in two
    ]
    forward = [dot(pairs[i], key[i]) for i in two]
    backward = [dot(pairs[i], jnp.concatenate([query[i], key[i]], axis=0), 0, 0) for i in two]
    by_state = [
        dot(jnp.concatenate([grad[i], -value_grad[i]], axis=0), state[i], 1, 1, passes=1)
        for i in two
    ]
    by_end = [dot(updates[i], end[i], 1, 1, passes=1) for i in two]
    for i in two:
        start = i * PAIRS
        dv_ref[:, start : start + WIDTH] = value_grad[i][:WIDTH].astype(BF16)
        dv_ref[:, start + WIDTH : start + PAIRS] = value_grad[i][WIDTH:].astype(BF16)
        slope = jnp.sum(pulled[i] * updates[i], axis=1, keepdims=True) / (1.0 + jnp.exp(logit[i]))
        dlogit_ref[pl.ds(first + i, 1), :] = row_of(slope)
        query_grad = forward[i][:WIDTH] + by_state[i][:WIDTH]
        query_grad = query_scale[i] * (
            query_grad - query[i] * jnp.sum(query[i] * query_grad, axis=1, keepdims=True)
        )
        dq_ref[:, i * WIDTH : (i + 1) * WIDTH] = query_grad.astype(BF16)
        key_grad = forward[i][WIDTH:] + backward[i] + by_end[i] + by_state[i][WIDTH:]
        key_grad = key_scale[i] * (
            key_grad - key[i] * jnp.sum(key[i] * key_grad, axis=1, keepdims=True)
        )
        dk_ref[:, start : start + WIDTH] = key_grad[:WIDTH].astype(BF16)
        dk_ref[:, start + WIDTH : start + PAIRS] = key_grad[WIDTH:].astype(BF16)


def pull(place, queries, keys, logits, reads, wy, state, end, head_grad):
    return call(
        pull_kernel,
        2,
        [
            by_columns(WIDTH),
            by_columns(PAIRS),
            whole(4, PAIRS),
            by_pair(PAIRS, PAIRS),
            by_pair(PAIRS, PAIRS),
            by_slot(WIDTH, WIDTH),
            by_slot(WIDTH, WIDTH),
            by_columns(WIDTH),
        ],
        [by_columns(WIDTH), by_columns(PAIRS), by_columns(PAIRS), whole(4, PAIRS)],
        [
            arr(BF16, WIDTH, 512),
            arr(BF16, WIDTH, 1024),
            arr(BF16, WIDTH, 1024),
            arr(F32, 4, PAIRS),
        ],
        4 * 14 * 2 * PAIRS**3,
        5 << 20,
    )(place, queries, keys, logits, reads, wy, state, end, head_grad)


def mul(a, b):
    return jnp.einsum("hij,hjk->hik", a, b, preferred_element_type=F32)


def mul_t(a, b):
    return jnp.einsum("hji,hjk->hik", a, b, preferred_element_type=F32)


def halves(x):
    return x[:, :, :WIDTH], x[:, :, WIDTH:]


def forward_states(place, mine, theirs, core, grad_full, weight):
    theirs = exchange(theirs, 1)
    even = jnp.where(core == 0, mine, theirs)
    odd = jnp.where(core == 0, theirs, mine)
    even_a, even_b = halves(even)
    odd_a, odd_b = halves(odd)
    joined = mul(odd_a, even)
    chip = jnp.concatenate(
        [joined[:, :, :WIDTH], joined[:, :, WIDTH:] + odd_b.astype(F32)], axis=2
    ).astype(BF16)
    one, two = send(chip, 2), send(chip, 4)
    window1, state = halves(one)
    step = mul(window1, two)
    state = state.astype(F32) + step[:, :, WIDTH:]
    window2 = step[:, :, :WIDTH].astype(BF16)
    step = mul(window2, send(jnp.concatenate([window2, state.astype(BF16)], axis=2), 4))
    state = state + step[:, :, WIDTH:]
    window4 = step[:, :, :WIDTH].astype(BF16)
    rounded = state.astype(BF16)
    both = jnp.concatenate([window4, rounded], axis=2)
    grad_full, both = lax.optimization_barrier((grad_full, both))
    near_a, near_b = halves(send(both, 8))
    mid_a, mid_b = halves(send(both, 16))
    far_b = send(rounded, 24)
    grad_other = exchange(grad_full, 1)
    kept_grad, given_grad = head_gradient(place, grad_full, grad_other, weight)
    kept_grad, given_grad, near_a, near_b, mid_a, mid_b, far_b = lax.optimization_barrier(
        (kept_grad, given_grad, near_a, near_b, mid_a, mid_b, far_b)
    )
    head_grad = (kept_grad, exchange(given_grad, 1))
    inner = (mid_b.astype(F32) + mul(mid_a, far_b)).astype(BF16)
    inner = (near_b.astype(F32) + mul(near_a, inner)).astype(BF16)
    first = (state + mul(window4, inner)).astype(BF16)
    window8 = mul(window4, near_a).astype(BF16)
    window12 = mul(window8, mid_a).astype(BF16)
    second = (mul(even_a, first) + even_b.astype(F32)).astype(BF16)
    kept = jnp.where(core == 0, first, second)
    given = jnp.where(core == 0, second, first)
    state_in = jnp.concatenate([kept, exchange(given, 1)], axis=0)
    return grad_full, grad_other, head_grad, state_in, (even_a, odd_a, window1, window2, window4, window8, window12)


def backward_states(mine, theirs, core, saved, gate):
    even_a, odd_a, window1, window2, window4, window8, window12 = saved
    theirs = exchange(theirs, 1)
    even = jnp.where(core == 0, mine, theirs)
    odd = jnp.where(core == 0, theirs, mine)
    total = even.astype(F32) + mul_t(even_a, odd)
    for window, distance in ((window1, 2), (window2, 4)):
        passed = mul_t(window, total.astype(BF16)).astype(BF16)
        if distance == 4:
            gate, passed = lax.optimization_barrier((gate, passed))
        total = total + send(passed, -distance).astype(F32)
    rounded = total.astype(BF16)
    second = send(rounded, -2).astype(F32)
    for window, distance in ((window4, 10), (window8, 18), (window12, 26)):
        second += send(mul_t(window, rounded).astype(BF16), -distance).astype(F32)
    second = second.astype(BF16)
    first = (odd.astype(F32) + mul_t(odd_a, second)).astype(BF16)
    kept = jnp.where(core == 0, first, second)
    given = jnp.where(core == 0, second, first)
    return gate, jnp.concatenate([kept, exchange(given, 1)], axis=0)


def local(queries, keys, values, beta_logit, out_weight, out_grad):
    index = lax.axis_index("ctx")
    core = index & 1
    place = jnp.stack([core, index >> 4]).astype(jnp.int32)
    rings = [[(half * 8 + z) * 2 + c for z in range(8)] for half in range(2) for c in range(2)]
    operands = (queries, keys, values, beta_logit)
    across = exchange(out_weight, 16)
    theirs, *filled = prepare(place, *operands, False)
    across, theirs = lax.optimization_barrier((across, theirs))
    weight_pair = jnp.stack([out_weight, across])
    weight_pair, *operands = lax.optimization_barrier((weight_pair, *operands))
    mine, reads, wy, qt, local_out = prepare(place, *operands, True, filled)
    weight_mine = lax.all_gather(weight_pair, "ctx", axis=0, axis_index_groups=rings)
    grad_full = lax.all_to_all(
        jnp.broadcast_to(out_grad[None], (8, WIDTH, 512)), "tp", 0, 0, tiled=True
    )
    grad_full, grad_other, head_grad, state, saved = forward_states(
        place, mine, theirs, core, grad_full, weight_mine
    )
    heads = head_outputs(place, qt, local_out, state)
    heads_other = exchange(heads, 1)
    terms = weight_terms(place, grad_full, grad_other, heads, heads_other)
    ring_sum = lax.psum_scatter(
        terms, "ctx", scatter_dimension=0, axis_index_groups=rings
    ).reshape(2, WIDTH, 512)
    head_grad, own, own_theirs = own_cotangent(place, *head_grad, qt)
    parts = mixed_parts(place, heads, heads_other, weight_mine)
    parts, end = backward_states(own, own_theirs, core, saved, parts)
    end, ring_sum = lax.optimization_barrier((end, ring_sum))
    weight_grad = ring_sum[0].astype(F32) + exchange(ring_sum[1], 16).astype(F32)
    parts = lax.all_to_all(parts, "tp", 0, 0, tiled=True)
    sums = jnp.sum(parts.astype(F32), axis=0).astype(BF16)
    kept, came = sums[:WIDTH], exchange(sums[WIDTH:], 1)
    first, second = jnp.where(core == 0, kept, came), jnp.where(core == 0, came, kept)
    mixed = jnp.concatenate(
        [first[:, :WIDTH], second[:, :WIDTH], first[:, WIDTH:], second[:, WIDTH:]], axis=1
    )
    query_grad, key_grad, value_grad, logit_grad = pull(
        place, queries, keys, beta_logit, reads, wy, state, end, head_grad
    )
    return mixed, query_grad, key_grad, value_grad, logit_grad, weight_grad


def solution(mesh):
    placed = P("ctx", "tp")
    return jax.shard_map(
        local,
        mesh=mesh,
        in_specs=(placed, placed, placed, P("tp", "ctx"), placed, placed),
        out_specs=(placed, placed, placed, placed, P("tp", "ctx"), placed),
        check_vma=False,
    )
```

```python
import functools
import math

import jax
import jax.numpy as jnp
from jax import lax
from jax.experimental import pallas as pl
from jax.experimental.pallas import tpu as pltpu
from jax.sharding import PartitionSpec as P

F32 = jnp.float32
BF16 = jnp.bfloat16
WIDTH = 128
VMEM = 62 << 20
PAIRS = 2 * WIDTH


def send(block, distance):
    devices = range(lax.axis_size("ctx"))
    route = [(i - distance, i) for i in devices if i - distance in devices]
    return lax.ppermute(block, "ctx", route)


def exchange(block, bit):
    route = [(i, i ^ bit) for i in range(lax.axis_size("ctx"))]
    return lax.ppermute(block, "ctx", route)


def split(x):
    high = x.astype(BF16)
    return high, (x - high.astype(F32)).astype(BF16)


def dot(a, b, ca=1, cb=0, passes=3):
    dims = (((ca,), (cb,)), ((), ()))
    mul = functools.partial(lax.dot_general, dimension_numbers=dims, preferred_element_type=F32)
    if passes == 1:
        return mul(a.astype(BF16), b.astype(BF16))
    if b.dtype == BF16:
        a_high, a_low = split(a)
        return mul(a_high, b) + mul(a_low, b)
    a_high, a_low = split(a)
    b_high, b_low = split(b)
    return mul(a_high, b_high) + (mul(a_low, b_high) + mul(a_high, b_low))


def inverse_norm(x):
    return lax.rsqrt(jnp.sum(x * x, axis=-1, keepdims=True) + 1e-06)


def order_of(shape, dim):
    p = lax.broadcasted_iota(jnp.int32, shape, dim)
    return 2 * (p & (WIDTH - 1)) + (p >> 7)


def column_of(row):
    shape = (PAIRS, PAIRS)
    time = lax.broadcasted_iota(jnp.int32, shape, 1)
    return jnp.sum(jnp.where(time == order_of(shape, 0), row, 0.0), axis=1, keepdims=True)


def row_of(column):
    shape = (PAIRS, PAIRS)
    time = lax.broadcasted_iota(jnp.int32, shape, 1)
    return jnp.sum(jnp.where(time == order_of(shape, 0), column, 0.0), axis=0, keepdims=True)


def visible_mask():
    shape = (WIDTH, PAIRS)
    token = lax.broadcasted_iota(jnp.int32, shape, 0)
    return (lax.broadcasted_iota(jnp.int32, shape, 1) & (WIDTH - 1)) <= token


def stacked(ref, i):
    start = i * PAIRS
    parts = [ref[:, start : start + WIDTH], ref[:, start + WIDTH : start + PAIRS]]
    return jnp.concatenate(parts, axis=0).astype(F32)


def prepare_kernel(mine, *refs):
    place, q_ref, k_ref, v_ref, logit_ref = refs[:5]
    first = 2 * (place[0] if mine else 1 - place[0])
    ab_ref, m_ref, wy_ref, qt_ref, local_ref = refs[-5:]
    two = range(2)
    shape = (PAIRS, PAIRS)
    row, col = order_of(shape, 0), order_of(shape, 1)
    identity = jnp.where(row == col, 1.0, 0.0).astype(F32)
    query = [q_ref[:, i * WIDTH : (i + 1) * WIDTH].astype(F32) for i in two]
    query = [x * inverse_norm(x) for x in query]
    key = [stacked(k_ref, i) for i in two]
    key = [x * inverse_norm(x) for x in key]
    strength = [2.0 / (1.0 + jnp.exp(-column_of(logit_ref[pl.ds(first + i, 1), :]))) for i in two]
    coupling = [jnp.where(col < row, strength[i] * dot(key[i], key[i], 1, 1), 0.0) for i in two]
    inverse = [identity - jnp.where((row >> 1) == (col >> 1), coupling[i], 0.0) for i in two]
    for level in range(1, 8):
        join = ((row >> (level + 1)) == (col >> (level + 1))) & ((row >> level) != (col >> level))
        edge = [jnp.where(join, coupling[i], 0.0) for i in two]
        step = [dot(inverse[i], edge[i], passes=1) for i in two]
        inverse = [inverse[i] - dot(step[i], inverse[i], passes=1) for i in two]
    rest = [identity - inverse[i] - dot(coupling[i], inverse[i]) for i in two]
    inverse = [inverse[i] + dot(inverse[i], rest[i], passes=1) for i in two]
    scores = [jnp.where(visible_mask(), dot(query[i], key[i], 1, 1), 0.0) for i in two]
    scaled = [strength[i] * jnp.concatenate([key[i], stacked(v_ref, i)], axis=1) for i in two]
    reads = [
        jnp.concatenate([dot(scores[i], inverse[i]), dot(key[i], inverse[i], 0, 0)], axis=0)
        for i in two
    ]
    product = [dot(reads[i], scaled[i]) for i in two]
    eye = identity[:WIDTH, :WIDTH]
    for i in two:
        ab_ref[i, :, :WIDTH] = (eye - product[i][WIDTH:, :WIDTH]).astype(BF16)
        ab_ref[i, :, WIDTH:] = product[i][WIDTH:, WIDTH:].astype(BF16)
        qt_ref[i] = query[i] - product[i][:WIDTH, :WIDTH]
        local_ref[i] = product[i][:WIDTH, WIDTH:]
        m_ref[i] = reads[i]
        wy_ref[i] = dot(inverse[i], scaled[i])


def slot(head, place):
    return (head + 2 * place[0]) % 4


def by_pair(*block):
    return pl.BlockSpec((2,) + block, lambda i, place: (i,) + (0,) * len(block))


def by_slot(*block):
    return pl.BlockSpec((2,) + block, lambda i, place: (i ^ place[0],) + (0,) * len(block))


def by_columns(width):
    return pl.BlockSpec((WIDTH, 2 * width), lambda i, place: (0, i))


def whole(*shape):
    return pl.BlockSpec(shape, lambda i, place: (0,) * len(shape))


def call(kernel, steps, in_specs, out_specs, out_shape, flops, moved, scratch=()):
    return pl.pallas_call(
        kernel,
        grid_spec=pltpu.PrefetchScalarGridSpec(
            num_scalar_prefetch=1,
            grid=(steps,),
            in_specs=in_specs,
            out_specs=out_specs,
            scratch_shapes=list(scratch),
        ),
        out_shape=out_shape,
        compiler_params=pltpu.CompilerParams(vmem_limit_bytes=VMEM),
        cost_estimate=pl.CostEstimate(flops=flops, bytes_accessed=moved, transcendentals=0),
    )


def arr(dtype, *shape):
    return jax.ShapeDtypeStruct(shape, dtype)


def prepare(place, queries, keys, values, logits, mine, filled=()):
    def pair(place):
        return place[0] if mine else 1 - place[0]

    def columns(width):
        return pl.BlockSpec((WIDTH, 2 * width), lambda i, place: (0, pair(place)))

    def heads(*block):
        return pl.BlockSpec((2,) + block, lambda i, place: (pair(place),) + (0,) * len(block))

    def stored(n):
        return arr(F32, 4, n, n)

    return pl.pallas_call(
        functools.partial(prepare_kernel, mine),
        grid_spec=pltpu.PrefetchScalarGridSpec(
            num_scalar_prefetch=1,
            grid=(1,),
            in_specs=[
                columns(WIDTH),
                columns(PAIRS),
                columns(PAIRS),
                whole(4, PAIRS),
            ]
            + [pl.BlockSpec(memory_space=pl.ANY)] * len(filled),
            out_specs=[
                pl.BlockSpec((2, WIDTH, PAIRS), lambda i, place: (0, 0, 0)),
                heads(PAIRS, PAIRS),
                heads(PAIRS, PAIRS),
                heads(WIDTH, WIDTH),
                heads(WIDTH, WIDTH),
            ],
        ),
        out_shape=[
            arr(BF16, 2, WIDTH, PAIRS),
            stored(PAIRS),
            stored(PAIRS),
            stored(WIDTH),
            stored(WIDTH),
        ],
        input_output_aliases={5 + i: 1 + i for i in range(len(filled))},
        compiler_params=pltpu.CompilerParams(vmem_limit_bytes=VMEM),
        cost_estimate=pl.CostEstimate(
            flops=(1 if mine else 100) << 20, bytes_accessed=1 << (16 if mine else 24), transcendentals=0
        ),
    )(place, queries, keys, values, logits, *filled)


STEPS = 4
BLOCKS = [(z, row) for z in range(2) for row in range(2)]


def grad_rows(place, step, own_ref, other_ref):
    def block(ref, z, row):
        column = pl.multiple_of(z * 256 + place[0] * 128, 128)
        return ref[(row ^ place[1]) * 4 + step, :, pl.ds(column, 128)]

    rows = [
        jnp.concatenate([block(ref, *place_of) for place_of in BLOCKS], axis=1)
        for ref in (own_ref, other_ref)
    ]
    return jnp.concatenate(rows, axis=0)


def weight_rows(ref):
    return jnp.concatenate([ref[z, row] for z, row in BLOCKS], axis=0)


def weight_tile():
    return pl.BlockSpec((2, 2, WIDTH, 512), lambda step, place: (step, 0, 0, 0))


def heads_kernel(place, qt_ref, local_ref, state_ref, heads_ref):
    for head in range(4):
        result = dot(qt_ref[head], state_ref[slot(head, place)]) + local_ref[head]
        heads_ref[:, head * WIDTH : (head + 1) * WIDTH] = result.astype(BF16)


def head_outputs(place, qt, local, state):
    square = whole(4, WIDTH, WIDTH)
    return call(
        heads_kernel,
        1,
        [square, square, square],
        whole(WIDTH, 512),
        arr(BF16, WIDTH, 512),
        2 * 4 * 128**3,
        1 << 20,
    )(place, qt, local, state)


def weight_terms_kernel(place, own_ref, other_ref, heads_ref, heads_other_ref, out_ref):
    product = lax.dot_general(
        grad_rows(place, pl.program_id(0), own_ref, other_ref),
        jnp.concatenate([heads_ref[...], heads_other_ref[...]], axis=0),
        (((0,), (0,)), ((), ())),
        preferred_element_type=F32,
    )
    product = (product * (1.0 / 64.0)).astype(BF16)
    for z in range(2):
        out_ref[z] = product[z * 256 : z * 256 + 256]


def weight_terms(place, grad_full, grad_other, heads, heads_other):
    return call(
        weight_terms_kernel,
        STEPS,
        [whole(8, WIDTH, 512), whole(8, WIDTH, 512), whole(WIDTH, 512), whole(WIDTH, 512)],
        pl.BlockSpec((2, 256, 512), lambda step, place: (step, 0, 0)),
        arr(BF16, 8, 256, 512),
        2 * 128 * 512 * 4096,
        5 << 20,
    )(place, grad_full, grad_other, heads, heads_other)


def mixed_kernel(place, heads_ref, heads_other_ref, weight_ref, out_ref):
    step = pl.program_id(0)
    product = lax.dot_general(
        jnp.concatenate([heads_ref[...], heads_other_ref[...]], axis=0),
        weight_rows(weight_ref),
        (((1,), (1,)), ((), ())),
        preferred_element_type=F32,
    ).astype(BF16)
    for i, (z, row) in enumerate(BLOCKS):
        owner = (row ^ place[1]) * 4 + step
        out_ref[owner, :, z * 128 : z * 128 + 128] = product[:, i * WIDTH : (i + 1) * WIDTH]


def mixed_parts(place, heads, heads_other, weight):
    return call(
        mixed_kernel,
        STEPS,
        [whole(WIDTH, 512), whole(WIDTH, 512), weight_tile()],
        whole(8, 256, 256),
        arr(BF16, 8, 256, 256),
        2 * 128 * 512 * 4096,
        3 << 20,
    )(place, heads, heads_other, weight)


def head_grad_kernel(place, own_ref, other_ref, weight_ref, kept_ref, given_ref):
    step = pl.program_id(0)
    total = jnp.dot(
        grad_rows(place, step, own_ref, other_ref),
        weight_rows(weight_ref),
        preferred_element_type=F32,
    )

    @pl.when(step == 0)
    def _():
        kept_ref[...] = total[:WIDTH]
        given_ref[...] = total[WIDTH:]

    @pl.when(step > 0)
    def _():
        kept_ref[...] += total[:WIDTH]
        given_ref[...] += total[WIDTH:]


def head_gradient(place, grad_full, grad_other, weight):
    part = arr(F32, WIDTH, 512)
    return call(
        head_grad_kernel,
        STEPS,
        [whole(8, WIDTH, 512), whole(8, WIDTH, 512), weight_tile()],
        [whole(WIDTH, 512), whole(WIDTH, 512)],
        [part, part],
        2 * 128 * 512 * 4096,
        5 << 20,
    )(place, grad_full, grad_other, weight)


def own_kernel(place, kept_ref, came_ref, qt_ref, grad_ref, mine_ref, theirs_ref):
    grad_ref[...] = kept_ref[...] + came_ref[...]
    for head in range(4):
        grad = grad_ref[:, head * WIDTH : (head + 1) * WIDTH]
        own = dot(qt_ref[head], grad, 0, 0, passes=1).astype(BF16)

        @pl.when(place[0] == head // 2)
        def _():
            mine_ref[head % 2] = own

        @pl.when(place[0] != head // 2)
        def _():
            theirs_ref[head % 2] = own


def own_cotangent(place, kept, came, qt):
    pair = arr(BF16, 2, WIDTH, WIDTH)
    return call(
        own_kernel,
        1,
        [whole(WIDTH, 512), whole(WIDTH, 512), whole(4, WIDTH, WIDTH)],
        [whole(WIDTH, 512), whole(2, WIDTH, WIDTH), whole(2, WIDTH, WIDTH)],
        [arr(F32, WIDTH, 512), pair, pair],
        2 * 4 * 128**3,
        1 << 20,
    )(place, kept, came, qt)


def pull_kernel(
    place, q_ref, k_ref, logit_ref, m_ref, wy_ref, state_ref, end_ref, grad_ref,
    dq_ref, dk_ref, dv_ref, dlogit_ref,
):
    two = range(2)
    shape = (PAIRS, PAIRS)
    before = order_of(shape, 1) < order_of(shape, 0)
    query = [q_ref[:, i * WIDTH : (i + 1) * WIDTH].astype(F32) for i in two]
    query_scale = [inverse_norm(x) for x in query]
    query = [query[i] * query_scale[i] for i in two]
    key = [stacked(k_ref, i) for i in two]
    key_scale = [inverse_norm(x) for x in key]
    key = [key[i] * key_scale[i] for i in two]
    first = 2 * pl.program_id(0)
    logit = [column_of(logit_ref[pl.ds(first + i, 1), :]) for i in two]
    state = [state_ref[i] for i in two]
    end = [end_ref[i] for i in two]
    grad = [grad_ref[:, i * WIDTH : (i + 1) * WIDTH] for i in two]
    updates = [wy_ref[i, :, WIDTH:] - dot(wy_ref[i, :, :WIDTH], state[i]) for i in two]
    pulled = [dot(m_ref[i], jnp.concatenate([grad[i], end[i].astype(F32)], axis=0), 0, 0) for i in two]
    value_grad = [2.0 / (1.0 + jnp.exp(-logit[i])) * pulled[i] for i in two]
    cross = [
        dot(jnp.concatenate([grad[i], value_grad[i]], axis=0), updates[i], 1, 1) for i in two
    ]
    pairs = [
        jnp.concatenate(
            [
                jnp.where(visible_mask(), cross[i][:WIDTH], 0.0),
                jnp.where(before, -cross[i][WIDTH:], 0.0),
            ],
            axis=0,
        )
        for i in two
    ]
    forward = [dot(pairs[i], key[i]) for i in two]
    backward = [dot(pairs[i], jnp.concatenate([query[i], key[i]], axis=0), 0, 0) for i in two]
    by_state = [
        dot(jnp.concatenate([grad[i], -value_grad[i]], axis=0), state[i], 1, 1, passes=1)
        for i in two
    ]
    by_end = [dot(updates[i], end[i], 1, 1, passes=1) for i in two]
    for i in two:
        start = i * PAIRS
        dv_ref[:, start : start + WIDTH] = value_grad[i][:WIDTH].astype(BF16)
        dv_ref[:, start + WIDTH : start + PAIRS] = value_grad[i][WIDTH:].astype(BF16)
        slope = jnp.sum(pulled[i] * updates[i], axis=1, keepdims=True) / (1.0 + jnp.exp(logit[i]))
        dlogit_ref[pl.ds(first + i, 1), :] = row_of(slope)
        query_grad = forward[i][:WIDTH] + by_state[i][:WIDTH]
        query_grad = query_scale[i] * (
            query_grad - query[i] * jnp.sum(query[i] * query_grad, axis=1, keepdims=True)
        )
        dq_ref[:, i * WIDTH : (i + 1) * WIDTH] = query_grad.astype(BF16)
        key_grad = forward[i][WIDTH:] + backward[i] + by_end[i] + by_state[i][WIDTH:]
        key_grad = key_scale[i] * (
            key_grad - key[i] * jnp.sum(key[i] * key_grad, axis=1, keepdims=True)
        )
        dk_ref[:, start : start + WIDTH] = key_grad[:WIDTH].astype(BF16)
        dk_ref[:, start + WIDTH : start + PAIRS] = key_grad[WIDTH:].astype(BF16)


def pull(place, queries, keys, logits, reads, wy, state, end, head_grad):
    return call(
        pull_kernel,
        2,
        [
            by_columns(WIDTH),
            by_columns(PAIRS),
            whole(4, PAIRS),
            by_pair(PAIRS, PAIRS),
            by_pair(PAIRS, PAIRS),
            by_slot(WIDTH, WIDTH),
            by_slot(WIDTH, WIDTH),
            by_columns(WIDTH),
        ],
        [by_columns(WIDTH), by_columns(PAIRS), by_columns(PAIRS), whole(4, PAIRS)],
        [
            arr(BF16, WIDTH, 512),
            arr(BF16, WIDTH, 1024),
            arr(BF16, WIDTH, 1024),
            arr(F32, 4, PAIRS),
        ],
        4 * 14 * 2 * PAIRS**3,
        5 << 20,
    )(place, queries, keys, logits, reads, wy, state, end, head_grad)


def mul(a, b):
    return jnp.einsum("hij,hjk->hik", a, b, preferred_element_type=F32)


def mul_t(a, b):
    return jnp.einsum("hji,hjk->hik", a, b, preferred_element_type=F32)


def halves(x):
    return x[:, :, :WIDTH], x[:, :, WIDTH:]


def forward_states(place, mine, theirs, core, grad_full, weight):
    theirs = exchange(theirs, 1)
    even = jnp.where(core == 0, mine, theirs)
    odd = jnp.where(core == 0, theirs, mine)
    even_a, even_b = halves(even)
    odd_a, odd_b = halves(odd)
    joined = mul(odd_a, even)
    chip = jnp.concatenate(
        [joined[:, :, :WIDTH], joined[:, :, WIDTH:] + odd_b.astype(F32)], axis=2
    ).astype(BF16)
    one, two = send(chip, 2), send(chip, 4)
    window1, state = halves(one)
    step = mul(window1, two)
    state = state.astype(F32) + step[:, :, WIDTH:]
    window2 = step[:, :, :WIDTH].astype(BF16)
    step = mul(window2, send(jnp.concatenate([window2, state.astype(BF16)], axis=2), 4))
    state = state + step[:, :, WIDTH:]
    window4 = step[:, :, :WIDTH].astype(BF16)
    rounded = state.astype(BF16)
    both = jnp.concatenate([window4, rounded], axis=2)
    grad_full, both = lax.optimization_barrier((grad_full, both))
    near, mid, far_b = send(both, 8), send(both, 16), send(rounded, 24)
    grad_other = exchange(grad_full, 1)
    kept_grad, given_grad = head_gradient(place, grad_full, grad_other, weight)
    kept_grad, given_grad, near, mid, far_b = lax.optimization_barrier(
        (kept_grad, given_grad, near, mid, far_b)
    )
    near_a, near_b = halves(near)
    mid_a, mid_b = halves(mid)
    head_grad = (kept_grad, exchange(given_grad, 1))
    inner = (mid_b.astype(F32) + mul(mid_a, far_b)).astype(BF16)
    inner = (near_b.astype(F32) + mul(near_a, inner)).astype(BF16)
    first = (state + mul(window4, inner)).astype(BF16)
    window8 = mul(window4, near_a).astype(BF16)
    window12 = mul(window8, mid_a).astype(BF16)
    second = (mul(even_a, first) + even_b.astype(F32)).astype(BF16)
    kept = jnp.where(core == 0, first, second)
    given = jnp.where(core == 0, second, first)
    state_in = jnp.concatenate([kept, exchange(given, 1)], axis=0)
    return grad_full, grad_other, head_grad, state_in, (even_a, odd_a, window1, window2, window4, window8, window12)


def backward_states(mine, theirs, core, saved, gate):
    even_a, odd_a, window1, window2, window4, window8, window12 = saved
    theirs = exchange(theirs, 1)
    even = jnp.where(core == 0, mine, theirs)
    odd = jnp.where(core == 0, theirs, mine)
    total = even.astype(F32) + mul_t(even_a, odd)
    for window, distance in ((window1, 2), (window2, 4)):
        passed = mul_t(window, total.astype(BF16)).astype(BF16)
        if distance == 4:
            gate, passed = lax.optimization_barrier((gate, passed))
        total = total + send(passed, -distance).astype(F32)
    rounded = total.astype(BF16)
    second = send(rounded, -2).astype(F32)
    for window, distance in ((window4, 10), (window8, 18), (window12, 26)):
        second += send(mul_t(window, rounded).astype(BF16), -distance).astype(F32)
    second = second.astype(BF16)
    first = (odd.astype(F32) + mul_t(odd_a, second)).astype(BF16)
    kept = jnp.where(core == 0, first, second)
    given = jnp.where(core == 0, second, first)
    return gate, jnp.concatenate([kept, exchange(given, 1)], axis=0)


def local(queries, keys, values, beta_logit, out_weight, out_grad):
    index = lax.axis_index("ctx")
    core = index & 1
    place = jnp.stack([core, index >> 4]).astype(jnp.int32)
    rings = [[(half * 8 + z) * 2 + c for z in range(8)] for half in range(2) for c in range(2)]
    operands = (queries, keys, values, beta_logit)
    across = exchange(out_weight, 16)
    theirs, *filled = prepare(place, *operands, False)
    across, theirs = lax.optimization_barrier((across, theirs))
    weight_pair = jnp.stack([out_weight, across])
    weight_pair, *operands = lax.optimization_barrier((weight_pair, *operands))
    mine, reads, wy, qt, local_out = prepare(place, *operands, True, filled)
    weight_mine = lax.all_gather(weight_pair, "ctx", axis=0, axis_index_groups=rings)
    grad_full = lax.all_to_all(
        jnp.broadcast_to(out_grad[None], (8, WIDTH, 512)), "tp", 0, 0, tiled=True
    )
    grad_full, grad_other, head_grad, state, saved = forward_states(
        place, mine, theirs, core, grad_full, weight_mine
    )
    heads = head_outputs(place, qt, local_out, state)
    heads_other = exchange(heads, 1)
    terms = weight_terms(place, grad_full, grad_other, heads, heads_other)
    ring_sum = lax.psum_scatter(
        terms, "ctx", scatter_dimension=0, axis_index_groups=rings
    ).reshape(2, WIDTH, 512)
    head_grad, own, own_theirs = own_cotangent(place, *head_grad, qt)
    parts = mixed_parts(place, heads, heads_other, weight_mine)
    parts, end = backward_states(own, own_theirs, core, saved, parts)
    end, ring_sum = lax.optimization_barrier((end, ring_sum))
    weight_grad = ring_sum[0].astype(F32) + exchange(ring_sum[1], 16).astype(F32)
    parts = lax.all_to_all(parts, "tp", 0, 0, tiled=True)
    sums = jnp.sum(parts.astype(F32), axis=0).astype(BF16)
    kept, came = sums[:WIDTH], exchange(sums[WIDTH:], 1)
    first, second = jnp.where(core == 0, kept, came), jnp.where(core == 0, came, kept)
    mixed = jnp.concatenate(
        [first[:, :WIDTH], second[:, :WIDTH], first[:, WIDTH:], second[:, WIDTH:]], axis=1
    )
    query_grad, key_grad, value_grad, logit_grad = pull(
        place, queries, keys, beta_logit, reads, wy, state, end, head_grad
    )
    return mixed, query_grad, key_grad, value_grad, logit_grad, weight_grad


def solution(mesh):
    placed = P("ctx", "tp")
    return jax.shard_map(
        local,
        mesh=mesh,
        in_specs=(placed, placed, placed, P("tp", "ctx"), placed, placed),
        out_specs=(placed, placed, placed, placed, P("tp", "ctx"), placed),
        check_vma=False,
    )
```

```python
import functools
import math

import jax
import jax.numpy as jnp
from jax import lax
from jax.experimental import pallas as pl
from jax.experimental.pallas import tpu as pltpu
from jax.sharding import PartitionSpec as P

F32 = jnp.float32
BF16 = jnp.bfloat16
WIDTH = 128
VMEM = 62 << 20
PAIRS = 2 * WIDTH


def send(block, distance):
    devices = range(lax.axis_size("ctx"))
    route = [(i - distance, i) for i in devices if i - distance in devices]
    return lax.ppermute(block, "ctx", route)


def exchange(block, bit):
    route = [(i, i ^ bit) for i in range(lax.axis_size("ctx"))]
    return lax.ppermute(block, "ctx", route)


def split(x):
    high = x.astype(BF16)
    return high, (x - high.astype(F32)).astype(BF16)


def dot(a, b, ca=1, cb=0, passes=3):
    dims = (((ca,), (cb,)), ((), ()))
    mul = functools.partial(lax.dot_general, dimension_numbers=dims, preferred_element_type=F32)
    if passes == 1:
        return mul(a.astype(BF16), b.astype(BF16))
    if b.dtype == BF16:
        a_high, a_low = split(a)
        return mul(a_high, b) + mul(a_low, b)
    a_high, a_low = split(a)
    b_high, b_low = split(b)
    return mul(a_high, b_high) + (mul(a_low, b_high) + mul(a_high, b_low))


def inverse_norm(x):
    return lax.rsqrt(jnp.sum(x * x, axis=-1, keepdims=True) + 1e-06)


def order_of(shape, dim):
    p = lax.broadcasted_iota(jnp.int32, shape, dim)
    return 2 * (p & (WIDTH - 1)) + (p >> 7)


def column_of(row):
    shape = (PAIRS, PAIRS)
    time = lax.broadcasted_iota(jnp.int32, shape, 1)
    return jnp.sum(jnp.where(time == order_of(shape, 0), row, 0.0), axis=1, keepdims=True)


def row_of(column):
    shape = (PAIRS, PAIRS)
    time = lax.broadcasted_iota(jnp.int32, shape, 1)
    return jnp.sum(jnp.where(time == order_of(shape, 0), column, 0.0), axis=0, keepdims=True)


def visible_mask():
    shape = (WIDTH, PAIRS)
    token = lax.broadcasted_iota(jnp.int32, shape, 0)
    return (lax.broadcasted_iota(jnp.int32, shape, 1) & (WIDTH - 1)) <= token


def stacked(ref, i):
    start = i * PAIRS
    parts = [ref[:, start : start + WIDTH], ref[:, start + WIDTH : start + PAIRS]]
    return jnp.concatenate(parts, axis=0).astype(F32)


def prepare_kernel(mine, *refs):
    place, q_ref, k_ref, v_ref, logit_ref = refs[:5]
    first = 2 * (place[0] if mine else 1 - place[0])
    ab_ref, m_ref, wy_ref, qt_ref, local_ref = refs[-5:]
    two = range(2)
    shape = (PAIRS, PAIRS)
    row, col = order_of(shape, 0), order_of(shape, 1)
    identity = jnp.where(row == col, 1.0, 0.0).astype(F32)
    query = [q_ref[:, i * WIDTH : (i + 1) * WIDTH].astype(F32) for i in two]
    query = [x * inverse_norm(x) for x in query]
    key = [stacked(k_ref, i) for i in two]
    key = [x * inverse_norm(x) for x in key]
    strength = [2.0 / (1.0 + jnp.exp(-column_of(logit_ref[pl.ds(first + i, 1), :]))) for i in two]
    coupling = [jnp.where(col < row, strength[i] * dot(key[i], key[i], 1, 1), 0.0) for i in two]
    inverse = [identity - jnp.where((row >> 1) == (col >> 1), coupling[i], 0.0) for i in two]
    for level in range(1, 8):
        join = ((row >> (level + 1)) == (col >> (level + 1))) & ((row >> level) != (col >> level))
        edge = [jnp.where(join, coupling[i], 0.0) for i in two]
        step = [dot(inverse[i], edge[i], passes=1) for i in two]
        inverse = [inverse[i] - dot(step[i], inverse[i], passes=1) for i in two]
    rest = [identity - inverse[i] - dot(coupling[i], inverse[i]) for i in two]
    inverse = [inverse[i] + dot(inverse[i], rest[i], passes=1) for i in two]
    scores = [jnp.where(visible_mask(), dot(query[i], key[i], 1, 1), 0.0) for i in two]
    scaled = [strength[i] * jnp.concatenate([key[i], stacked(v_ref, i)], axis=1) for i in two]
    reads = [
        jnp.concatenate([dot(scores[i], inverse[i]), dot(key[i], inverse[i], 0, 0)], axis=0)
        for i in two
    ]
    product = [dot(reads[i], scaled[i]) for i in two]
    eye = identity[:WIDTH, :WIDTH]
    for i in two:
        ab_ref[i, :, :WIDTH] = (eye - product[i][WIDTH:, :WIDTH]).astype(BF16)
        ab_ref[i, :, WIDTH:] = product[i][WIDTH:, WIDTH:].astype(BF16)
        qt_ref[i] = query[i] - product[i][:WIDTH, :WIDTH]
        local_ref[i] = product[i][:WIDTH, WIDTH:]
        m_ref[i] = reads[i]
        wy_ref[i] = dot(inverse[i], scaled[i])


def slot(head, place):
    return (head + 2 * place[0]) % 4


def by_pair(*block):
    return pl.BlockSpec((2,) + block, lambda i, place: (i,) + (0,) * len(block))


def by_slot(*block):
    return pl.BlockSpec((2,) + block, lambda i, place: (i ^ place[0],) + (0,) * len(block))


def by_columns(width):
    return pl.BlockSpec((WIDTH, 2 * width), lambda i, place: (0, i))


def whole(*shape):
    return pl.BlockSpec(shape, lambda i, place: (0,) * len(shape))


def call(kernel, steps, in_specs, out_specs, out_shape, flops, moved, scratch=()):
    return pl.pallas_call(
        kernel,
        grid_spec=pltpu.PrefetchScalarGridSpec(
            num_scalar_prefetch=1,
            grid=(steps,),
            in_specs=in_specs,
            out_specs=out_specs,
            scratch_shapes=list(scratch),
        ),
        out_shape=out_shape,
        compiler_params=pltpu.CompilerParams(vmem_limit_bytes=VMEM),
        cost_estimate=pl.CostEstimate(flops=flops, bytes_accessed=moved, transcendentals=0),
    )


def arr(dtype, *shape):
    return jax.ShapeDtypeStruct(shape, dtype)


def prepare(place, queries, keys, values, logits, mine, filled=()):
    def pair(place):
        return place[0] if mine else 1 - place[0]

    def columns(width):
        return pl.BlockSpec((WIDTH, 2 * width), lambda i, place: (0, pair(place)))

    def heads(*block):
        return pl.BlockSpec((2,) + block, lambda i, place: (pair(place),) + (0,) * len(block))

    def stored(n):
        return arr(F32, 4, n, n)

    return pl.pallas_call(
        functools.partial(prepare_kernel, mine),
        grid_spec=pltpu.PrefetchScalarGridSpec(
            num_scalar_prefetch=1,
            grid=(1,),
            in_specs=[
                columns(WIDTH),
                columns(PAIRS),
                columns(PAIRS),
                whole(4, PAIRS),
            ]
            + [pl.BlockSpec(memory_space=pl.ANY)] * len(filled),
            out_specs=[
                pl.BlockSpec((2, WIDTH, PAIRS), lambda i, place: (0, 0, 0)),
                heads(PAIRS, PAIRS),
                heads(PAIRS, PAIRS),
                heads(WIDTH, WIDTH),
                heads(WIDTH, WIDTH),
            ],
        ),
        out_shape=[
            arr(BF16, 2, WIDTH, PAIRS),
            stored(PAIRS),
            stored(PAIRS),
            stored(WIDTH),
            stored(WIDTH),
        ],
        input_output_aliases={5 + i: 1 + i for i in range(len(filled))},
        compiler_params=pltpu.CompilerParams(vmem_limit_bytes=VMEM),
        cost_estimate=pl.CostEstimate(
            flops=1 << 20, bytes_accessed=1 << 16, transcendentals=0
        ),
    )(place, queries, keys, values, logits, *filled)


STEPS = 4


def feature_columns(ref, place, owner):
    blocks = [ref[owner, :, pl.ds(pl.multiple_of(z * 256 + place[0] * 128, 128), 128)] for z in range(2)]
    return jnp.concatenate(blocks, axis=1)


def pack_kernel(place, own_ref, other_ref, out_ref):
    owner = (1 - place[1]) * 4 + pl.program_id(0)
    out_ref[0, 0] = feature_columns(own_ref, place, owner)
    out_ref[0, 1] = feature_columns(other_ref, place, owner)


def pack(place, grad_full, grad_other):
    return call(
        pack_kernel,
        STEPS,
        [whole(8, WIDTH, 512), whole(8, WIDTH, 512)],
        pl.BlockSpec((1, 2, WIDTH, 256), lambda step, place: (step, 0, 0, 0)),
        arr(BF16, 4, 2, WIDTH, 256),
        1 << 20,
        3 << 20,
    )(place, grad_full, grad_other)


def grad_rows(place, own_ref, other_ref, across_ref):
    owner = place[1] * 4 + pl.program_id(0)
    rows = [feature_columns(ref, place, owner) for ref in (own_ref, other_ref)]
    return jnp.concatenate(rows + [across_ref[0, 0], across_ref[0, 1]], axis=0)


def grad_specs():
    return [
        whole(8, WIDTH, 512),
        whole(8, WIDTH, 512),
        pl.BlockSpec((1, 2, WIDTH, 256), lambda step, place: (step, 0, 0, 0)),
    ]


def weight_tile():
    return pl.BlockSpec((2, WIDTH, 512), lambda step, place: (step, 0, 0))


def heads_kernel(place, qt_ref, local_ref, state_ref, heads_ref):
    for head in range(4):
        result = dot(qt_ref[head], state_ref[slot(head, place)]) + local_ref[head]
        heads_ref[:, head * WIDTH : (head + 1) * WIDTH] = result.astype(BF16)


def head_outputs(place, qt, local, state):
    square = whole(4, WIDTH, WIDTH)
    return call(
        heads_kernel,
        1,
        [square, square, square],
        whole(WIDTH, 512),
        arr(BF16, WIDTH, 512),
        2 * 4 * 128**3,
        1 << 20,
    )(place, qt, local, state)


def weight_terms_kernel(place, own_ref, other_ref, across_ref, heads_ref, heads_across_ref, out_ref):
    product = lax.dot_general(
        grad_rows(place, own_ref, other_ref, across_ref),
        jnp.concatenate([heads_ref[0], heads_ref[1], heads_across_ref[0], heads_across_ref[1]], axis=0),
        (((0,), (0,)), ((), ())),
        preferred_element_type=F32,
    )
    product = (product * (1.0 / 64.0)).astype(BF16)
    out_ref[0] = product[:WIDTH]
    out_ref[1] = product[WIDTH:]


def weight_terms(place, grads, heads, heads_across):
    return call(
        weight_terms_kernel,
        STEPS,
        grad_specs() + [whole(2, WIDTH, 512), whole(2, WIDTH, 512)],
        weight_tile(),
        arr(BF16, 8, WIDTH, 512),
        2 * 128 * 512 * 4096,
        4 << 20,
    )(place, *grads, heads, heads_across)


def mixed_kernel(place, heads_ref, weight_ref, across_ref, out_ref):
    step = pl.program_id(0)
    rows = [ref[z] for ref in (weight_ref, across_ref) for z in range(2)]
    product = lax.dot_general(
        jnp.concatenate([heads_ref[0], heads_ref[1]], axis=0),
        jnp.concatenate(rows, axis=0),
        (((1,), (1,)), ((), ())),
        preferred_element_type=F32,
    ).astype(BF16)
    out_ref[place[1] * 4 + step] = product[:, :256]
    out_ref[(1 - place[1]) * 4 + step] = product[:, 256:]


def mixed_parts(place, heads, weight, weight_across):
    return call(
        mixed_kernel,
        STEPS,
        [whole(2, WIDTH, 512), weight_tile(), weight_tile()],
        whole(8, 256, 256),
        arr(BF16, 8, 256, 256),
        2 * 128 * 512 * 4096,
        3 << 20,
    )(place, heads, weight, weight_across)


def head_grad_kernel(place, own_ref, other_ref, across_ref, weight_ref, kept_ref, given_ref):
    step = pl.program_id(0)
    total = jnp.dot(
        grad_rows(place, own_ref, other_ref, across_ref),
        jnp.concatenate([weight_ref[0], weight_ref[1]], axis=0),
        preferred_element_type=F32,
    )
    parts = [total[i * WIDTH : (i + 1) * WIDTH] for i in range(4)]

    @pl.when(step == 0)
    def _():
        kept_ref[0] = parts[0]
        kept_ref[1] = parts[2]
        given_ref[0] = parts[1]
        given_ref[1] = parts[3]

    @pl.when(step > 0)
    def _():
        kept_ref[0] += parts[0]
        kept_ref[1] += parts[2]
        given_ref[0] += parts[1]
        given_ref[1] += parts[3]


def head_gradient(place, grads, weight):
    part = arr(F32, 2, WIDTH, 512)
    return call(
        head_grad_kernel,
        STEPS,
        grad_specs() + [weight_tile()],
        [whole(2, WIDTH, 512), whole(2, WIDTH, 512)],
        [part, part],
        2 * 128 * 512 * 4096,
        4 << 20,
    )(place, *grads, weight)


def own_kernel(place, kept_ref, came_ref, qt_ref, grad_ref, mine_ref, theirs_ref):
    grad_ref[...] = kept_ref[...] + came_ref[...].astype(F32)
    for head in range(4):
        grad = grad_ref[:, head * WIDTH : (head + 1) * WIDTH]
        own = dot(qt_ref[head], grad, 0, 0, passes=1).astype(BF16)

        @pl.when(place[0] == head // 2)
        def _():
            mine_ref[head % 2] = own

        @pl.when(place[0] != head // 2)
        def _():
            theirs_ref[head % 2] = own


def own_cotangent(place, kept, came, qt):
    pair = arr(BF16, 2, WIDTH, WIDTH)
    return call(
        own_kernel,
        1,
        [whole(WIDTH, 512), whole(WIDTH, 512), whole(4, WIDTH, WIDTH)],
        [whole(WIDTH, 512), whole(2, WIDTH, WIDTH), whole(2, WIDTH, WIDTH)],
        [arr(F32, WIDTH, 512), pair, pair],
        2 * 4 * 128**3,
        1 << 20,
    )(place, kept, came, qt)


def pull_kernel(
    place, q_ref, k_ref, logit_ref, m_ref, wy_ref, state_ref, end_ref, grad_ref,
    dq_ref, dk_ref, dv_ref, dlogit_ref,
):
    two = range(2)
    shape = (PAIRS, PAIRS)
    before = order_of(shape, 1) < order_of(shape, 0)
    query = [q_ref[:, i * WIDTH : (i + 1) * WIDTH].astype(F32) for i in two]
    query_scale = [inverse_norm(x) for x in query]
    query = [query[i] * query_scale[i] for i in two]
    key = [stacked(k_ref, i) for i in two]
    key_scale = [inverse_norm(x) for x in key]
    key = [key[i] * key_scale[i] for i in two]
    first = 2 * pl.program_id(0)
    logit = [column_of(logit_ref[pl.ds(first + i, 1), :]) for i in two]
    state = [state_ref[i] for i in two]
    end = [end_ref[i] for i in two]
    grad = [grad_ref[:, i * WIDTH : (i + 1) * WIDTH] for i in two]
    updates = [wy_ref[i, :, WIDTH:] - dot(wy_ref[i, :, :WIDTH], state[i]) for i in two]
    pulled = [dot(m_ref[i], jnp.concatenate([grad[i], end[i].astype(F32)], axis=0), 0, 0) for i in two]
    value_grad = [2.0 / (1.0 + jnp.exp(-logit[i])) * pulled[i] for i in two]
    cross = [
        dot(jnp.concatenate([grad[i], value_grad[i]], axis=0), updates[i], 1, 1) for i in two
    ]
    pairs = [
        jnp.concatenate(
            [
                jnp.where(visible_mask(), cross[i][:WIDTH], 0.0),
                jnp.where(before, -cross[i][WIDTH:], 0.0),
            ],
            axis=0,
        )
        for i in two
    ]
    forward = [dot(pairs[i], key[i]) for i in two]
    backward = [dot(pairs[i], jnp.concatenate([query[i], key[i]], axis=0), 0, 0) for i in two]
    by_state = [
        dot(jnp.concatenate([grad[i], -value_grad[i]], axis=0), state[i], 1, 1, passes=1)
        for i in two
    ]
    by_end = [dot(updates[i], end[i], 1, 1, passes=1) for i in two]
    for i in two:
        start = i * PAIRS
        dv_ref[:, start : start + WIDTH] = value_grad[i][:WIDTH].astype(BF16)
        dv_ref[:, start + WIDTH : start + PAIRS] = value_grad[i][WIDTH:].astype(BF16)
        slope = jnp.sum(pulled[i] * updates[i], axis=1, keepdims=True) / (1.0 + jnp.exp(logit[i]))
        dlogit_ref[pl.ds(first + i, 1), :] = row_of(slope)
        query_grad = forward[i][:WIDTH] + by_state[i][:WIDTH]
        query_grad = query_scale[i] * (
            query_grad - query[i] * jnp.sum(query[i] * query_grad, axis=1, keepdims=True)
        )
        dq_ref[:, i * WIDTH : (i + 1) * WIDTH] = query_grad.astype(BF16)
        key_grad = forward[i][WIDTH:] + backward[i] + by_end[i] + by_state[i][WIDTH:]
        key_grad = key_scale[i] * (
            key_grad - key[i] * jnp.sum(key[i] * key_grad, axis=1, keepdims=True)
        )
        dk_ref[:, start : start + WIDTH] = key_grad[:WIDTH].astype(BF16)
        dk_ref[:, start + WIDTH : start + PAIRS] = key_grad[WIDTH:].astype(BF16)


def pull(place, queries, keys, logits, reads, wy, state, end, head_grad):
    return call(
        pull_kernel,
        2,
        [
            by_columns(WIDTH),
            by_columns(PAIRS),
            whole(4, PAIRS),
            by_pair(PAIRS, PAIRS),
            by_pair(PAIRS, PAIRS),
            by_slot(WIDTH, WIDTH),
            by_slot(WIDTH, WIDTH),
            by_columns(WIDTH),
        ],
        [by_columns(WIDTH), by_columns(PAIRS), by_columns(PAIRS), whole(4, PAIRS)],
        [
            arr(BF16, WIDTH, 512),
            arr(BF16, WIDTH, 1024),
            arr(BF16, WIDTH, 1024),
            arr(F32, 4, PAIRS),
        ],
        4 * 14 * 2 * PAIRS**3,
        5 << 20,
    )(place, queries, keys, logits, reads, wy, state, end, head_grad)


def mul(a, b):
    return jnp.einsum("hij,hjk->hik", a, b, preferred_element_type=F32)


def mul_t(a, b):
    return jnp.einsum("hji,hjk->hik", a, b, preferred_element_type=F32)


def halves(x):
    return x[:, :, :WIDTH], x[:, :, WIDTH:]


def forward_states(place, mine, theirs, core, grad_full, weight):
    theirs = exchange(theirs, 1)
    even = jnp.where(core == 0, mine, theirs)
    odd = jnp.where(core == 0, theirs, mine)
    even_a, even_b = halves(even)
    odd_a, odd_b = halves(odd)
    joined = mul(odd_a, even)
    chip = jnp.concatenate(
        [joined[:, :, :WIDTH], joined[:, :, WIDTH:] + odd_b.astype(F32)], axis=2
    ).astype(BF16)
    grad_full, chip = lax.optimization_barrier((grad_full, chip))
    one, two = send(chip, 2), send(chip, 4)
    grad_other = exchange(grad_full, 1)
    grads = (grad_full, grad_other, exchange(pack(place, grad_full, grad_other), 16))
    window1, state = halves(one)
    step = mul(window1, two)
    state = state.astype(F32) + step[:, :, WIDTH:]
    window2 = step[:, :, :WIDTH].astype(BF16)
    step = mul(window2, send(jnp.concatenate([window2, state.astype(BF16)], axis=2), 4))
    state = state + step[:, :, WIDTH:]
    window4 = step[:, :, :WIDTH].astype(BF16)
    rounded = state.astype(BF16)
    both = jnp.concatenate([window4, rounded], axis=2)
    near, mid, far_b = send(both, 8), send(both, 16), send(rounded, 24)
    kept_grad, given_grad = head_gradient(place, grads, weight)
    kept_grad, given_grad, near, mid, far_b = lax.optimization_barrier(
        (kept_grad, given_grad, near, mid, far_b)
    )
    near_a, near_b = halves(near)
    mid_a, mid_b = halves(mid)
    given_grad = exchange(given_grad, 1)
    across_grad = exchange((kept_grad[1] + given_grad[1]).astype(BF16), 16)
    head_grad = (kept_grad[0] + given_grad[0], across_grad)
    inner = (mid_b.astype(F32) + mul(mid_a, far_b)).astype(BF16)
    inner = (near_b.astype(F32) + mul(near_a, inner)).astype(BF16)
    first = (state + mul(window4, inner)).astype(BF16)
    window8 = mul(window4, near_a).astype(BF16)
    window12 = mul(window8, mid_a).astype(BF16)
    second = (mul(even_a, first) + even_b.astype(F32)).astype(BF16)
    kept = jnp.where(core == 0, first, second)
    given = jnp.where(core == 0, second, first)
    state_in = jnp.concatenate([kept, exchange(given, 1)], axis=0)
    return grads, head_grad, state_in, (even_a, odd_a, window1, window2, window4, window8, window12)


def backward_states(mine, theirs, core, saved, gate):
    even_a, odd_a, window1, window2, window4, window8, window12 = saved
    theirs = exchange(theirs, 1)
    even = jnp.where(core == 0, mine, theirs)
    odd = jnp.where(core == 0, theirs, mine)
    total = even.astype(F32) + mul_t(even_a, odd)
    for window, distance in ((window1, 2), (window2, 4)):
        passed = mul_t(window, total.astype(BF16)).astype(BF16)
        if distance == 4:
            gate, passed = lax.optimization_barrier((gate, passed))
        total = total + send(passed, -distance).astype(F32)
    rounded = total.astype(BF16)
    second = send(rounded, -2).astype(F32)
    for window, distance in ((window4, 10), (window8, 18), (window12, 26)):
        second += send(mul_t(window, rounded).astype(BF16), -distance).astype(F32)
    second = second.astype(BF16)
    first = (odd.astype(F32) + mul_t(odd_a, second)).astype(BF16)
    kept = jnp.where(core == 0, first, second)
    given = jnp.where(core == 0, second, first)
    return gate, jnp.concatenate([kept, exchange(given, 1)], axis=0)


def local(queries, keys, values, beta_logit, out_weight, out_grad):
    index = lax.axis_index("ctx")
    core = index & 1
    place = jnp.stack([core, index >> 4]).astype(jnp.int32)
    rings = [[(half * 8 + z) * 2 + c for z in range(8)] for half in range(2) for c in range(2)]
    operands = (queries, keys, values, beta_logit)
    grad_full = lax.all_to_all(
        jnp.broadcast_to(out_grad[None], (8, WIDTH, 512)), "tp", 0, 0, tiled=True
    )
    weight = lax.all_gather(out_weight, "ctx", axis=0, axis_index_groups=rings)
    theirs, *filled = prepare(place, *operands, False)
    mine, reads, wy, qt, local_out = prepare(place, *operands, True, filled)
    grads, head_grad, state, saved = forward_states(place, mine, theirs, core, grad_full, weight)
    head_grad, own, own_theirs = own_cotangent(place, *head_grad, qt)
    heads = head_outputs(place, qt, local_out, state)
    heads = jnp.stack([heads, exchange(heads, 1)])
    terms = weight_terms(place, grads, heads, exchange(heads, 16))
    weight_grad = lax.psum_scatter(
        terms, "ctx", scatter_dimension=0, axis_index_groups=rings
    ).astype(F32)
    parts = mixed_parts(place, heads, weight, exchange(weight, 16))
    parts, end = backward_states(own, own_theirs, core, saved, parts)
    parts = lax.all_to_all(parts, "tp", 0, 0, tiled=True)
    sums = jnp.sum(parts.astype(F32), axis=0).astype(BF16)
    kept, came = sums[:WIDTH], exchange(sums[WIDTH:], 1)
    first, second = jnp.where(core == 0, kept, came), jnp.where(core == 0, came, kept)
    mixed = jnp.concatenate(
        [first[:, :WIDTH], second[:, :WIDTH], first[:, WIDTH:], second[:, WIDTH:]], axis=1
    )
    query_grad, key_grad, value_grad, logit_grad = pull(
        place, queries, keys, beta_logit, reads, wy, state, end, head_grad
    )
    return mixed, query_grad, key_grad, value_grad, logit_grad, weight_grad


def solution(mesh):
    placed = P("ctx", "tp")
    return jax.shard_map(
        local,
        mesh=mesh,
        in_specs=(placed, placed, placed, P("tp", "ctx"), placed, placed),
        out_specs=(placed, placed, placed, placed, P("tp", "ctx"), placed),
        check_vma=False,
    )
```

```python
import functools
import math

import jax
import jax.numpy as jnp
from jax import lax
from jax.experimental import pallas as pl
from jax.experimental.pallas import tpu as pltpu
from jax.sharding import PartitionSpec as P

F32 = jnp.float32
BF16 = jnp.bfloat16
WIDTH = 128
VMEM = 62 << 20
PAIRS = 2 * WIDTH


def send(block, distance):
    devices = range(lax.axis_size("ctx"))
    route = [(i - distance, i) for i in devices if i - distance in devices]
    return lax.ppermute(block, "ctx", route)


def exchange(block, bit):
    route = [(i, i ^ bit) for i in range(lax.axis_size("ctx"))]
    return lax.ppermute(block, "ctx", route)


def split(x):
    high = x.astype(BF16)
    return high, (x - high.astype(F32)).astype(BF16)


def dot(a, b, ca=1, cb=0, passes=3):
    dims = (((ca,), (cb,)), ((), ()))
    mul = functools.partial(lax.dot_general, dimension_numbers=dims, preferred_element_type=F32)
    if passes == 1:
        return mul(a.astype(BF16), b.astype(BF16))
    if b.dtype == BF16:
        a_high, a_low = split(a)
        return mul(a_high, b) + mul(a_low, b)
    a_high, a_low = split(a)
    b_high, b_low = split(b)
    return mul(a_high, b_high) + (mul(a_low, b_high) + mul(a_high, b_low))


def inverse_norm(x):
    return lax.rsqrt(jnp.sum(x * x, axis=-1, keepdims=True) + 1e-06)


def order_of(shape, dim):
    p = lax.broadcasted_iota(jnp.int32, shape, dim)
    return 2 * (p & (WIDTH - 1)) + (p >> 7)


def column_of(row):
    shape = (PAIRS, PAIRS)
    time = lax.broadcasted_iota(jnp.int32, shape, 1)
    return jnp.sum(jnp.where(time == order_of(shape, 0), row, 0.0), axis=1, keepdims=True)


def row_of(column):
    shape = (PAIRS, PAIRS)
    time = lax.broadcasted_iota(jnp.int32, shape, 1)
    return jnp.sum(jnp.where(time == order_of(shape, 0), column, 0.0), axis=0, keepdims=True)


def visible_mask():
    shape = (WIDTH, PAIRS)
    token = lax.broadcasted_iota(jnp.int32, shape, 0)
    return (lax.broadcasted_iota(jnp.int32, shape, 1) & (WIDTH - 1)) <= token


def stacked(ref, i):
    start = i * PAIRS
    parts = [ref[:, start : start + WIDTH], ref[:, start + WIDTH : start + PAIRS]]
    return jnp.concatenate(parts, axis=0).astype(F32)


def prepare_kernel(mine, *refs):
    place, q_ref, k_ref, v_ref, logit_ref = refs[:5]
    first = 2 * (place[0] if mine else 1 - place[0])
    ab_ref, m_ref, wy_ref, qt_ref, local_ref = refs[-5:]
    two = range(2)
    shape = (PAIRS, PAIRS)
    row, col = order_of(shape, 0), order_of(shape, 1)
    identity = jnp.where(row == col, 1.0, 0.0).astype(F32)
    query = [q_ref[:, i * WIDTH : (i + 1) * WIDTH].astype(F32) for i in two]
    query = [x * inverse_norm(x) for x in query]
    key = [stacked(k_ref, i) for i in two]
    key = [x * inverse_norm(x) for x in key]
    strength = [2.0 / (1.0 + jnp.exp(-column_of(logit_ref[pl.ds(first + i, 1), :]))) for i in two]
    coupling = [jnp.where(col < row, strength[i] * dot(key[i], key[i], 1, 1), 0.0) for i in two]
    inverse = [identity - jnp.where((row >> 1) == (col >> 1), coupling[i], 0.0) for i in two]
    for level in range(1, 8):
        join = ((row >> (level + 1)) == (col >> (level + 1))) & ((row >> level) != (col >> level))
        edge = [jnp.where(join, coupling[i], 0.0) for i in two]
        step = [dot(inverse[i], edge[i], passes=1) for i in two]
        inverse = [inverse[i] - dot(step[i], inverse[i], passes=1) for i in two]
    rest = [identity - inverse[i] - dot(coupling[i], inverse[i]) for i in two]
    inverse = [inverse[i] + dot(inverse[i], rest[i], passes=1) for i in two]
    scores = [jnp.where(visible_mask(), dot(query[i], key[i], 1, 1), 0.0) for i in two]
    scaled = [strength[i] * jnp.concatenate([key[i], stacked(v_ref, i)], axis=1) for i in two]
    reads = [
        jnp.concatenate([dot(scores[i], inverse[i]), dot(key[i], inverse[i], 0, 0)], axis=0)
        for i in two
    ]
    product = [dot(reads[i], scaled[i]) for i in two]
    eye = identity[:WIDTH, :WIDTH]
    for i in two:
        ab_ref[i, :, :WIDTH] = (eye - product[i][WIDTH:, :WIDTH]).astype(BF16)
        ab_ref[i, :, WIDTH:] = product[i][WIDTH:, WIDTH:].astype(BF16)
        qt_ref[i] = query[i] - product[i][:WIDTH, :WIDTH]
        local_ref[i] = product[i][:WIDTH, WIDTH:]
        m_ref[i] = reads[i]
        wy_ref[i] = dot(inverse[i], scaled[i])


def slot(head, place):
    return (head + 2 * place[0]) % 4


def by_pair(*block):
    return pl.BlockSpec((2,) + block, lambda i, place: (i,) + (0,) * len(block))


def by_slot(*block):
    return pl.BlockSpec((2,) + block, lambda i, place: (i ^ place[0],) + (0,) * len(block))


def by_columns(width):
    return pl.BlockSpec((WIDTH, 2 * width), lambda i, place: (0, i))


def whole(*shape):
    return pl.BlockSpec(shape, lambda i, place: (0,) * len(shape))


def call(kernel, steps, in_specs, out_specs, out_shape, flops, moved, scratch=()):
    return pl.pallas_call(
        kernel,
        grid_spec=pltpu.PrefetchScalarGridSpec(
            num_scalar_prefetch=1,
            grid=(steps,),
            in_specs=in_specs,
            out_specs=out_specs,
            scratch_shapes=list(scratch),
        ),
        out_shape=out_shape,
        compiler_params=pltpu.CompilerParams(vmem_limit_bytes=VMEM),
        cost_estimate=pl.CostEstimate(flops=flops, bytes_accessed=moved, transcendentals=0),
    )


def arr(dtype, *shape):
    return jax.ShapeDtypeStruct(shape, dtype)


def prepare(place, queries, keys, values, logits, mine, filled=()):
    def pair(place):
        return place[0] if mine else 1 - place[0]

    def columns(width):
        return pl.BlockSpec((WIDTH, 2 * width), lambda i, place: (0, pair(place)))

    def heads(*block):
        return pl.BlockSpec((2,) + block, lambda i, place: (pair(place),) + (0,) * len(block))

    def stored(n):
        return arr(F32, 4, n, n)

    return pl.pallas_call(
        functools.partial(prepare_kernel, mine),
        grid_spec=pltpu.PrefetchScalarGridSpec(
            num_scalar_prefetch=1,
            grid=(1,),
            in_specs=[
                columns(WIDTH),
                columns(PAIRS),
                columns(PAIRS),
                whole(4, PAIRS),
            ]
            + [pl.BlockSpec(memory_space=pl.ANY)] * len(filled),
            out_specs=[
                pl.BlockSpec((2, WIDTH, PAIRS), lambda i, place: (0, 0, 0)),
                heads(PAIRS, PAIRS),
                heads(PAIRS, PAIRS),
                heads(WIDTH, WIDTH),
                heads(WIDTH, WIDTH),
            ],
        ),
        out_shape=[
            arr(BF16, 2, WIDTH, PAIRS),
            stored(PAIRS),
            stored(PAIRS),
            stored(WIDTH),
            stored(WIDTH),
        ],
        input_output_aliases={5 + i: 1 + i for i in range(len(filled))},
        compiler_params=pltpu.CompilerParams(vmem_limit_bytes=VMEM),
        cost_estimate=pl.CostEstimate(
            flops=(1 if mine else 100) << 20, bytes_accessed=1 << (16 if mine else 24), transcendentals=0
        ),
    )(place, queries, keys, values, logits, *filled)


STEPS = 4
BLOCKS = [(z, row) for z in range(2) for row in range(2)]


def grad_rows(place, step, own_ref, other_ref):
    def block(ref, z, row):
        column = pl.multiple_of(z * 256 + place[0] * 128, 128)
        return ref[(row ^ place[1]) * 4 + step, :, pl.ds(column, 128)]

    rows = [
        jnp.concatenate([block(ref, *place_of) for place_of in BLOCKS], axis=1)
        for ref in (own_ref, other_ref)
    ]
    return jnp.concatenate(rows, axis=0)


def weight_rows(ref):
    return jnp.concatenate([ref[z, row] for z, row in BLOCKS], axis=0)


def weight_tile():
    return pl.BlockSpec((2, 2, WIDTH, 512), lambda step, place: (step, 0, 0, 0))


def heads_kernel(place, qt_ref, local_ref, state_ref, heads_ref):
    for head in range(4):
        result = dot(qt_ref[head], state_ref[slot(head, place)]) + local_ref[head]
        heads_ref[:, head * WIDTH : (head + 1) * WIDTH] = result.astype(BF16)


def head_outputs(place, qt, local, state):
    square = whole(4, WIDTH, WIDTH)
    return call(
        heads_kernel,
        1,
        [square, square, square],
        whole(WIDTH, 512),
        arr(BF16, WIDTH, 512),
        2 * 4 * 128**3,
        1 << 20,
    )(place, qt, local, state)


def weight_terms_kernel(place, own_ref, other_ref, heads_ref, heads_other_ref, out_ref):
    product = lax.dot_general(
        grad_rows(place, pl.program_id(0), own_ref, other_ref),
        jnp.concatenate([heads_ref[...], heads_other_ref[...]], axis=0),
        (((0,), (0,)), ((), ())),
        preferred_element_type=F32,
    )
    product = (product * (1.0 / 64.0)).astype(BF16)
    for z in range(2):
        out_ref[z] = product[z * 256 : z * 256 + 256]


def weight_terms(place, grad_full, grad_other, heads, heads_other):
    return call(
        weight_terms_kernel,
        STEPS,
        [whole(8, WIDTH, 512), whole(8, WIDTH, 512), whole(WIDTH, 512), whole(WIDTH, 512)],
        pl.BlockSpec((2, 256, 512), lambda step, place: (step, 0, 0)),
        arr(BF16, 8, 256, 512),
        2 * 128 * 512 * 4096,
        5 << 20,
    )(place, grad_full, grad_other, heads, heads_other)


def mixed_kernel(place, heads_ref, heads_other_ref, weight_ref, out_ref):
    step = pl.program_id(0)
    product = lax.dot_general(
        jnp.concatenate([heads_ref[...], heads_other_ref[...]], axis=0),
        weight_rows(weight_ref),
        (((1,), (1,)), ((), ())),
        preferred_element_type=F32,
    ).astype(BF16)
    for i, (z, row) in enumerate(BLOCKS):
        owner = (row ^ place[1]) * 4 + step
        out_ref[owner, :, z * 128 : z * 128 + 128] = product[:, i * WIDTH : (i + 1) * WIDTH]


def mixed_parts(place, heads, heads_other, weight):
    return call(
        mixed_kernel,
        STEPS,
        [whole(WIDTH, 512), whole(WIDTH, 512), weight_tile()],
        whole(8, 256, 256),
        arr(BF16, 8, 256, 256),
        2 * 128 * 512 * 4096,
        3 << 20,
    )(place, heads, heads_other, weight)


def head_grad_kernel(place, own_ref, other_ref, weight_ref, kept_ref, given_ref):
    step = pl.program_id(0)
    total = jnp.dot(
        grad_rows(place, step, own_ref, other_ref),
        weight_rows(weight_ref),
        preferred_element_type=F32,
    )

    @pl.when(step == 0)
    def _():
        kept_ref[...] = total[:WIDTH]
        given_ref[...] = total[WIDTH:]

    @pl.when(step > 0)
    def _():
        kept_ref[...] += total[:WIDTH]
        given_ref[...] += total[WIDTH:]


def head_gradient(place, grad_full, grad_other, weight):
    part = arr(F32, WIDTH, 512)
    return call(
        head_grad_kernel,
        STEPS,
        [whole(8, WIDTH, 512), whole(8, WIDTH, 512), weight_tile()],
        [whole(WIDTH, 512), whole(WIDTH, 512)],
        [part, part],
        2 * 128 * 512 * 4096,
        5 << 20,
    )(place, grad_full, grad_other, weight)


def own_kernel(place, kept_ref, came_ref, qt_ref, grad_ref, mine_ref, theirs_ref):
    grad_ref[...] = kept_ref[...] + came_ref[...]
    for head in range(4):
        grad = grad_ref[:, head * WIDTH : (head + 1) * WIDTH]
        own = dot(qt_ref[head], grad, 0, 0, passes=1).astype(BF16)

        @pl.when(place[0] == head // 2)
        def _():
            mine_ref[head % 2] = own

        @pl.when(place[0] != head // 2)
        def _():
            theirs_ref[head % 2] = own


def own_cotangent(place, kept, came, qt):
    pair = arr(BF16, 2, WIDTH, WIDTH)
    return call(
        own_kernel,
        1,
        [whole(WIDTH, 512), whole(WIDTH, 512), whole(4, WIDTH, WIDTH)],
        [whole(WIDTH, 512), whole(2, WIDTH, WIDTH), whole(2, WIDTH, WIDTH)],
        [arr(F32, WIDTH, 512), pair, pair],
        2 * 4 * 128**3,
        1 << 20,
    )(place, kept, came, qt)


def pull_kernel(
    place, q_ref, k_ref, logit_ref, m_ref, wy_ref, state_ref, end_ref, grad_ref,
    dq_ref, dk_ref, dv_ref, dlogit_ref,
):
    two = range(2)
    shape = (PAIRS, PAIRS)
    before = order_of(shape, 1) < order_of(shape, 0)
    query = [q_ref[:, i * WIDTH : (i + 1) * WIDTH].astype(F32) for i in two]
    query_scale = [inverse_norm(x) for x in query]
    query = [query[i] * query_scale[i] for i in two]
    key = [stacked(k_ref, i) for i in two]
    key_scale = [inverse_norm(x) for x in key]
    key = [key[i] * key_scale[i] for i in two]
    first = 2 * pl.program_id(0)
    logit = [column_of(logit_ref[pl.ds(first + i, 1), :]) for i in two]
    state = [state_ref[i] for i in two]
    end = [end_ref[i] for i in two]
    grad = [grad_ref[:, i * WIDTH : (i + 1) * WIDTH] for i in two]
    updates = [wy_ref[i, :, WIDTH:] - dot(wy_ref[i, :, :WIDTH], state[i]) for i in two]
    pulled = [dot(m_ref[i], jnp.concatenate([grad[i], end[i].astype(F32)], axis=0), 0, 0) for i in two]
    value_grad = [2.0 / (1.0 + jnp.exp(-logit[i])) * pulled[i] for i in two]
    cross = [
        dot(jnp.concatenate([grad[i], value_grad[i]], axis=0), updates[i], 1, 1) for i in two
    ]
    pairs = [
        jnp.concatenate(
            [
                jnp.where(visible_mask(), cross[i][:WIDTH], 0.0),
                jnp.where(before, -cross[i][WIDTH:], 0.0),
            ],
            axis=0,
        )
        for i in two
    ]
    forward = [dot(pairs[i], key[i]) for i in two]
    backward = [dot(pairs[i], jnp.concatenate([query[i], key[i]], axis=0), 0, 0) for i in two]
    by_state = [
        dot(jnp.concatenate([grad[i], -value_grad[i]], axis=0), state[i], 1, 1, passes=1)
        for i in two
    ]
    by_end = [dot(updates[i], end[i], 1, 1, passes=1) for i in two]
    for i in two:
        start = i * PAIRS
        dv_ref[:, start : start + WIDTH] = value_grad[i][:WIDTH].astype(BF16)
        dv_ref[:, start + WIDTH : start + PAIRS] = value_grad[i][WIDTH:].astype(BF16)
        slope = jnp.sum(pulled[i] * updates[i], axis=1, keepdims=True) / (1.0 + jnp.exp(logit[i]))
        dlogit_ref[pl.ds(first + i, 1), :] = row_of(slope)
        query_grad = forward[i][:WIDTH] + by_state[i][:WIDTH]
        query_grad = query_scale[i] * (
            query_grad - query[i] * jnp.sum(query[i] * query_grad, axis=1, keepdims=True)
        )
        dq_ref[:, i * WIDTH : (i + 1) * WIDTH] = query_grad.astype(BF16)
        key_grad = forward[i][WIDTH:] + backward[i] + by_end[i] + by_state[i][WIDTH:]
        key_grad = key_scale[i] * (
            key_grad - key[i] * jnp.sum(key[i] * key_grad, axis=1, keepdims=True)
        )
        dk_ref[:, start : start + WIDTH] = key_grad[:WIDTH].astype(BF16)
        dk_ref[:, start + WIDTH : start + PAIRS] = key_grad[WIDTH:].astype(BF16)


def pull(place, queries, keys, logits, reads, wy, state, end, head_grad):
    return call(
        pull_kernel,
        2,
        [
            by_columns(WIDTH),
            by_columns(PAIRS),
            whole(4, PAIRS),
            by_pair(PAIRS, PAIRS),
            by_pair(PAIRS, PAIRS),
            by_slot(WIDTH, WIDTH),
            by_slot(WIDTH, WIDTH),
            by_columns(WIDTH),
        ],
        [by_columns(WIDTH), by_columns(PAIRS), by_columns(PAIRS), whole(4, PAIRS)],
        [
            arr(BF16, WIDTH, 512),
            arr(BF16, WIDTH, 1024),
            arr(BF16, WIDTH, 1024),
            arr(F32, 4, PAIRS),
        ],
        4 * 14 * 2 * PAIRS**3,
        5 << 20,
    )(place, queries, keys, logits, reads, wy, state, end, head_grad)


def mul(a, b):
    return jnp.einsum("hij,hjk->hik", a, b, preferred_element_type=F32)


def mul_t(a, b):
    return jnp.einsum("hji,hjk->hik", a, b, preferred_element_type=F32)


def halves(x):
    return x[:, :, :WIDTH], x[:, :, WIDTH:]


def forward_states(place, mine, theirs, core, grad_full, weight):
    theirs = exchange(theirs, 1)
    even = jnp.where(core == 0, mine, theirs)
    odd = jnp.where(core == 0, theirs, mine)
    even_a, even_b = halves(even)
    odd_a, odd_b = halves(odd)
    joined = mul(odd_a, even)
    chip = jnp.concatenate(
        [joined[:, :, :WIDTH], joined[:, :, WIDTH:] + odd_b.astype(F32)], axis=2
    ).astype(BF16)
    one, two, three, four = [send(chip, 2 * k) for k in range(1, 5)]
    window1, state = halves(one)
    third, inner = halves(three)
    outer = mul(window1, two)
    state = state.astype(F32) + outer[:, :, WIDTH:]
    window2 = outer[:, :, :WIDTH].astype(BF16)
    step = mul(third, four)
    inner = (inner.astype(F32) + step[:, :, WIDTH:]).astype(BF16)
    step = jnp.concatenate([step[:, :, :WIDTH].astype(BF16), inner, third], axis=2)
    step = mul(window2, step)
    window4 = step[:, :, :WIDTH].astype(BF16)
    state = state + step[:, :, WIDTH : 2 * WIDTH]
    window3 = step[:, :, 2 * WIDTH :].astype(BF16)
    rounded = state.astype(BF16)
    both = jnp.concatenate([window4, rounded], axis=2)
    grad_full, both = lax.optimization_barrier((grad_full, both))
    near, mid, far_b = send(both, 8), send(both, 16), send(rounded, 24)
    grad_other = exchange(grad_full, 1)
    kept_grad, given_grad = head_gradient(place, grad_full, grad_other, weight)
    kept_grad, given_grad, near, mid, far_b = lax.optimization_barrier(
        (kept_grad, given_grad, near, mid, far_b)
    )
    near_a, near_b = halves(near)
    mid_a, mid_b = halves(mid)
    head_grad = (kept_grad, exchange(given_grad, 1))
    inner = (mid_b.astype(F32) + mul(mid_a, far_b)).astype(BF16)
    inner = (near_b.astype(F32) + mul(near_a, inner)).astype(BF16)
    first = (state + mul(window4, inner)).astype(BF16)
    window8 = mul(window4, near_a).astype(BF16)
    window12 = mul(window8, mid_a).astype(BF16)
    second = (mul(even_a, first) + even_b.astype(F32)).astype(BF16)
    kept = jnp.where(core == 0, first, second)
    given = jnp.where(core == 0, second, first)
    state_in = jnp.concatenate([kept, exchange(given, 1)], axis=0)
    return grad_full, grad_other, head_grad, state_in, (even_a, odd_a, (window1, window2, window3), window4, window8, window12)


def backward_states(mine, theirs, core, saved, gate):
    even_a, odd_a, near_windows, window4, window8, window12 = saved
    theirs = exchange(theirs, 1)
    even = jnp.where(core == 0, mine, theirs)
    odd = jnp.where(core == 0, theirs, mine)
    total = even.astype(F32) + mul_t(even_a, odd)
    rounded = total.astype(BF16)
    for k, window in enumerate(near_windows):
        total = total + send(mul_t(window, rounded).astype(BF16), -2 * k - 2).astype(F32)
    rounded = total.astype(BF16)
    second = send(rounded, -2).astype(F32)
    for window, distance in ((window4, 10), (window8, 18), (window12, 26)):
        second += send(mul_t(window, rounded).astype(BF16), -distance).astype(F32)
    second = second.astype(BF16)
    first = (odd.astype(F32) + mul_t(odd_a, second)).astype(BF16)
    kept = jnp.where(core == 0, first, second)
    given = jnp.where(core == 0, second, first)
    return gate, jnp.concatenate([kept, exchange(given, 1)], axis=0)


def local(queries, keys, values, beta_logit, out_weight, out_grad):
    index = lax.axis_index("ctx")
    core = index & 1
    place = jnp.stack([core, index >> 4]).astype(jnp.int32)
    rings = [[(half * 8 + z) * 2 + c for z in range(8)] for half in range(2) for c in range(2)]
    operands = (queries, keys, values, beta_logit)
    across = exchange(out_weight, 16)
    theirs, *filled = prepare(place, *operands, False)
    across, theirs = lax.optimization_barrier((across, theirs))
    weight_pair = jnp.stack([out_weight, across])
    weight_pair, *operands = lax.optimization_barrier((weight_pair, *operands))
    mine, reads, wy, qt, local_out = prepare(place, *operands, True, filled)
    weight_mine = lax.all_gather(weight_pair, "ctx", axis=0, axis_index_groups=rings)
    grad_full = lax.all_to_all(
        jnp.broadcast_to(out_grad[None], (8, WIDTH, 512)), "tp", 0, 0, tiled=True
    )
    grad_full, grad_other, head_grad, state, saved = forward_states(
        place, mine, theirs, core, grad_full, weight_mine
    )
    heads = head_outputs(place, qt, local_out, state)
    heads_other = exchange(heads, 1)
    terms = weight_terms(place, grad_full, grad_other, heads, heads_other)
    ring_sum = lax.psum_scatter(
        terms, "ctx", scatter_dimension=0, axis_index_groups=rings
    ).reshape(2, WIDTH, 512)
    head_grad, own, own_theirs = own_cotangent(place, *head_grad, qt)
    parts = mixed_parts(place, heads, heads_other, weight_mine)
    parts, end = backward_states(own, own_theirs, core, saved, parts)
    end, ring_sum = lax.optimization_barrier((end, ring_sum))
    weight_grad = ring_sum[0].astype(F32) + exchange(ring_sum[1], 16).astype(F32)
    parts = lax.all_to_all(parts, "tp", 0, 0, tiled=True)
    sums = jnp.sum(parts.astype(F32), axis=0).astype(BF16)
    kept, came = sums[:WIDTH], exchange(sums[WIDTH:], 1)
    first, second = jnp.where(core == 0, kept, came), jnp.where(core == 0, came, kept)
    mixed = jnp.concatenate(
        [first[:, :WIDTH], second[:, :WIDTH], first[:, WIDTH:], second[:, WIDTH:]], axis=1
    )
    query_grad, key_grad, value_grad, logit_grad = pull(
        place, queries, keys, beta_logit, reads, wy, state, end, head_grad
    )
    return mixed, query_grad, key_grad, value_grad, logit_grad, weight_grad


def solution(mesh):
    placed = P("ctx", "tp")
    return jax.shard_map(
        local,
        mesh=mesh,
        in_specs=(placed, placed, placed, P("tp", "ctx"), placed, placed),
        out_specs=(placed, placed, placed, placed, P("tp", "ctx"), placed),
        check_vma=False,
    )
```

```python
import functools
import math

import jax
import jax.numpy as jnp
from jax import lax
from jax.experimental import pallas as pl
from jax.experimental.pallas import tpu as pltpu
from jax.sharding import PartitionSpec as P

F32 = jnp.float32
BF16 = jnp.bfloat16
WIDTH = 128
VMEM = 62 << 20
PAIRS = 2 * WIDTH


def send(block, distance):
    devices = range(lax.axis_size("ctx"))
    route = [(i - distance, i) for i in devices if i - distance in devices]
    return lax.ppermute(block, "ctx", route)


def exchange(block, bit):
    route = [(i, i ^ bit) for i in range(lax.axis_size("ctx"))]
    return lax.ppermute(block, "ctx", route)


def split(x):
    high = x.astype(BF16)
    return high, (x - high.astype(F32)).astype(BF16)


def dot(a, b, ca=1, cb=0, passes=3):
    dims = (((ca,), (cb,)), ((), ()))
    mul = functools.partial(lax.dot_general, dimension_numbers=dims, preferred_element_type=F32)
    if passes == 1:
        return mul(a.astype(BF16), b.astype(BF16))
    if b.dtype == BF16:
        a_high, a_low = split(a)
        return mul(a_high, b) + mul(a_low, b)
    a_high, a_low = split(a)
    b_high, b_low = split(b)
    return mul(a_high, b_high) + (mul(a_low, b_high) + mul(a_high, b_low))


def inverse_norm(x):
    return lax.rsqrt(jnp.sum(x * x, axis=-1, keepdims=True) + 1e-06)


def order_of(shape, dim):
    p = lax.broadcasted_iota(jnp.int32, shape, dim)
    return 2 * (p & (WIDTH - 1)) + (p >> 7)


def column_of(row):
    shape = (PAIRS, PAIRS)
    time = lax.broadcasted_iota(jnp.int32, shape, 1)
    return jnp.sum(jnp.where(time == order_of(shape, 0), row, 0.0), axis=1, keepdims=True)


def row_of(column):
    shape = (PAIRS, PAIRS)
    time = lax.broadcasted_iota(jnp.int32, shape, 1)
    return jnp.sum(jnp.where(time == order_of(shape, 0), column, 0.0), axis=0, keepdims=True)


def visible_mask():
    shape = (WIDTH, PAIRS)
    token = lax.broadcasted_iota(jnp.int32, shape, 0)
    return (lax.broadcasted_iota(jnp.int32, shape, 1) & (WIDTH - 1)) <= token


def stacked(ref, i):
    start = i * PAIRS
    parts = [ref[:, start : start + WIDTH], ref[:, start + WIDTH : start + PAIRS]]
    return jnp.concatenate(parts, axis=0).astype(F32)


def prepare_kernel(mine, *refs):
    place, q_ref, k_ref, v_ref, logit_ref = refs[:5]
    first = 2 * (place[0] if mine else 1 - place[0])
    ab_ref, m_ref, wy_ref, qt_ref, local_ref = refs[-5:]
    two = range(2)
    shape = (PAIRS, PAIRS)
    row, col = order_of(shape, 0), order_of(shape, 1)
    identity = jnp.where(row == col, 1.0, 0.0).astype(F32)
    query = [q_ref[:, i * WIDTH : (i + 1) * WIDTH].astype(F32) for i in two]
    query = [x * inverse_norm(x) for x in query]
    key = [stacked(k_ref, i) for i in two]
    key = [x * inverse_norm(x) for x in key]
    strength = [2.0 / (1.0 + jnp.exp(-column_of(logit_ref[pl.ds(first + i, 1), :]))) for i in two]
    coupling = [jnp.where(col < row, strength[i] * dot(key[i], key[i], 1, 1), 0.0) for i in two]
    inverse = [identity - jnp.where((row >> 1) == (col >> 1), coupling[i], 0.0) for i in two]
    for level in range(1, 8):
        join = ((row >> (level + 1)) == (col >> (level + 1))) & ((row >> level) != (col >> level))
        edge = [jnp.where(join, coupling[i], 0.0) for i in two]
        step = [dot(inverse[i], edge[i], passes=1) for i in two]
        inverse = [inverse[i] - dot(step[i], inverse[i], passes=1) for i in two]
    rest = [identity - inverse[i] - dot(coupling[i], inverse[i]) for i in two]
    inverse = [inverse[i] + dot(inverse[i], rest[i], passes=1) for i in two]
    scores = [jnp.where(visible_mask(), dot(query[i], key[i], 1, 1), 0.0) for i in two]
    scaled = [strength[i] * jnp.concatenate([key[i], stacked(v_ref, i)], axis=1) for i in two]
    reads = [
        jnp.concatenate([dot(scores[i], inverse[i]), dot(key[i], inverse[i], 0, 0)], axis=0)
        for i in two
    ]
    product = [dot(reads[i], scaled[i]) for i in two]
    eye = identity[:WIDTH, :WIDTH]
    for i in two:
        ab_ref[i, :, :WIDTH] = (eye - product[i][WIDTH:, :WIDTH]).astype(BF16)
        ab_ref[i, :, WIDTH:] = product[i][WIDTH:, WIDTH:].astype(BF16)
        qt_ref[i] = query[i] - product[i][:WIDTH, :WIDTH]
        local_ref[i] = product[i][:WIDTH, WIDTH:]
        m_ref[i] = reads[i]
        wy_ref[i] = dot(inverse[i], scaled[i])


def slot(head, place):
    return (head + 2 * place[0]) % 4


def by_pair(*block):
    return pl.BlockSpec((2,) + block, lambda i, place: (i,) + (0,) * len(block))


def by_slot(*block):
    return pl.BlockSpec((2,) + block, lambda i, place: (i ^ place[0],) + (0,) * len(block))


def by_columns(width):
    return pl.BlockSpec((WIDTH, 2 * width), lambda i, place: (0, i))


def whole(*shape):
    return pl.BlockSpec(shape, lambda i, place: (0,) * len(shape))


def call(kernel, steps, in_specs, out_specs, out_shape, flops, moved, scratch=()):
    return pl.pallas_call(
        kernel,
        grid_spec=pltpu.PrefetchScalarGridSpec(
            num_scalar_prefetch=1,
            grid=(steps,),
            in_specs=in_specs,
            out_specs=out_specs,
            scratch_shapes=list(scratch),
        ),
        out_shape=out_shape,
        compiler_params=pltpu.CompilerParams(vmem_limit_bytes=VMEM),
        cost_estimate=pl.CostEstimate(flops=flops, bytes_accessed=moved, transcendentals=0),
    )


def arr(dtype, *shape):
    return jax.ShapeDtypeStruct(shape, dtype)


def prepare(place, queries, keys, values, logits, mine, filled=()):
    def pair(place):
        return place[0] if mine else 1 - place[0]

    def columns(width):
        return pl.BlockSpec((WIDTH, 2 * width), lambda i, place: (0, pair(place)))

    def heads(*block):
        return pl.BlockSpec((2,) + block, lambda i, place: (pair(place),) + (0,) * len(block))

    def stored(n):
        return arr(F32, 4, n, n)

    return pl.pallas_call(
        functools.partial(prepare_kernel, mine),
        grid_spec=pltpu.PrefetchScalarGridSpec(
            num_scalar_prefetch=1,
            grid=(1,),
            in_specs=[
                columns(WIDTH),
                columns(PAIRS),
                columns(PAIRS),
                whole(4, PAIRS),
            ]
            + [pl.BlockSpec(memory_space=pl.ANY)] * len(filled),
            out_specs=[
                pl.BlockSpec((2, WIDTH, PAIRS), lambda i, place: (0, 0, 0)),
                heads(PAIRS, PAIRS),
                heads(PAIRS, PAIRS),
                heads(WIDTH, WIDTH),
                heads(WIDTH, WIDTH),
            ],
        ),
        out_shape=[
            arr(BF16, 2, WIDTH, PAIRS),
            stored(PAIRS),
            stored(PAIRS),
            stored(WIDTH),
            stored(WIDTH),
        ],
        input_output_aliases={5 + i: 1 + i for i in range(len(filled))},
        compiler_params=pltpu.CompilerParams(vmem_limit_bytes=VMEM),
        cost_estimate=pl.CostEstimate(
            flops=(1 if mine else 100) << 20, bytes_accessed=1 << (16 if mine else 24), transcendentals=0
        ),
    )(place, queries, keys, values, logits, *filled)


STEPS = 4
BLOCKS = [(z, row) for z in range(2) for row in range(2)]


def grad_rows(place, step, own_ref, other_ref):
    def block(ref, z, row):
        column = pl.multiple_of(z * 256 + place[0] * 128, 128)
        return ref[(row ^ place[1]) * 4 + step, :, pl.ds(column, 128)]

    rows = [
        jnp.concatenate([block(ref, *place_of) for place_of in BLOCKS], axis=1)
        for ref in (own_ref, other_ref)
    ]
    return jnp.concatenate(rows, axis=0)


def weight_rows(ref):
    return jnp.concatenate([ref[z, row] for z, row in BLOCKS], axis=0)


def weight_tile():
    return pl.BlockSpec((2, 2, WIDTH, 512), lambda step, place: (step, 0, 0, 0))


def heads_kernel(place, qt_ref, local_ref, state_ref, heads_ref):
    for head in range(4):
        result = dot(qt_ref[head], state_ref[slot(head, place)]) + local_ref[head]
        heads_ref[:, head * WIDTH : (head + 1) * WIDTH] = result.astype(BF16)


def head_outputs(place, qt, local, state):
    square = whole(4, WIDTH, WIDTH)
    return call(
        heads_kernel,
        1,
        [square, square, square],
        whole(WIDTH, 512),
        arr(BF16, WIDTH, 512),
        2 * 4 * 128**3,
        1 << 20,
    )(place, qt, local, state)


def weight_terms_kernel(place, own_ref, other_ref, heads_ref, heads_other_ref, out_ref):
    product = lax.dot_general(
        grad_rows(place, pl.program_id(0), own_ref, other_ref),
        jnp.concatenate([heads_ref[...], heads_other_ref[...]], axis=0),
        (((0,), (0,)), ((), ())),
        preferred_element_type=F32,
    )
    product = (product * (1.0 / 64.0)).astype(BF16)
    for z in range(2):
        out_ref[z] = product[z * 256 : z * 256 + 256]


def weight_terms(place, grad_full, grad_other, heads, heads_other):
    return call(
        weight_terms_kernel,
        STEPS,
        [whole(8, WIDTH, 512), whole(8, WIDTH, 512), whole(WIDTH, 512), whole(WIDTH, 512)],
        pl.BlockSpec((2, 256, 512), lambda step, place: (step, 0, 0)),
        arr(BF16, 8, 256, 512),
        2 * 128 * 512 * 4096,
        5 << 20,
    )(place, grad_full, grad_other, heads, heads_other)


def mixed_kernel(place, heads_ref, heads_other_ref, weight_ref, out_ref):
    step = pl.program_id(0)
    product = lax.dot_general(
        jnp.concatenate([heads_ref[...], heads_other_ref[...]], axis=0),
        weight_rows(weight_ref),
        (((1,), (1,)), ((), ())),
        preferred_element_type=F32,
    ).astype(BF16)
    for i, (z, row) in enumerate(BLOCKS):
        owner = (row ^ place[1]) * 4 + step
        out_ref[owner, :, z * 128 : z * 128 + 128] = product[:, i * WIDTH : (i + 1) * WIDTH]


def mixed_parts(place, heads, heads_other, weight):
    return call(
        mixed_kernel,
        STEPS,
        [whole(WIDTH, 512), whole(WIDTH, 512), weight_tile()],
        whole(8, 256, 256),
        arr(BF16, 8, 256, 256),
        2 * 128 * 512 * 4096,
        3 << 20,
    )(place, heads, heads_other, weight)


def head_grad_kernel(place, own_ref, other_ref, weight_ref, kept_ref, given_ref):
    step = pl.program_id(0)
    total = jnp.dot(
        grad_rows(place, step, own_ref, other_ref),
        weight_rows(weight_ref),
        preferred_element_type=F32,
    )

    @pl.when(step == 0)
    def _():
        kept_ref[...] = total[:WIDTH]
        given_ref[...] = total[WIDTH:]

    @pl.when(step > 0)
    def _():
        kept_ref[...] += total[:WIDTH]
        given_ref[...] += total[WIDTH:]


def head_gradient(place, grad_full, grad_other, weight):
    part = arr(F32, WIDTH, 512)
    return call(
        head_grad_kernel,
        STEPS,
        [whole(8, WIDTH, 512), whole(8, WIDTH, 512), weight_tile()],
        [whole(WIDTH, 512), whole(WIDTH, 512)],
        [part, part],
        2 * 128 * 512 * 4096,
        5 << 20,
    )(place, grad_full, grad_other, weight)


def own_kernel(place, kept_ref, came_ref, qt_ref, grad_ref, mine_ref, theirs_ref):
    grad_ref[...] = kept_ref[...] + came_ref[...]
    for head in range(4):
        grad = grad_ref[:, head * WIDTH : (head + 1) * WIDTH]
        own = dot(qt_ref[head], grad, 0, 0, passes=1).astype(BF16)

        @pl.when(place[0] == head // 2)
        def _():
            mine_ref[head % 2] = own

        @pl.when(place[0] != head // 2)
        def _():
            theirs_ref[head % 2] = own


def own_cotangent(place, kept, came, qt):
    pair = arr(BF16, 2, WIDTH, WIDTH)
    return call(
        own_kernel,
        1,
        [whole(WIDTH, 512), whole(WIDTH, 512), whole(4, WIDTH, WIDTH)],
        [whole(WIDTH, 512), whole(2, WIDTH, WIDTH), whole(2, WIDTH, WIDTH)],
        [arr(F32, WIDTH, 512), pair, pair],
        1 << 10,
        1 << 10,
    )(place, kept, came, qt)


def pull_kernel(
    place, q_ref, k_ref, logit_ref, m_ref, wy_ref, state_ref, end_ref, grad_ref,
    dq_ref, dk_ref, dv_ref, dlogit_ref,
):
    two = range(2)
    shape = (PAIRS, PAIRS)
    before = order_of(shape, 1) < order_of(shape, 0)
    query = [q_ref[:, i * WIDTH : (i + 1) * WIDTH].astype(F32) for i in two]
    query_scale = [inverse_norm(x) for x in query]
    query = [query[i] * query_scale[i] for i in two]
    key = [stacked(k_ref, i) for i in two]
    key_scale = [inverse_norm(x) for x in key]
    key = [key[i] * key_scale[i] for i in two]
    first = 2 * pl.program_id(0)
    logit = [column_of(logit_ref[pl.ds(first + i, 1), :]) for i in two]
    state = [state_ref[i] for i in two]
    end = [end_ref[i] for i in two]
    grad = [grad_ref[:, i * WIDTH : (i + 1) * WIDTH] for i in two]
    updates = [wy_ref[i, :, WIDTH:] - dot(wy_ref[i, :, :WIDTH], state[i]) for i in two]
    pulled = [dot(m_ref[i], jnp.concatenate([grad[i], end[i].astype(F32)], axis=0), 0, 0) for i in two]
    value_grad = [2.0 / (1.0 + jnp.exp(-logit[i])) * pulled[i] for i in two]
    cross = [
        dot(jnp.concatenate([grad[i], value_grad[i]], axis=0), updates[i], 1, 1) for i in two
    ]
    pairs = [
        jnp.concatenate(
            [
                jnp.where(visible_mask(), cross[i][:WIDTH], 0.0),
                jnp.where(before, -cross[i][WIDTH:], 0.0),
            ],
            axis=0,
        )
        for i in two
    ]
    forward = [dot(pairs[i], key[i]) for i in two]
    backward = [dot(pairs[i], jnp.concatenate([query[i], key[i]], axis=0), 0, 0) for i in two]
    by_state = [
        dot(jnp.concatenate([grad[i], -value_grad[i]], axis=0), state[i], 1, 1, passes=1)
        for i in two
    ]
    by_end = [dot(updates[i], end[i], 1, 1, passes=1) for i in two]
    for i in two:
        start = i * PAIRS
        dv_ref[:, start : start + WIDTH] = value_grad[i][:WIDTH].astype(BF16)
        dv_ref[:, start + WIDTH : start + PAIRS] = value_grad[i][WIDTH:].astype(BF16)
        slope = jnp.sum(pulled[i] * updates[i], axis=1, keepdims=True) / (1.0 + jnp.exp(logit[i]))
        dlogit_ref[pl.ds(first + i, 1), :] = row_of(slope)
        query_grad = forward[i][:WIDTH] + by_state[i][:WIDTH]
        query_grad = query_scale[i] * (
            query_grad - query[i] * jnp.sum(query[i] * query_grad, axis=1, keepdims=True)
        )
        dq_ref[:, i * WIDTH : (i + 1) * WIDTH] = query_grad.astype(BF16)
        key_grad = forward[i][WIDTH:] + backward[i] + by_end[i] + by_state[i][WIDTH:]
        key_grad = key_scale[i] * (
            key_grad - key[i] * jnp.sum(key[i] * key_grad, axis=1, keepdims=True)
        )
        dk_ref[:, start : start + WIDTH] = key_grad[:WIDTH].astype(BF16)
        dk_ref[:, start + WIDTH : start + PAIRS] = key_grad[WIDTH:].astype(BF16)


def pull(place, queries, keys, logits, reads, wy, state, end, head_grad):
    return call(
        pull_kernel,
        2,
        [
            by_columns(WIDTH),
            by_columns(PAIRS),
            whole(4, PAIRS),
            by_pair(PAIRS, PAIRS),
            by_pair(PAIRS, PAIRS),
            by_slot(WIDTH, WIDTH),
            by_slot(WIDTH, WIDTH),
            by_columns(WIDTH),
        ],
        [by_columns(WIDTH), by_columns(PAIRS), by_columns(PAIRS), whole(4, PAIRS)],
        [
            arr(BF16, WIDTH, 512),
            arr(BF16, WIDTH, 1024),
            arr(BF16, WIDTH, 1024),
            arr(F32, 4, PAIRS),
        ],
        4 * 14 * 2 * PAIRS**3,
        5 << 20,
    )(place, queries, keys, logits, reads, wy, state, end, head_grad)


def mul(a, b):
    return jnp.einsum("hij,hjk->hik", a, b, preferred_element_type=F32)


def mul_t(a, b):
    return jnp.einsum("hji,hjk->hik", a, b, preferred_element_type=F32)


def halves(x):
    return x[:, :, :WIDTH], x[:, :, WIDTH:]


def forward_states(place, mine, theirs, core, grad_full, weight, qt):
    theirs = exchange(theirs, 1)
    even = jnp.where(core == 0, mine, theirs)
    odd = jnp.where(core == 0, theirs, mine)
    even_a, even_b = halves(even)
    odd_a, odd_b = halves(odd)
    joined = mul(odd_a, even)
    chip = jnp.concatenate(
        [joined[:, :, :WIDTH], joined[:, :, WIDTH:] + odd_b.astype(F32)], axis=2
    ).astype(BF16)
    one, two = send(chip, 2), send(chip, 4)
    window1, state = halves(one)
    step = mul(window1, two)
    state = state.astype(F32) + step[:, :, WIDTH:]
    window2 = step[:, :, :WIDTH].astype(BF16)
    step = mul(window2, send(jnp.concatenate([window2, state.astype(BF16)], axis=2), 4))
    state = state + step[:, :, WIDTH:]
    window4 = step[:, :, :WIDTH].astype(BF16)
    rounded = state.astype(BF16)
    both = jnp.concatenate([window4, rounded], axis=2)
    grad_full, both = lax.optimization_barrier((grad_full, both))
    near = send(both, 8)
    grad_other = exchange(grad_full, 1)
    kept_grad, given_grad = head_gradient(place, grad_full, grad_other, weight)
    kept_grad, given_grad, near = lax.optimization_barrier((kept_grad, given_grad, near))
    step = mul(window4, near)
    window8 = step[:, :, :WIDTH].astype(BF16)
    state = state + step[:, :, WIDTH:]
    far = send(jnp.concatenate([window4, state.astype(BF16)], axis=2), 16)
    head_grad, own, own_theirs = own_cotangent(place, kept_grad, exchange(given_grad, 1), qt)
    head_grad, own, own_theirs, far = lax.optimization_barrier((head_grad, own, own_theirs, far))
    step = mul(window8, far)
    window12 = step[:, :, :WIDTH].astype(BF16)
    first = (state + step[:, :, WIDTH:]).astype(BF16)
    second = (mul(even_a, first) + even_b.astype(F32)).astype(BF16)
    kept = jnp.where(core == 0, first, second)
    given = jnp.where(core == 0, second, first)
    state_in = jnp.concatenate([kept, exchange(given, 1)], axis=0)
    head_grad = (head_grad, own, own_theirs)
    return grad_full, grad_other, head_grad, state_in, (even_a, odd_a, window1, window2, window4, window8, window12)


def backward_states(mine, theirs, core, saved, gate):
    even_a, odd_a, window1, window2, window4, window8, window12 = saved
    theirs = exchange(theirs, 1)
    even = jnp.where(core == 0, mine, theirs)
    odd = jnp.where(core == 0, theirs, mine)
    total = even.astype(F32) + mul_t(even_a, odd)
    for window, distance in ((window1, 2), (window2, 4)):
        passed = mul_t(window, total.astype(BF16)).astype(BF16)
        came = send(passed, -distance)
        if distance == 2:
            gate, came = lax.optimization_barrier((gate, came))
        total = total + came.astype(F32)
    rounded = total.astype(BF16)
    second = send(rounded, -2).astype(F32)
    for window, distance in ((window4, 10), (window8, 18), (window12, 26)):
        second += send(mul_t(window, rounded).astype(BF16), -distance).astype(F32)
    second = second.astype(BF16)
    first = (odd.astype(F32) + mul_t(odd_a, second)).astype(BF16)
    kept = jnp.where(core == 0, first, second)
    given = jnp.where(core == 0, second, first)
    return gate, jnp.concatenate([kept, exchange(given, 1)], axis=0)


def local(queries, keys, values, beta_logit, out_weight, out_grad):
    index = lax.axis_index("ctx")
    core = index & 1
    place = jnp.stack([core, index >> 4]).astype(jnp.int32)
    rings = [[(half * 8 + z) * 2 + c for z in range(8)] for half in range(2) for c in range(2)]
    operands = (queries, keys, values, beta_logit)
    across = exchange(out_weight, 16)
    theirs, *filled = prepare(place, *operands, False)
    across, theirs = lax.optimization_barrier((across, theirs))
    weight_pair = jnp.stack([out_weight, across])
    weight_pair, *operands = lax.optimization_barrier((weight_pair, *operands))
    mine, reads, wy, qt, local_out = prepare(place, *operands, True, filled)
    weight_mine = lax.all_gather(weight_pair, "ctx", axis=0, axis_index_groups=rings)
    grad_full = lax.all_to_all(
        jnp.broadcast_to(out_grad[None], (8, WIDTH, 512)), "tp", 0, 0, tiled=True
    )
    grad_full, grad_other, head_grad, state, saved = forward_states(
        place, mine, theirs, core, grad_full, weight_mine, qt
    )
    heads = head_outputs(place, qt, local_out, state)
    heads_other = exchange(heads, 1)
    terms = weight_terms(place, grad_full, grad_other, heads, heads_other)
    ring_sum = lax.psum_scatter(
        terms, "ctx", scatter_dimension=0, axis_index_groups=rings
    ).reshape(2, WIDTH, 512)
    head_grad, own, own_theirs = head_grad
    parts = mixed_parts(place, heads, heads_other, weight_mine)
    parts, end = backward_states(own, own_theirs, core, saved, parts)
    end, ring_sum = lax.optimization_barrier((end, ring_sum))
    weight_grad = ring_sum[0].astype(F32) + exchange(ring_sum[1], 16).astype(F32)
    parts = lax.all_to_all(parts, "tp", 0, 0, tiled=True)
    sums = jnp.sum(parts.astype(F32), axis=0).astype(BF16)
    kept, came = sums[:WIDTH], exchange(sums[WIDTH:], 1)
    first, second = jnp.where(core == 0, kept, came), jnp.where(core == 0, came, kept)
    mixed = jnp.concatenate(
        [first[:, :WIDTH], second[:, :WIDTH], first[:, WIDTH:], second[:, WIDTH:]], axis=1
    )
    query_grad, key_grad, value_grad, logit_grad = pull(
        place, queries, keys, beta_logit, reads, wy, state, end, head_grad
    )
    return mixed, query_grad, key_grad, value_grad, logit_grad, weight_grad


def solution(mesh):
    placed = P("ctx", "tp")
    return jax.shard_map(
        local,
        mesh=mesh,
        in_specs=(placed, placed, placed, P("tp", "ctx"), placed, placed),
        out_specs=(placed, placed, placed, placed, P("tp", "ctx"), placed),
        check_vma=False,
    )
```

```python
import functools
import math

import jax
import jax.numpy as jnp
from jax import lax
from jax.experimental import pallas as pl
from jax.experimental.pallas import tpu as pltpu
from jax.sharding import PartitionSpec as P

F32 = jnp.float32
BF16 = jnp.bfloat16
WIDTH = 128
VMEM = 62 << 20
PAIRS = 2 * WIDTH


def send(block, distance):
    devices = range(lax.axis_size("ctx"))
    route = [(i - distance, i) for i in devices if i - distance in devices]
    return lax.ppermute(block, "ctx", route)


def exchange(block, bit):
    route = [(i, i ^ bit) for i in range(lax.axis_size("ctx"))]
    return lax.ppermute(block, "ctx", route)


def split(x):
    high = x.astype(BF16)
    return high, (x - high.astype(F32)).astype(BF16)


def dot(a, b, ca=1, cb=0, passes=3):
    dims = (((ca,), (cb,)), ((), ()))
    mul = functools.partial(lax.dot_general, dimension_numbers=dims, preferred_element_type=F32)
    if passes == 1:
        return mul(a.astype(BF16), b.astype(BF16))
    if b.dtype == BF16:
        a_high, a_low = split(a)
        return mul(a_high, b) + mul(a_low, b)
    a_high, a_low = split(a)
    b_high, b_low = split(b)
    return mul(a_high, b_high) + (mul(a_low, b_high) + mul(a_high, b_low))


def inverse_norm(x):
    return lax.rsqrt(jnp.sum(x * x, axis=-1, keepdims=True) + 1e-06)


def order_of(shape, dim):
    p = lax.broadcasted_iota(jnp.int32, shape, dim)
    return 2 * (p & (WIDTH - 1)) + (p >> 7)


def column_of(row):
    shape = (PAIRS, PAIRS)
    time = lax.broadcasted_iota(jnp.int32, shape, 1)
    return jnp.sum(jnp.where(time == order_of(shape, 0), row, 0.0), axis=1, keepdims=True)


def row_of(column):
    shape = (PAIRS, PAIRS)
    time = lax.broadcasted_iota(jnp.int32, shape, 1)
    return jnp.sum(jnp.where(time == order_of(shape, 0), column, 0.0), axis=0, keepdims=True)


def visible_mask():
    shape = (WIDTH, PAIRS)
    token = lax.broadcasted_iota(jnp.int32, shape, 0)
    return (lax.broadcasted_iota(jnp.int32, shape, 1) & (WIDTH - 1)) <= token


def stacked(ref, i):
    start = i * PAIRS
    parts = [ref[:, start : start + WIDTH], ref[:, start + WIDTH : start + PAIRS]]
    return jnp.concatenate(parts, axis=0).astype(F32)


def prepare_kernel(mine, *refs):
    place, q_ref, k_ref, v_ref, logit_ref = refs[:5]
    first = 2 * (place[0] if mine else 1 - place[0])
    ab_ref, m_ref, wy_ref, qt_ref, local_ref = refs[-5:]
    two = range(2)
    shape = (PAIRS, PAIRS)
    row, col = order_of(shape, 0), order_of(shape, 1)
    identity = jnp.where(row == col, 1.0, 0.0).astype(F32)
    query = [q_ref[:, i * WIDTH : (i + 1) * WIDTH].astype(F32) for i in two]
    query = [x * inverse_norm(x) for x in query]
    key = [stacked(k_ref, i) for i in two]
    key = [x * inverse_norm(x) for x in key]
    strength = [2.0 / (1.0 + jnp.exp(-column_of(logit_ref[pl.ds(first + i, 1), :]))) for i in two]
    coupling = [jnp.where(col < row, strength[i] * dot(key[i], key[i], 1, 1), 0.0) for i in two]
    inverse = [identity - jnp.where((row >> 1) == (col >> 1), coupling[i], 0.0) for i in two]
    for level in range(1, 8):
        join = ((row >> (level + 1)) == (col >> (level + 1))) & ((row >> level) != (col >> level))
        edge = [jnp.where(join, coupling[i], 0.0) for i in two]
        step = [dot(inverse[i], edge[i], passes=1) for i in two]
        inverse = [inverse[i] - dot(step[i], inverse[i], passes=1) for i in two]
    rest = [identity - inverse[i] - dot(coupling[i], inverse[i]) for i in two]
    inverse = [inverse[i] + dot(inverse[i], rest[i], passes=1) for i in two]
    scores = [jnp.where(visible_mask(), dot(query[i], key[i], 1, 1), 0.0) for i in two]
    scaled = [strength[i] * jnp.concatenate([key[i], stacked(v_ref, i)], axis=1) for i in two]
    reads = [
        jnp.concatenate([dot(scores[i], inverse[i]), dot(key[i], inverse[i], 0, 0)], axis=0)
        for i in two
    ]
    product = [dot(reads[i], scaled[i]) for i in two]
    eye = identity[:WIDTH, :WIDTH]
    for i in two:
        ab_ref[i, :, :WIDTH] = (eye - product[i][WIDTH:, :WIDTH]).astype(BF16)
        ab_ref[i, :, WIDTH:] = product[i][WIDTH:, WIDTH:].astype(BF16)
        qt_ref[i] = query[i] - product[i][:WIDTH, :WIDTH]
        local_ref[i] = product[i][:WIDTH, WIDTH:]
        m_ref[i] = reads[i]
        wy_ref[i] = dot(inverse[i], scaled[i])


def slot(head, place):
    return (head + 2 * place[0]) % 4


def by_pair(*block):
    return pl.BlockSpec((2,) + block, lambda i, place: (i,) + (0,) * len(block))


def by_slot(*block):
    return pl.BlockSpec((2,) + block, lambda i, place: (i ^ place[0],) + (0,) * len(block))


def by_columns(width):
    return pl.BlockSpec((WIDTH, 2 * width), lambda i, place: (0, i))


def whole(*shape):
    return pl.BlockSpec(shape, lambda i, place: (0,) * len(shape))


def call(kernel, steps, in_specs, out_specs, out_shape, flops, moved, scratch=()):
    return pl.pallas_call(
        kernel,
        grid_spec=pltpu.PrefetchScalarGridSpec(
            num_scalar_prefetch=1,
            grid=(steps,),
            in_specs=in_specs,
            out_specs=out_specs,
            scratch_shapes=list(scratch),
        ),
        out_shape=out_shape,
        compiler_params=pltpu.CompilerParams(vmem_limit_bytes=VMEM),
        cost_estimate=pl.CostEstimate(flops=flops, bytes_accessed=moved, transcendentals=0),
    )


def arr(dtype, *shape):
    return jax.ShapeDtypeStruct(shape, dtype)


def prepare(place, queries, keys, values, logits, mine, filled=()):
    def pair(place):
        return place[0] if mine else 1 - place[0]

    def columns(width):
        return pl.BlockSpec((WIDTH, 2 * width), lambda i, place: (0, pair(place)))

    def heads(*block):
        return pl.BlockSpec((2,) + block, lambda i, place: (pair(place),) + (0,) * len(block))

    def stored(n):
        return arr(F32, 4, n, n)

    return pl.pallas_call(
        functools.partial(prepare_kernel, mine),
        grid_spec=pltpu.PrefetchScalarGridSpec(
            num_scalar_prefetch=1,
            grid=(1,),
            in_specs=[
                columns(WIDTH),
                columns(PAIRS),
                columns(PAIRS),
                whole(4, PAIRS),
            ]
            + [pl.BlockSpec(memory_space=pl.ANY)] * len(filled),
            out_specs=[
                pl.BlockSpec((2, WIDTH, PAIRS), lambda i, place: (0, 0, 0)),
                heads(PAIRS, PAIRS),
                heads(PAIRS, PAIRS),
                heads(WIDTH, WIDTH),
                heads(WIDTH, WIDTH),
            ],
        ),
        out_shape=[
            arr(BF16, 2, WIDTH, PAIRS),
            stored(PAIRS),
            stored(PAIRS),
            stored(WIDTH),
            stored(WIDTH),
        ],
        input_output_aliases={5 + i: 1 + i for i in range(len(filled))},
        compiler_params=pltpu.CompilerParams(vmem_limit_bytes=VMEM),
        cost_estimate=pl.CostEstimate(
            flops=(1 if mine else 100) << 20, bytes_accessed=1 << (16 if mine else 24), transcendentals=0
        ),
    )(place, queries, keys, values, logits, *filled)


STEPS = 4
BLOCKS = [(z, row) for z in range(2) for row in range(2)]


def grad_rows(place, step, own_ref, other_ref):
    def block(ref, z, row):
        column = pl.multiple_of(z * 256 + place[0] * 128, 128)
        return ref[(row ^ place[1]) * 4 + step, :, pl.ds(column, 128)]

    rows = [
        jnp.concatenate([block(ref, *place_of) for place_of in BLOCKS], axis=1)
        for ref in (own_ref, other_ref)
    ]
    return jnp.concatenate(rows, axis=0)


def weight_rows(ref):
    return jnp.concatenate([ref[z, row] for z, row in BLOCKS], axis=0)


def weight_tile():
    return pl.BlockSpec((2, 2, WIDTH, 512), lambda step, place: (step, 0, 0, 0))


def heads_kernel(place, qt_ref, local_ref, state_ref, heads_ref):
    for head in range(4):
        result = dot(qt_ref[head], state_ref[slot(head, place)]) + local_ref[head]
        heads_ref[:, head * WIDTH : (head + 1) * WIDTH] = result.astype(BF16)


def head_outputs(place, qt, local, state):
    square = whole(4, WIDTH, WIDTH)
    return call(
        heads_kernel,
        1,
        [square, square, square],
        whole(WIDTH, 512),
        arr(BF16, WIDTH, 512),
        2 * 4 * 128**3,
        1 << 20,
    )(place, qt, local, state)


def weight_terms_kernel(place, own_ref, other_ref, heads_ref, heads_other_ref, out_ref):
    product = lax.dot_general(
        grad_rows(place, pl.program_id(0), own_ref, other_ref),
        jnp.concatenate([heads_ref[...], heads_other_ref[...]], axis=0),
        (((0,), (0,)), ((), ())),
        preferred_element_type=F32,
    )
    product = (product * (1.0 / 64.0)).astype(BF16)
    for z in range(2):
        out_ref[z] = product[z * 256 : z * 256 + 256]


def weight_terms(place, grad_full, grad_other, heads, heads_other):
    return call(
        weight_terms_kernel,
        STEPS,
        [whole(8, WIDTH, 512), whole(8, WIDTH, 512), whole(WIDTH, 512), whole(WIDTH, 512)],
        pl.BlockSpec((2, 256, 512), lambda step, place: (step, 0, 0)),
        arr(BF16, 8, 256, 512),
        2 * 128 * 512 * 4096,
        5 << 20,
    )(place, grad_full, grad_other, heads, heads_other)


def mixed_kernel(place, heads_ref, heads_other_ref, weight_ref, out_ref):
    step = pl.program_id(0)
    product = lax.dot_general(
        jnp.concatenate([heads_ref[...], heads_other_ref[...]], axis=0),
        weight_rows(weight_ref),
        (((1,), (1,)), ((), ())),
        preferred_element_type=F32,
    ).astype(BF16)
    for i, (z, row) in enumerate(BLOCKS):
        owner = (row ^ place[1]) * 4 + step
        out_ref[owner, :, z * 128 : z * 128 + 128] = product[:, i * WIDTH : (i + 1) * WIDTH]


def mixed_parts(place, heads, heads_other, weight):
    return call(
        mixed_kernel,
        STEPS,
        [whole(WIDTH, 512), whole(WIDTH, 512), weight_tile()],
        whole(8, 256, 256),
        arr(BF16, 8, 256, 256),
        2 * 128 * 512 * 4096,
        3 << 20,
    )(place, heads, heads_other, weight)


def head_grad_kernel(place, own_ref, other_ref, weight_ref, kept_ref, given_ref):
    step = pl.program_id(0)
    total = jnp.dot(
        grad_rows(place, step, own_ref, other_ref),
        weight_rows(weight_ref),
        preferred_element_type=F32,
    )

    @pl.when(step == 0)
    def _():
        kept_ref[...] = total[:WIDTH]
        given_ref[...] = total[WIDTH:]

    @pl.when(step > 0)
    def _():
        kept_ref[...] += total[:WIDTH]
        given_ref[...] += total[WIDTH:]


def head_gradient(place, grad_full, grad_other, weight):
    part = arr(F32, WIDTH, 512)
    return call(
        head_grad_kernel,
        STEPS,
        [whole(8, WIDTH, 512), whole(8, WIDTH, 512), weight_tile()],
        [whole(WIDTH, 512), whole(WIDTH, 512)],
        [part, part],
        2 * 128 * 512 * 4096,
        5 << 20,
    )(place, grad_full, grad_other, weight)


def own_kernel(place, kept_ref, came_ref, qt_ref, grad_ref, mine_ref, theirs_ref):
    grad_ref[...] = kept_ref[...] + came_ref[...]
    for head in range(4):
        grad = grad_ref[:, head * WIDTH : (head + 1) * WIDTH]
        own = dot(qt_ref[head], grad, 0, 0, passes=1).astype(BF16)

        @pl.when(place[0] == head // 2)
        def _():
            mine_ref[head % 2] = own

        @pl.when(place[0] != head // 2)
        def _():
            theirs_ref[head % 2] = own


def own_cotangent(place, kept, came, qt):
    pair = arr(BF16, 2, WIDTH, WIDTH)
    return call(
        own_kernel,
        1,
        [whole(WIDTH, 512), whole(WIDTH, 512), whole(4, WIDTH, WIDTH)],
        [whole(WIDTH, 512), whole(2, WIDTH, WIDTH), whole(2, WIDTH, WIDTH)],
        [arr(F32, WIDTH, 512), pair, pair],
        2 * 4 * 128**3,
        1 << 20,
    )(place, kept, came, qt)


def pull_kernel(
    place, q_ref, k_ref, logit_ref, m_ref, wy_ref, state_ref, end_ref, grad_ref,
    dq_ref, dk_ref, dv_ref, dlogit_ref,
):
    two = range(2)
    shape = (PAIRS, PAIRS)
    before = order_of(shape, 1) < order_of(shape, 0)
    query = [q_ref[:, i * WIDTH : (i + 1) * WIDTH].astype(F32) for i in two]
    query_scale = [inverse_norm(x) for x in query]
    query = [query[i] * query_scale[i] for i in two]
    key = [stacked(k_ref, i) for i in two]
    key_scale = [inverse_norm(x) for x in key]
    key = [key[i] * key_scale[i] for i in two]
    first = 2 * pl.program_id(0)
    logit = [column_of(logit_ref[pl.ds(first + i, 1), :]) for i in two]
    state = [state_ref[i] for i in two]
    end = [end_ref[i] for i in two]
    grad = [grad_ref[:, i * WIDTH : (i + 1) * WIDTH] for i in two]
    updates = [wy_ref[i, :, WIDTH:] - dot(wy_ref[i, :, :WIDTH], state[i]) for i in two]
    pulled = [dot(m_ref[i], jnp.concatenate([grad[i], end[i].astype(F32)], axis=0), 0, 0) for i in two]
    value_grad = [2.0 / (1.0 + jnp.exp(-logit[i])) * pulled[i] for i in two]
    cross = [
        dot(jnp.concatenate([grad[i], value_grad[i]], axis=0), updates[i], 1, 1) for i in two
    ]
    pairs = [
        jnp.concatenate(
            [
                jnp.where(visible_mask(), cross[i][:WIDTH], 0.0),
                jnp.where(before, -cross[i][WIDTH:], 0.0),
            ],
            axis=0,
        )
        for i in two
    ]
    forward = [dot(pairs[i], key[i]) for i in two]
    backward = [dot(pairs[i], jnp.concatenate([query[i], key[i]], axis=0), 0, 0) for i in two]
    by_state = [
        dot(jnp.concatenate([grad[i], -value_grad[i]], axis=0), state[i], 1, 1, passes=1)
        for i in two
    ]
    by_end = [dot(updates[i], end[i], 1, 1, passes=1) for i in two]
    for i in two:
        start = i * PAIRS
        dv_ref[:, start : start + WIDTH] = value_grad[i][:WIDTH].astype(BF16)
        dv_ref[:, start + WIDTH : start + PAIRS] = value_grad[i][WIDTH:].astype(BF16)
        slope = jnp.sum(pulled[i] * updates[i], axis=1, keepdims=True) / (1.0 + jnp.exp(logit[i]))
        dlogit_ref[pl.ds(first + i, 1), :] = row_of(slope)
        query_grad = forward[i][:WIDTH] + by_state[i][:WIDTH]
        query_grad = query_scale[i] * (
            query_grad - query[i] * jnp.sum(query[i] * query_grad, axis=1, keepdims=True)
        )
        dq_ref[:, i * WIDTH : (i + 1) * WIDTH] = query_grad.astype(BF16)
        key_grad = forward[i][WIDTH:] + backward[i] + by_end[i] + by_state[i][WIDTH:]
        key_grad = key_scale[i] * (
            key_grad - key[i] * jnp.sum(key[i] * key_grad, axis=1, keepdims=True)
        )
        dk_ref[:, start : start + WIDTH] = key_grad[:WIDTH].astype(BF16)
        dk_ref[:, start + WIDTH : start + PAIRS] = key_grad[WIDTH:].astype(BF16)


def pull(place, queries, keys, logits, reads, wy, state, end, head_grad):
    return call(
        pull_kernel,
        2,
        [
            by_columns(WIDTH),
            by_columns(PAIRS),
            whole(4, PAIRS),
            by_pair(PAIRS, PAIRS),
            by_pair(PAIRS, PAIRS),
            by_slot(WIDTH, WIDTH),
            by_slot(WIDTH, WIDTH),
            by_columns(WIDTH),
        ],
        [by_columns(WIDTH), by_columns(PAIRS), by_columns(PAIRS), whole(4, PAIRS)],
        [
            arr(BF16, WIDTH, 512),
            arr(BF16, WIDTH, 1024),
            arr(BF16, WIDTH, 1024),
            arr(F32, 4, PAIRS),
        ],
        4 * 14 * 2 * PAIRS**3,
        5 << 20,
    )(place, queries, keys, logits, reads, wy, state, end, head_grad)


def mul(a, b):
    return jnp.einsum("hij,hjk->hik", a, b, preferred_element_type=F32)


def mul_t(a, b):
    return jnp.einsum("hji,hjk->hik", a, b, preferred_element_type=F32)


def halves(x):
    return x[:, :, :WIDTH], x[:, :, WIDTH:]


def forward_states(place, mine, theirs, index, core, grad_full, weight):
    theirs = exchange(theirs, 1)
    even = jnp.where(core == 0, mine, theirs)
    odd = jnp.where(core == 0, theirs, mine)
    even_a, even_b = halves(even)
    odd_a, odd_b = halves(odd)
    joined = mul(odd_a, even)
    chip = jnp.concatenate(
        [joined[:, :, :WIDTH], joined[:, :, WIDTH:] + odd_b.astype(F32)], axis=2
    ).astype(BF16)
    total, levels = chip, []
    diagonal = jnp.broadcast_to(jnp.eye(WIDTH, dtype=BF16), (2, WIDTH, WIDTH))
    for bit in (2, 4, 8):
        came = exchange(total, bit)
        if bit == 8:
            grad_other, came = lax.optimization_barrier((exchange(grad_full, 1), came))
        upper = (index & bit) != 0
        left, right = jnp.where(upper, came, total), jnp.where(upper, total, came)
        right_a, right_b = halves(right)
        step = mul(right_a, left)
        total = jnp.concatenate(
            [step[:, :, :WIDTH], step[:, :, WIDTH:] + right_b.astype(F32)], axis=2
        ).astype(BF16)
        came_a, came_b = halves(came)
        if not levels:
            levels.append((bit, left[:, :, :WIDTH], None))
            before, state = jnp.where(upper, came_a, diagonal), jnp.where(upper, came_b, 0.0)
            state = state.astype(F32)
            after = jnp.where(upper, diagonal, came_a)
        else:
            levels.append((bit, left[:, :, :WIDTH], after))
            step = mul(before, came)
            before = jnp.where(upper, step[:, :, :WIDTH].astype(BF16), before)
            state = jnp.where(upper, state + step[:, :, WIDTH:], state)
            after = jnp.where(upper, after, mul(came_a, after).astype(BF16))
    weight, total = lax.optimization_barrier((weight, total))
    far = send(total[:, :, WIDTH:], 16)
    kept_grad, given_grad = head_gradient(place, grad_full, grad_other, weight)
    kept_grad, given_grad, far = lax.optimization_barrier((kept_grad, given_grad, far))
    head_grad = (kept_grad, exchange(given_grad, 1))
    first = (state + mul(before, far)).astype(BF16)
    second = (mul(even_a, first) + even_b.astype(F32)).astype(BF16)
    kept = jnp.where(core == 0, first, second)
    given = jnp.where(core == 0, second, first)
    state_in = jnp.concatenate([kept, exchange(given, 1)], axis=0)
    return grad_full, grad_other, head_grad, state_in, (even_a, odd_a, levels, after)


def backward_states(mine, theirs, index, core, saved, gate):
    even_a, odd_a, levels, after = saved
    theirs = exchange(theirs, 1)
    even = jnp.where(core == 0, mine, theirs)
    odd = jnp.where(core == 0, theirs, mine)
    total = (even.astype(F32) + mul_t(even_a, odd)).astype(BF16)
    for bit, left_a, window in levels:
        came = exchange(total, bit)
        upper = (index & bit) != 0
        if window is None:
            gate, came = lax.optimization_barrier((gate, came))
            second = jnp.where(upper, 0.0, came.astype(F32))
        else:
            second = jnp.where(upper, second, second + mul_t(window, came))
        left, right = jnp.where(upper, came, total), jnp.where(upper, total, came)
        total = (left.astype(F32) + mul_t(left_a, right)).astype(BF16)
    second = second + mul_t(after, send(total, -16))
    second = second.astype(BF16)
    first = (odd.astype(F32) + mul_t(odd_a, second)).astype(BF16)
    kept = jnp.where(core == 0, first, second)
    given = jnp.where(core == 0, second, first)
    return gate, jnp.concatenate([kept, exchange(given, 1)], axis=0)


def local(queries, keys, values, beta_logit, out_weight, out_grad):
    index = lax.axis_index("ctx")
    core = index & 1
    place = jnp.stack([core, index >> 4]).astype(jnp.int32)
    rings = [[(half * 8 + z) * 2 + c for z in range(8)] for half in range(2) for c in range(2)]
    operands = (queries, keys, values, beta_logit)
    across = exchange(out_weight, 16)
    theirs, *filled = prepare(place, *operands, False)
    across, theirs = lax.optimization_barrier((across, theirs))
    weight_pair = jnp.stack([out_weight, across])
    weight_pair, *operands = lax.optimization_barrier((weight_pair, *operands))
    mine, reads, wy, qt, local_out = prepare(place, *operands, True, filled)
    weight_mine = lax.all_gather(weight_pair, "ctx", axis=0, axis_index_groups=rings)
    grad_full = lax.all_to_all(
        jnp.broadcast_to(out_grad[None], (8, WIDTH, 512)), "tp", 0, 0, tiled=True
    )
    grad_full, grad_other, head_grad, state, saved = forward_states(
        place, mine, theirs, index, core, grad_full, weight_mine
    )
    heads = head_outputs(place, qt, local_out, state)
    heads_other = exchange(heads, 1)
    terms = weight_terms(place, grad_full, grad_other, heads, heads_other)
    ring_sum = lax.psum_scatter(
        terms, "ctx", scatter_dimension=0, axis_index_groups=rings
    ).reshape(2, WIDTH, 512)
    head_grad, own, own_theirs = own_cotangent(place, *head_grad, qt)
    parts = mixed_parts(place, heads, heads_other, weight_mine)
    parts, end = backward_states(own, own_theirs, index, core, saved, parts)
    end, ring_sum = lax.optimization_barrier((end, ring_sum))
    weight_grad = ring_sum[0].astype(F32) + exchange(ring_sum[1], 16).astype(F32)
    parts = lax.all_to_all(parts, "tp", 0, 0, tiled=True)
    sums = jnp.sum(parts.astype(F32), axis=0).astype(BF16)
    kept, came = sums[:WIDTH], exchange(sums[WIDTH:], 1)
    first, second = jnp.where(core == 0, kept, came), jnp.where(core == 0, came, kept)
    mixed = jnp.concatenate(
        [first[:, :WIDTH], second[:, :WIDTH], first[:, WIDTH:], second[:, WIDTH:]], axis=1
    )
    query_grad, key_grad, value_grad, logit_grad = pull(
        place, queries, keys, beta_logit, reads, wy, state, end, head_grad
    )
    return mixed, query_grad, key_grad, value_grad, logit_grad, weight_grad


def solution(mesh):
    placed = P("ctx", "tp")
    return jax.shard_map(
        local,
        mesh=mesh,
        in_specs=(placed, placed, placed, P("tp", "ctx"), placed, placed),
        out_specs=(placed, placed, placed, placed, P("tp", "ctx"), placed),
        check_vma=False,
    )
```

```python
import functools
import math

import jax
import jax.numpy as jnp
from jax import lax
from jax.experimental import pallas as pl
from jax.experimental.pallas import tpu as pltpu
from jax.sharding import PartitionSpec as P

F32 = jnp.float32
BF16 = jnp.bfloat16
WIDTH = 128
VMEM = 62 << 20
PAIRS = 2 * WIDTH


def send(block, distance):
    devices = range(lax.axis_size("ctx"))
    route = [(i - distance, i) for i in devices if i - distance in devices]
    return lax.ppermute(block, "ctx", route)


def exchange(block, bit):
    route = [(i, i ^ bit) for i in range(lax.axis_size("ctx"))]
    return lax.ppermute(block, "ctx", route)


def split(x):
    high = x.astype(BF16)
    return high, (x - high.astype(F32)).astype(BF16)


def dot(a, b, ca=1, cb=0, passes=3):
    dims = (((ca,), (cb,)), ((), ()))
    mul = functools.partial(lax.dot_general, dimension_numbers=dims, preferred_element_type=F32)
    if passes == 1:
        return mul(a.astype(BF16), b.astype(BF16))
    if b.dtype == BF16:
        a_high, a_low = split(a)
        return mul(a_high, b) + mul(a_low, b)
    a_high, a_low = split(a)
    b_high, b_low = split(b)
    return mul(a_high, b_high) + (mul(a_low, b_high) + mul(a_high, b_low))


def inverse_norm(x):
    return lax.rsqrt(jnp.sum(x * x, axis=-1, keepdims=True) + 1e-06)


def order_of(shape, dim):
    p = lax.broadcasted_iota(jnp.int32, shape, dim)
    return 2 * (p & (WIDTH - 1)) + (p >> 7)


def column_of(row):
    shape = (PAIRS, PAIRS)
    time = lax.broadcasted_iota(jnp.int32, shape, 1)
    return jnp.sum(jnp.where(time == order_of(shape, 0), row, 0.0), axis=1, keepdims=True)


def row_of(column):
    shape = (PAIRS, PAIRS)
    time = lax.broadcasted_iota(jnp.int32, shape, 1)
    return jnp.sum(jnp.where(time == order_of(shape, 0), column, 0.0), axis=0, keepdims=True)


def visible_mask():
    shape = (WIDTH, PAIRS)
    token = lax.broadcasted_iota(jnp.int32, shape, 0)
    return (lax.broadcasted_iota(jnp.int32, shape, 1) & (WIDTH - 1)) <= token


def stacked(ref, i):
    start = i * PAIRS
    parts = [ref[:, start : start + WIDTH], ref[:, start + WIDTH : start + PAIRS]]
    return jnp.concatenate(parts, axis=0).astype(F32)


def prepare_kernel(mine, *refs):
    place, q_ref, k_ref, v_ref, logit_ref = refs[:5]
    first = 2 * (place[0] if mine else 1 - place[0])
    ab_ref, m_ref, wy_ref, qt_ref, local_ref = refs[-5:]
    two = range(2)
    shape = (PAIRS, PAIRS)
    row, col = order_of(shape, 0), order_of(shape, 1)
    identity = jnp.where(row == col, 1.0, 0.0).astype(F32)
    query = [q_ref[:, i * WIDTH : (i + 1) * WIDTH].astype(F32) for i in two]
    query = [x * inverse_norm(x) for x in query]
    key = [stacked(k_ref, i) for i in two]
    key = [x * inverse_norm(x) for x in key]
    strength = [2.0 / (1.0 + jnp.exp(-column_of(logit_ref[pl.ds(first + i, 1), :]))) for i in two]
    coupling = [jnp.where(col < row, strength[i] * dot(key[i], key[i], 1, 1), 0.0) for i in two]
    inverse = [identity - jnp.where((row >> 1) == (col >> 1), coupling[i], 0.0) for i in two]
    for level in range(1, 8):
        join = ((row >> (level + 1)) == (col >> (level + 1))) & ((row >> level) != (col >> level))
        edge = [jnp.where(join, coupling[i], 0.0) for i in two]
        step = [dot(inverse[i], edge[i], passes=1) for i in two]
        inverse = [inverse[i] - dot(step[i], inverse[i], passes=1) for i in two]
    rest = [identity - inverse[i] - dot(coupling[i], inverse[i]) for i in two]
    inverse = [inverse[i] + dot(inverse[i], rest[i], passes=1) for i in two]
    scores = [jnp.where(visible_mask(), dot(query[i], key[i], 1, 1), 0.0) for i in two]
    scaled = [strength[i] * jnp.concatenate([key[i], stacked(v_ref, i)], axis=1) for i in two]
    reads = [
        jnp.concatenate([dot(scores[i], inverse[i]), dot(key[i], inverse[i], 0, 0)], axis=0)
        for i in two
    ]
    product = [dot(reads[i], scaled[i]) for i in two]
    eye = identity[:WIDTH, :WIDTH]
    for i in two:
        ab_ref[i, :, :WIDTH] = (eye - product[i][WIDTH:, :WIDTH]).astype(BF16)
        ab_ref[i, :, WIDTH:] = product[i][WIDTH:, WIDTH:].astype(BF16)
        qt_ref[i] = query[i] - product[i][:WIDTH, :WIDTH]
        local_ref[i] = product[i][:WIDTH, WIDTH:]
        m_ref[i] = reads[i]
        wy_ref[i] = dot(inverse[i], scaled[i])


def slot(head, place):
    return (head + 2 * place[0]) % 4


def by_pair(*block):
    return pl.BlockSpec((2,) + block, lambda i, place: (i,) + (0,) * len(block))


def by_slot(*block):
    return pl.BlockSpec((2,) + block, lambda i, place: (i ^ place[0],) + (0,) * len(block))


def by_columns(width):
    return pl.BlockSpec((WIDTH, 2 * width), lambda i, place: (0, i))


def whole(*shape):
    return pl.BlockSpec(shape, lambda i, place: (0,) * len(shape))


def call(kernel, steps, in_specs, out_specs, out_shape, flops, moved, scratch=()):
    return pl.pallas_call(
        kernel,
        grid_spec=pltpu.PrefetchScalarGridSpec(
            num_scalar_prefetch=1,
            grid=(steps,),
            in_specs=in_specs,
            out_specs=out_specs,
            scratch_shapes=list(scratch),
        ),
        out_shape=out_shape,
        compiler_params=pltpu.CompilerParams(vmem_limit_bytes=VMEM),
        cost_estimate=pl.CostEstimate(flops=flops, bytes_accessed=moved, transcendentals=0),
    )


def arr(dtype, *shape):
    return jax.ShapeDtypeStruct(shape, dtype)


def prepare(place, queries, keys, values, logits, mine, filled=()):
    def pair(place):
        return place[0] if mine else 1 - place[0]

    def columns(width):
        return pl.BlockSpec((WIDTH, 2 * width), lambda i, place: (0, pair(place)))

    def heads(*block):
        return pl.BlockSpec((2,) + block, lambda i, place: (pair(place),) + (0,) * len(block))

    def stored(n):
        return arr(F32, 4, n, n)

    return pl.pallas_call(
        functools.partial(prepare_kernel, mine),
        grid_spec=pltpu.PrefetchScalarGridSpec(
            num_scalar_prefetch=1,
            grid=(1,),
            in_specs=[
                columns(WIDTH),
                columns(PAIRS),
                columns(PAIRS),
                whole(4, PAIRS),
            ]
            + [pl.BlockSpec(memory_space=pl.ANY)] * len(filled),
            out_specs=[
                pl.BlockSpec((2, WIDTH, PAIRS), lambda i, place: (0, 0, 0)),
                heads(PAIRS, PAIRS),
                heads(PAIRS, PAIRS),
                heads(WIDTH, WIDTH),
                heads(WIDTH, WIDTH),
            ],
        ),
        out_shape=[
            arr(BF16, 2, WIDTH, PAIRS),
            stored(PAIRS),
            stored(PAIRS),
            stored(WIDTH),
            stored(WIDTH),
        ],
        input_output_aliases={5 + i: 1 + i for i in range(len(filled))},
        compiler_params=pltpu.CompilerParams(vmem_limit_bytes=VMEM),
        cost_estimate=pl.CostEstimate(
            flops=(1 if mine else 100) << 20, bytes_accessed=1 << (16 if mine else 24), transcendentals=0
        ),
    )(place, queries, keys, values, logits, *filled)


STEPS = 4
BLOCKS = [(z, row) for z in range(2) for row in range(2)]


def grad_rows(place, refs):
    def block(ref, z):
        return ref[0, :, pl.ds(pl.multiple_of(z * 256 + place[0] * 128, 128), 128)]

    rows = [
        jnp.concatenate([block(refs[2 * core + row], z) for z, row in BLOCKS], axis=1)
        for core in range(2)
    ]
    return jnp.concatenate(rows, axis=0)


def grad_specs():
    def tile(row):
        return pl.BlockSpec(
            (1, WIDTH, 512), lambda step, place: ((row ^ place[1]) * 4 + step, 0, 0)
        )

    return [tile(0), tile(1), tile(0), tile(1)]


def weight_rows(ref):
    return jnp.concatenate([ref[z, row] for z, row in BLOCKS], axis=0)


def weight_tile():
    return pl.BlockSpec((2, 2, WIDTH, 512), lambda step, place: (step, 0, 0, 0))


def heads_kernel(
    place, qt_ref, local_ref, state_ref, kept_ref, came_ref,
    heads_ref, grad_ref, mine_ref, theirs_ref,
):
    grad_ref[...] = kept_ref[...] + came_ref[...]
    for head in range(4):
        columns = slice(head * WIDTH, (head + 1) * WIDTH)
        result = dot(qt_ref[head], state_ref[slot(head, place)]) + local_ref[head]
        heads_ref[:, columns] = result.astype(BF16)
        own = dot(qt_ref[head], grad_ref[:, columns], 0, 0, passes=1).astype(BF16)

        @pl.when(place[0] == head // 2)
        def _():
            mine_ref[head % 2] = own

        @pl.when(place[0] != head // 2)
        def _():
            theirs_ref[head % 2] = own


def head_outputs(place, qt, local, state, kept, came):
    square, pair = whole(4, WIDTH, WIDTH), arr(BF16, 2, WIDTH, WIDTH)
    return call(
        heads_kernel,
        1,
        [square, square, square, whole(WIDTH, 512), whole(WIDTH, 512)],
        [whole(WIDTH, 512), whole(WIDTH, 512), whole(2, WIDTH, WIDTH), whole(2, WIDTH, WIDTH)],
        [arr(BF16, WIDTH, 512), arr(F32, WIDTH, 512), pair, pair],
        2 * 8 * 128**3,
        2 << 20,
    )(place, qt, local, state, kept, came)


def weight_terms_kernel(place, *refs):
    heads_ref, heads_other_ref, out_ref = refs[4:]
    product = lax.dot_general(
        grad_rows(place, refs[:4]),
        jnp.concatenate([heads_ref[...], heads_other_ref[...]], axis=0),
        (((0,), (0,)), ((), ())),
        preferred_element_type=F32,
    )
    product = (product * (1.0 / 64.0)).astype(BF16)
    for z in range(2):
        out_ref[z] = product[z * 256 : z * 256 + 256]


def weight_terms(place, grad_full, grad_other, heads, heads_other):
    return call(
        weight_terms_kernel,
        STEPS,
        grad_specs() + [whole(WIDTH, 512), whole(WIDTH, 512)],
        pl.BlockSpec((2, 256, 512), lambda step, place: (step, 0, 0)),
        arr(BF16, 8, 256, 512),
        2 * 128 * 512 * 4096,
        5 << 20,
    )(place, grad_full, grad_full, grad_other, grad_other, heads, heads_other)


def mixed_kernel(place, heads_ref, heads_other_ref, weight_ref, out_ref):
    step = pl.program_id(0)
    product = lax.dot_general(
        jnp.concatenate([heads_ref[...], heads_other_ref[...]], axis=0),
        weight_rows(weight_ref),
        (((1,), (1,)), ((), ())),
        preferred_element_type=F32,
    ).astype(BF16)
    for i, (z, row) in enumerate(BLOCKS):
        owner = (row ^ place[1]) * 4 + step
        out_ref[owner, :, z * 128 : z * 128 + 128] = product[:, i * WIDTH : (i + 1) * WIDTH]


def mixed_parts(place, heads, heads_other, weight):
    return call(
        mixed_kernel,
        STEPS,
        [whole(WIDTH, 512), whole(WIDTH, 512), weight_tile()],
        whole(8, 256, 256),
        arr(BF16, 8, 256, 256),
        2 * 128 * 512 * 4096,
        3 << 20,
    )(place, heads, heads_other, weight)


def head_grad_kernel(place, *refs):
    step = pl.program_id(0)
    weight_ref, kept_ref, given_ref = refs[4:]
    total = jnp.dot(
        grad_rows(place, refs[:4]),
        weight_rows(weight_ref),
        preferred_element_type=F32,
    )

    @pl.when(step == 0)
    def _():
        kept_ref[...] = total[:WIDTH]
        given_ref[...] = total[WIDTH:]

    @pl.when(step > 0)
    def _():
        kept_ref[...] += total[:WIDTH]
        given_ref[...] += total[WIDTH:]


def head_gradient(place, grad_full, grad_other, weight):
    part = arr(F32, WIDTH, 512)
    return call(
        head_grad_kernel,
        STEPS,
        grad_specs() + [weight_tile()],
        [whole(WIDTH, 512), whole(WIDTH, 512)],
        [part, part],
        2 * 128 * 512 * 4096,
        5 << 20,
    )(place, grad_full, grad_full, grad_other, grad_other, weight)


def pull_kernel(
    place, q_ref, k_ref, logit_ref, m_ref, wy_ref, state_ref, end_ref, grad_ref,
    dq_ref, dk_ref, dv_ref, dlogit_ref,
):
    two = range(2)
    shape = (PAIRS, PAIRS)
    before = order_of(shape, 1) < order_of(shape, 0)
    query = [q_ref[:, i * WIDTH : (i + 1) * WIDTH].astype(F32) for i in two]
    query_scale = [inverse_norm(x) for x in query]
    query = [query[i] * query_scale[i] for i in two]
    key = [stacked(k_ref, i) for i in two]
    key_scale = [inverse_norm(x) for x in key]
    key = [key[i] * key_scale[i] for i in two]
    first = 2 * pl.program_id(0)
    logit = [column_of(logit_ref[pl.ds(first + i, 1), :]) for i in two]
    state = [state_ref[i] for i in two]
    end = [end_ref[i] for i in two]
    grad = [grad_ref[:, i * WIDTH : (i + 1) * WIDTH] for i in two]
    updates = [wy_ref[i, :, WIDTH:] - dot(wy_ref[i, :, :WIDTH], state[i]) for i in two]
    pulled = [dot(m_ref[i], jnp.concatenate([grad[i], end[i].astype(F32)], axis=0), 0, 0) for i in two]
    value_grad = [2.0 / (1.0 + jnp.exp(-logit[i])) * pulled[i] for i in two]
    cross = [
        dot(jnp.concatenate([grad[i], value_grad[i]], axis=0), updates[i], 1, 1) for i in two
    ]
    pairs = [
        jnp.concatenate(
            [
                jnp.where(visible_mask(), cross[i][:WIDTH], 0.0),
                jnp.where(before, -cross[i][WIDTH:], 0.0),
            ],
            axis=0,
        )
        for i in two
    ]
    forward = [dot(pairs[i], key[i]) for i in two]
    backward = [dot(pairs[i], jnp.concatenate([query[i], key[i]], axis=0), 0, 0) for i in two]
    by_state = [
        dot(jnp.concatenate([grad[i], -value_grad[i]], axis=0), state[i], 1, 1, passes=1)
        for i in two
    ]
    by_end = [dot(updates[i], end[i], 1, 1, passes=1) for i in two]
    for i in two:
        start = i * PAIRS
        dv_ref[:, start : start + WIDTH] = value_grad[i][:WIDTH].astype(BF16)
        dv_ref[:, start + WIDTH : start + PAIRS] = value_grad[i][WIDTH:].astype(BF16)
        slope = jnp.sum(pulled[i] * updates[i], axis=1, keepdims=True) / (1.0 + jnp.exp(logit[i]))
        dlogit_ref[pl.ds(first + i, 1), :] = row_of(slope)
        query_grad = forward[i][:WIDTH] + by_state[i][:WIDTH]
        query_grad = query_scale[i] * (
            query_grad - query[i] * jnp.sum(query[i] * query_grad, axis=1, keepdims=True)
        )
        dq_ref[:, i * WIDTH : (i + 1) * WIDTH] = query_grad.astype(BF16)
        key_grad = forward[i][WIDTH:] + backward[i] + by_end[i] + by_state[i][WIDTH:]
        key_grad = key_scale[i] * (
            key_grad - key[i] * jnp.sum(key[i] * key_grad, axis=1, keepdims=True)
        )
        dk_ref[:, start : start + WIDTH] = key_grad[:WIDTH].astype(BF16)
        dk_ref[:, start + WIDTH : start + PAIRS] = key_grad[WIDTH:].astype(BF16)


def pull(place, queries, keys, logits, reads, wy, state, end, head_grad):
    return call(
        pull_kernel,
        2,
        [
            by_columns(WIDTH),
            by_columns(PAIRS),
            whole(4, PAIRS),
            by_pair(PAIRS, PAIRS),
            by_pair(PAIRS, PAIRS),
            by_slot(WIDTH, WIDTH),
            by_slot(WIDTH, WIDTH),
            by_columns(WIDTH),
        ],
        [by_columns(WIDTH), by_columns(PAIRS), by_columns(PAIRS), whole(4, PAIRS)],
        [
            arr(BF16, WIDTH, 512),
            arr(BF16, WIDTH, 1024),
            arr(BF16, WIDTH, 1024),
            arr(F32, 4, PAIRS),
        ],
        4 * 14 * 2 * PAIRS**3,
        5 << 20,
    )(place, queries, keys, logits, reads, wy, state, end, head_grad)


def mul(a, b):
    return jnp.einsum("hij,hjk->hik", a, b, preferred_element_type=F32)


def mul_t(a, b):
    return jnp.einsum("hji,hjk->hik", a, b, preferred_element_type=F32)


def halves(x):
    return x[:, :, :WIDTH], x[:, :, WIDTH:]


def forward_states(place, mine, theirs, index, core, grad_full, weight):
    theirs = exchange(theirs, 1)
    even = jnp.where(core == 0, mine, theirs)
    odd = jnp.where(core == 0, theirs, mine)
    even_a, even_b = halves(even)
    odd_a, odd_b = halves(odd)
    joined = mul(odd_a, even)
    chip = jnp.concatenate(
        [joined[:, :, :WIDTH], joined[:, :, WIDTH:] + odd_b.astype(F32)], axis=2
    ).astype(BF16)
    total, levels = chip, []
    diagonal = jnp.broadcast_to(jnp.eye(WIDTH, dtype=BF16), (2, WIDTH, WIDTH))
    for bit in (2, 4, 8):
        came = exchange(total, bit)
        if bit == 8:
            grad_other, came = lax.optimization_barrier((exchange(grad_full, 1), came))
        upper = (index & bit) != 0
        left, right = jnp.where(upper, came, total), jnp.where(upper, total, came)
        right_a, right_b = halves(right)
        step = mul(right_a, left)
        total = jnp.concatenate(
            [step[:, :, :WIDTH], step[:, :, WIDTH:] + right_b.astype(F32)], axis=2
        ).astype(BF16)
        came_a, came_b = halves(came)
        if not levels:
            levels.append((bit, left[:, :, :WIDTH], None))
            before, state = jnp.where(upper, came_a, diagonal), jnp.where(upper, came_b, 0.0)
            state = state.astype(F32)
            after = jnp.where(upper, diagonal, came_a)
        else:
            levels.append((bit, left[:, :, :WIDTH], after))
            step = mul(before, came)
            before = jnp.where(upper, step[:, :, :WIDTH].astype(BF16), before)
            state = jnp.where(upper, state + step[:, :, WIDTH:], state)
            after = jnp.where(upper, after, mul(came_a, after).astype(BF16))
    weight, total = lax.optimization_barrier((weight, total))
    far = send(total[:, :, WIDTH:], 16)
    kept_grad, given_grad = head_gradient(place, grad_full, grad_other, weight)
    kept_grad, given_grad, far = lax.optimization_barrier((kept_grad, given_grad, far))
    head_grad = (kept_grad, exchange(given_grad, 1))
    first = (state + mul(before, far)).astype(BF16)
    second = (mul(even_a, first) + even_b.astype(F32)).astype(BF16)
    kept = jnp.where(core == 0, first, second)
    given = jnp.where(core == 0, second, first)
    state_in = jnp.concatenate([kept, exchange(given, 1)], axis=0)
    return grad_full, grad_other, head_grad, state_in, (even_a, odd_a, levels, after)


def backward_states(mine, theirs, index, core, saved, gate, last):
    even_a, odd_a, levels, after = saved
    theirs = exchange(theirs, 1)
    even = jnp.where(core == 0, mine, theirs)
    odd = jnp.where(core == 0, theirs, mine)
    total = (even.astype(F32) + mul_t(even_a, odd)).astype(BF16)
    for bit, left_a, window in levels:
        came = exchange(total, bit)
        upper = (index & bit) != 0
        if window is None:
            gate, came = lax.optimization_barrier((gate, came))
            second = jnp.where(upper, 0.0, came.astype(F32))
        else:
            second = jnp.where(upper, second, second + mul_t(window, came))
        left, right = jnp.where(upper, came, total), jnp.where(upper, total, came)
        total = (left.astype(F32) + mul_t(left_a, right)).astype(BF16)
    second = second + mul_t(after, send(total, -16))
    second = second.astype(BF16)
    first = (odd.astype(F32) + mul_t(odd_a, second)).astype(BF16)
    kept = jnp.where(core == 0, first, second)
    given = jnp.where(core == 0, second, first)
    last, given = lax.optimization_barrier((last, given))
    return gate, last, jnp.concatenate([kept, exchange(given, 1)], axis=0)


def local(queries, keys, values, beta_logit, out_weight, out_grad):
    index = lax.axis_index("ctx")
    core = index & 1
    place = jnp.stack([core, index >> 4]).astype(jnp.int32)
    rings = [[(half * 8 + z) * 2 + c for z in range(8)] for half in range(2) for c in range(2)]
    operands = (queries, keys, values, beta_logit)
    across = exchange(out_weight, 16)
    theirs, *filled = prepare(place, *operands, False)
    across, theirs = lax.optimization_barrier((across, theirs))
    weight_pair = jnp.stack([out_weight, across])
    weight_pair, *operands = lax.optimization_barrier((weight_pair, *operands))
    mine, reads, wy, qt, local_out = prepare(place, *operands, True, filled)
    weight_mine = lax.all_gather(weight_pair, "ctx", axis=0, axis_index_groups=rings)
    grad_full = lax.all_to_all(
        jnp.broadcast_to(out_grad[None], (8, WIDTH, 512)), "tp", 0, 0, tiled=True
    )
    grad_full, grad_other, head_grad, state, saved = forward_states(
        place, mine, theirs, index, core, grad_full, weight_mine
    )
    heads, head_grad, own, own_theirs = head_outputs(place, qt, local_out, state, *head_grad)
    heads_other = exchange(heads, 1)
    terms = weight_terms(place, grad_full, grad_other, heads, heads_other)
    ring_sum = lax.psum_scatter(
        terms, "ctx", scatter_dimension=0, axis_index_groups=rings
    ).reshape(2, WIDTH, 512)
    parts = mixed_parts(place, heads, heads_other, weight_mine)
    parts, ring_sum, end = backward_states(own, own_theirs, index, core, saved, parts, ring_sum)
    weight_grad = ring_sum[0].astype(F32) + exchange(ring_sum[1], 16).astype(F32)
    parts = lax.all_to_all(parts, "tp", 0, 0, tiled=True)
    sums = jnp.sum(parts.astype(F32), axis=0).astype(BF16)
    kept, came = sums[:WIDTH], exchange(sums[WIDTH:], 1)
    first, second = jnp.where(core == 0, kept, came), jnp.where(core == 0, came, kept)
    mixed = jnp.concatenate(
        [first[:, :WIDTH], second[:, :WIDTH], first[:, WIDTH:], second[:, WIDTH:]], axis=1
    )
    query_grad, key_grad, value_grad, logit_grad = pull(
        place, queries, keys, beta_logit, reads, wy, state, end, head_grad
    )
    return mixed, query_grad, key_grad, value_grad, logit_grad, weight_grad


def solution(mesh):
    placed = P("ctx", "tp")
    return jax.shard_map(
        local,
        mesh=mesh,
        in_specs=(placed, placed, placed, P("tp", "ctx"), placed, placed),
        out_specs=(placed, placed, placed, placed, P("tp", "ctx"), placed),
        check_vma=False,
    )
```

```python
import functools
import math

import jax
import jax.numpy as jnp
from jax import lax
from jax.experimental import pallas as pl
from jax.experimental.pallas import tpu as pltpu
from jax.sharding import PartitionSpec as P

F32 = jnp.float32
BF16 = jnp.bfloat16
WIDTH = 128
VMEM = 62 << 20
PAIRS = 2 * WIDTH


def send(block, distance):
    devices = range(lax.axis_size("ctx"))
    route = [(i - distance, i) for i in devices if i - distance in devices]
    return lax.ppermute(block, "ctx", route)


def exchange(block, bit):
    route = [(i, i ^ bit) for i in range(lax.axis_size("ctx"))]
    return lax.ppermute(block, "ctx", route)


def split(x):
    high = x.astype(BF16)
    return high, (x - high.astype(F32)).astype(BF16)


def dot(a, b, ca=1, cb=0, passes=3):
    dims = (((ca,), (cb,)), ((), ()))
    mul = functools.partial(lax.dot_general, dimension_numbers=dims, preferred_element_type=F32)
    if passes == 1:
        return mul(a.astype(BF16), b.astype(BF16))
    if b.dtype == BF16:
        a_high, a_low = split(a)
        return mul(a_high, b) + mul(a_low, b)
    a_high, a_low = split(a)
    b_high, b_low = split(b)
    return mul(a_high, b_high) + (mul(a_low, b_high) + mul(a_high, b_low))


def inverse_norm(x):
    return lax.rsqrt(jnp.sum(x * x, axis=-1, keepdims=True) + 1e-06)


def order_of(shape, dim):
    p = lax.broadcasted_iota(jnp.int32, shape, dim)
    return 2 * (p & (WIDTH - 1)) + (p >> 7)


def column_of(row):
    shape = (PAIRS, PAIRS)
    time = lax.broadcasted_iota(jnp.int32, shape, 1)
    return jnp.sum(jnp.where(time == order_of(shape, 0), row, 0.0), axis=1, keepdims=True)


def row_of(column):
    shape = (PAIRS, PAIRS)
    time = lax.broadcasted_iota(jnp.int32, shape, 1)
    return jnp.sum(jnp.where(time == order_of(shape, 0), column, 0.0), axis=0, keepdims=True)


def visible_mask():
    shape = (WIDTH, PAIRS)
    token = lax.broadcasted_iota(jnp.int32, shape, 0)
    return (lax.broadcasted_iota(jnp.int32, shape, 1) & (WIDTH - 1)) <= token


def stacked(ref, i):
    start = i * PAIRS
    parts = [ref[:, start : start + WIDTH], ref[:, start + WIDTH : start + PAIRS]]
    return jnp.concatenate(parts, axis=0).astype(F32)


def prepare_kernel(mine, *refs):
    place, q_ref, k_ref, v_ref, logit_ref = refs[:5]
    first = 2 * (place[0] if mine else 1 - place[0])
    ab_ref, m_ref, wy_ref, qt_ref, local_ref = refs[-5:]
    two = range(2)
    shape = (PAIRS, PAIRS)
    row, col = order_of(shape, 0), order_of(shape, 1)
    identity = jnp.where(row == col, 1.0, 0.0).astype(F32)
    query = [q_ref[:, i * WIDTH : (i + 1) * WIDTH].astype(F32) for i in two]
    query = [x * inverse_norm(x) for x in query]
    key = [stacked(k_ref, i) for i in two]
    key = [x * inverse_norm(x) for x in key]
    strength = [2.0 / (1.0 + jnp.exp(-column_of(logit_ref[pl.ds(first + i, 1), :]))) for i in two]
    coupling = [jnp.where(col < row, strength[i] * dot(key[i], key[i], 1, 1), 0.0) for i in two]
    inverse = [identity - jnp.where((row >> 1) == (col >> 1), coupling[i], 0.0) for i in two]
    for level in range(1, 8):
        join = ((row >> (level + 1)) == (col >> (level + 1))) & ((row >> level) != (col >> level))
        edge = [jnp.where(join, coupling[i], 0.0) for i in two]
        step = [dot(inverse[i], edge[i], passes=1) for i in two]
        inverse = [inverse[i] - dot(step[i], inverse[i], passes=1) for i in two]
    rest = [identity - inverse[i] - dot(coupling[i], inverse[i]) for i in two]
    inverse = [inverse[i] + dot(inverse[i], rest[i], passes=1) for i in two]
    scores = [jnp.where(visible_mask(), dot(query[i], key[i], 1, 1), 0.0) for i in two]
    scaled = [strength[i] * jnp.concatenate([key[i], stacked(v_ref, i)], axis=1) for i in two]
    reads = [
        jnp.concatenate([dot(scores[i], inverse[i]), dot(key[i], inverse[i], 0, 0)], axis=0)
        for i in two
    ]
    product = [dot(reads[i], scaled[i]) for i in two]
    eye = identity[:WIDTH, :WIDTH]
    for i in two:
        ab_ref[i, :, :WIDTH] = (eye - product[i][WIDTH:, :WIDTH]).astype(BF16)
        ab_ref[i, :, WIDTH:] = product[i][WIDTH:, WIDTH:].astype(BF16)
        qt_ref[i] = query[i] - product[i][:WIDTH, :WIDTH]
        local_ref[i] = product[i][:WIDTH, WIDTH:]
        m_ref[i] = reads[i]
        wy_ref[i] = dot(inverse[i], scaled[i])


def slot(head, place):
    return (head + 2 * place[0]) % 4


def by_pair(*block):
    return pl.BlockSpec((2,) + block, lambda i, place: (i,) + (0,) * len(block))


def by_slot(*block):
    return pl.BlockSpec((2,) + block, lambda i, place: (i ^ place[0],) + (0,) * len(block))


def by_columns(width):
    return pl.BlockSpec((WIDTH, 2 * width), lambda i, place: (0, i))


def whole(*shape):
    return pl.BlockSpec(shape, lambda i, place: (0,) * len(shape))


def call(kernel, steps, in_specs, out_specs, out_shape, flops, moved, scratch=()):
    return pl.pallas_call(
        kernel,
        grid_spec=pltpu.PrefetchScalarGridSpec(
            num_scalar_prefetch=1,
            grid=(steps,),
            in_specs=in_specs,
            out_specs=out_specs,
            scratch_shapes=list(scratch),
        ),
        out_shape=out_shape,
        compiler_params=pltpu.CompilerParams(vmem_limit_bytes=VMEM),
        cost_estimate=pl.CostEstimate(flops=flops, bytes_accessed=moved, transcendentals=0),
    )


def arr(dtype, *shape):
    return jax.ShapeDtypeStruct(shape, dtype)


def prepare(place, queries, keys, values, logits, mine, filled=()):
    def pair(place):
        return place[0] if mine else 1 - place[0]

    def columns(width):
        return pl.BlockSpec((WIDTH, 2 * width), lambda i, place: (0, pair(place)))

    def heads(*block):
        return pl.BlockSpec((2,) + block, lambda i, place: (pair(place),) + (0,) * len(block))

    def stored(n):
        return arr(F32, 4, n, n)

    return pl.pallas_call(
        functools.partial(prepare_kernel, mine),
        grid_spec=pltpu.PrefetchScalarGridSpec(
            num_scalar_prefetch=1,
            grid=(1,),
            in_specs=[
                columns(WIDTH),
                columns(PAIRS),
                columns(PAIRS),
                whole(4, PAIRS),
            ]
            + [pl.BlockSpec(memory_space=pl.ANY)] * len(filled),
            out_specs=[
                pl.BlockSpec((2, WIDTH, PAIRS), lambda i, place: (0, 0, 0)),
                heads(PAIRS, PAIRS),
                heads(PAIRS, PAIRS),
                heads(WIDTH, WIDTH),
                heads(WIDTH, WIDTH),
            ],
        ),
        out_shape=[
            arr(BF16, 2, WIDTH, PAIRS),
            stored(PAIRS),
            stored(PAIRS),
            stored(WIDTH),
            stored(WIDTH),
        ],
        input_output_aliases={5 + i: 1 + i for i in range(len(filled))},
        compiler_params=pltpu.CompilerParams(vmem_limit_bytes=VMEM),
        cost_estimate=pl.CostEstimate(
            flops=1 << 10, bytes_accessed=1 << 10, transcendentals=0
        ),
    )(place, queries, keys, values, logits, *filled)


STEPS = 4
BLOCKS = [(z, row) for z in range(2) for row in range(2)]


def grad_rows(place, refs):
    def block(ref, z):
        return ref[0, :, pl.ds(pl.multiple_of(z * 256 + place[0] * 128, 128), 128)]

    rows = [
        jnp.concatenate([block(refs[2 * core + row], z) for z, row in BLOCKS], axis=1)
        for core in range(2)
    ]
    return jnp.concatenate(rows, axis=0)


def grad_specs():
    def tile(row):
        return pl.BlockSpec(
            (1, WIDTH, 512), lambda step, place: ((row ^ place[1]) * 4 + step, 0, 0)
        )

    return [tile(0), tile(1), tile(0), tile(1)]


def weight_rows(refs):
    return jnp.concatenate([refs[row][z] for z, row in BLOCKS], axis=0)


def weight_tile():
    return pl.BlockSpec((2, WIDTH, 512), lambda step, place: (step, 0, 0))


def heads_kernel(
    place, qt_ref, local_ref, state_ref, kept_ref, came_ref,
    heads_ref, grad_ref, mine_ref, theirs_ref,
):
    grad_ref[...] = kept_ref[...] + came_ref[...]
    for head in range(4):
        columns = slice(head * WIDTH, (head + 1) * WIDTH)
        result = dot(qt_ref[head], state_ref[slot(head, place)]) + local_ref[head]
        heads_ref[:, columns] = result.astype(BF16)
        own = dot(qt_ref[head], grad_ref[:, columns], 0, 0, passes=1).astype(BF16)

        @pl.when(place[0] == head // 2)
        def _():
            mine_ref[head % 2] = own

        @pl.when(place[0] != head // 2)
        def _():
            theirs_ref[head % 2] = own


def head_outputs(place, qt, local, state, kept, came):
    square, pair = whole(4, WIDTH, WIDTH), arr(BF16, 2, WIDTH, WIDTH)
    return call(
        heads_kernel,
        1,
        [square, square, square, whole(WIDTH, 512), whole(WIDTH, 512)],
        [whole(WIDTH, 512), whole(WIDTH, 512), whole(2, WIDTH, WIDTH), whole(2, WIDTH, WIDTH)],
        [arr(BF16, WIDTH, 512), arr(F32, WIDTH, 512), pair, pair],
        2 * 8 * 128**3,
        2 << 20,
    )(place, qt, local, state, kept, came)


def weight_terms_kernel(place, *refs):
    heads_ref, heads_other_ref, out_ref = refs[4:]
    product = lax.dot_general(
        grad_rows(place, refs[:4]),
        jnp.concatenate([heads_ref[...], heads_other_ref[...]], axis=0),
        (((0,), (0,)), ((), ())),
        preferred_element_type=F32,
    )
    product = (product * (1.0 / 64.0)).astype(BF16)
    for z in range(2):
        out_ref[z] = product[z * 256 : z * 256 + 256]


def weight_terms(place, grad_full, grad_other, heads, heads_other):
    return call(
        weight_terms_kernel,
        STEPS,
        grad_specs() + [whole(WIDTH, 512), whole(WIDTH, 512)],
        pl.BlockSpec((2, 256, 512), lambda step, place: (step, 0, 0)),
        arr(BF16, 8, 256, 512),
        2 * 128 * 512 * 4096,
        5 << 20,
    )(place, grad_full, grad_full, grad_other, grad_other, heads, heads_other)


def mixed_kernel(place, heads_ref, heads_other_ref, weight_ref, across_ref, out_ref):
    step = pl.program_id(0)
    product = lax.dot_general(
        jnp.concatenate([heads_ref[...], heads_other_ref[...]], axis=0),
        weight_rows((weight_ref, across_ref)),
        (((1,), (1,)), ((), ())),
        preferred_element_type=F32,
    ).astype(BF16)
    for i, (z, row) in enumerate(BLOCKS):
        owner = (row ^ place[1]) * 4 + step
        out_ref[owner, :, z * 128 : z * 128 + 128] = product[:, i * WIDTH : (i + 1) * WIDTH]


def mixed_parts(place, heads, heads_other, weight, across):
    return call(
        mixed_kernel,
        STEPS,
        [whole(WIDTH, 512), whole(WIDTH, 512), weight_tile(), weight_tile()],
        whole(8, 256, 256),
        arr(BF16, 8, 256, 256),
        2 * 128 * 512 * 4096,
        3 << 20,
    )(place, heads, heads_other, weight, across)


def head_grad_kernel(place, *refs):
    step = pl.program_id(0)
    *weight_refs, kept_ref, given_ref = refs[4:]
    total = jnp.dot(
        grad_rows(place, refs[:4]),
        weight_rows(weight_refs),
        preferred_element_type=F32,
    )

    @pl.when(step == 0)
    def _():
        kept_ref[...] = total[:WIDTH]
        given_ref[...] = total[WIDTH:]

    @pl.when(step > 0)
    def _():
        kept_ref[...] += total[:WIDTH]
        given_ref[...] += total[WIDTH:]


def head_gradient(place, grad_full, grad_other, weight, across):
    part = arr(F32, WIDTH, 512)
    return call(
        head_grad_kernel,
        STEPS,
        grad_specs() + [weight_tile(), weight_tile()],
        [whole(WIDTH, 512), whole(WIDTH, 512)],
        [part, part],
        2 * 128 * 512 * 4096,
        5 << 20,
    )(place, grad_full, grad_full, grad_other, grad_other, weight, across)


def pull_kernel(
    place, q_ref, k_ref, logit_ref, m_ref, wy_ref, state_ref, end_ref, grad_ref,
    dq_ref, dk_ref, dv_ref, dlogit_ref,
):
    two = range(2)
    shape = (PAIRS, PAIRS)
    before = order_of(shape, 1) < order_of(shape, 0)
    query = [q_ref[:, i * WIDTH : (i + 1) * WIDTH].astype(F32) for i in two]
    query_scale = [inverse_norm(x) for x in query]
    query = [query[i] * query_scale[i] for i in two]
    key = [stacked(k_ref, i) for i in two]
    key_scale = [inverse_norm(x) for x in key]
    key = [key[i] * key_scale[i] for i in two]
    first = 2 * pl.program_id(0)
    logit = [column_of(logit_ref[pl.ds(first + i, 1), :]) for i in two]
    state = [state_ref[i] for i in two]
    end = [end_ref[i] for i in two]
    grad = [grad_ref[:, i * WIDTH : (i + 1) * WIDTH] for i in two]
    updates = [wy_ref[i, :, WIDTH:] - dot(wy_ref[i, :, :WIDTH], state[i]) for i in two]
    pulled = [dot(m_ref[i], jnp.concatenate([grad[i], end[i].astype(F32)], axis=0), 0, 0) for i in two]
    value_grad = [2.0 / (1.0 + jnp.exp(-logit[i])) * pulled[i] for i in two]
    cross = [
        dot(jnp.concatenate([grad[i], value_grad[i]], axis=0), updates[i], 1, 1) for i in two
    ]
    pairs = [
        jnp.concatenate(
            [
                jnp.where(visible_mask(), cross[i][:WIDTH], 0.0),
                jnp.where(before, -cross[i][WIDTH:], 0.0),
            ],
            axis=0,
        )
        for i in two
    ]
    forward = [dot(pairs[i], key[i]) for i in two]
    backward = [dot(pairs[i], jnp.concatenate([query[i], key[i]], axis=0), 0, 0) for i in two]
    by_state = [
        dot(jnp.concatenate([grad[i], -value_grad[i]], axis=0), state[i], 1, 1, passes=1)
        for i in two
    ]
    by_end = [dot(updates[i], end[i], 1, 1, passes=1) for i in two]
    for i in two:
        start = i * PAIRS
        dv_ref[:, start : start + WIDTH] = value_grad[i][:WIDTH].astype(BF16)
        dv_ref[:, start + WIDTH : start + PAIRS] = value_grad[i][WIDTH:].astype(BF16)
        slope = jnp.sum(pulled[i] * updates[i], axis=1, keepdims=True) / (1.0 + jnp.exp(logit[i]))
        dlogit_ref[pl.ds(first + i, 1), :] = row_of(slope)
        query_grad = forward[i][:WIDTH] + by_state[i][:WIDTH]
        query_grad = query_scale[i] * (
            query_grad - query[i] * jnp.sum(query[i] * query_grad, axis=1, keepdims=True)
        )
        dq_ref[:, i * WIDTH : (i + 1) * WIDTH] = query_grad.astype(BF16)
        key_grad = forward[i][WIDTH:] + backward[i] + by_end[i] + by_state[i][WIDTH:]
        key_grad = key_scale[i] * (
            key_grad - key[i] * jnp.sum(key[i] * key_grad, axis=1, keepdims=True)
        )
        dk_ref[:, start : start + WIDTH] = key_grad[:WIDTH].astype(BF16)
        dk_ref[:, start + WIDTH : start + PAIRS] = key_grad[WIDTH:].astype(BF16)


def pull(place, queries, keys, logits, reads, wy, state, end, head_grad):
    return call(
        pull_kernel,
        2,
        [
            by_columns(WIDTH),
            by_columns(PAIRS),
            whole(4, PAIRS),
            by_pair(PAIRS, PAIRS),
            by_pair(PAIRS, PAIRS),
            by_slot(WIDTH, WIDTH),
            by_slot(WIDTH, WIDTH),
            by_columns(WIDTH),
        ],
        [by_columns(WIDTH), by_columns(PAIRS), by_columns(PAIRS), whole(4, PAIRS)],
        [
            arr(BF16, WIDTH, 512),
            arr(BF16, WIDTH, 1024),
            arr(BF16, WIDTH, 1024),
            arr(F32, 4, PAIRS),
        ],
        4 * 14 * 2 * PAIRS**3,
        5 << 20,
    )(place, queries, keys, logits, reads, wy, state, end, head_grad)


def mul(a, b):
    return jnp.einsum("hij,hjk->hik", a, b, preferred_element_type=F32)


def mul_t(a, b):
    return jnp.einsum("hji,hjk->hik", a, b, preferred_element_type=F32)


def halves(x):
    return x[:, :, :WIDTH], x[:, :, WIDTH:]


def forward_states(place, mine, theirs, index, core, grad_full, weight):
    theirs = exchange(theirs, 1)
    even = jnp.where(core == 0, mine, theirs)
    odd = jnp.where(core == 0, theirs, mine)
    even_a, even_b = halves(even)
    odd_a, odd_b = halves(odd)
    joined = mul(odd_a, even)
    chip = jnp.concatenate(
        [joined[:, :, :WIDTH], joined[:, :, WIDTH:] + odd_b.astype(F32)], axis=2
    ).astype(BF16)
    total, levels = chip, []
    diagonal = jnp.broadcast_to(jnp.eye(WIDTH, dtype=BF16), (2, WIDTH, WIDTH))
    for bit in (2, 4, 8):
        came = exchange(total, bit)
        if bit == 4:
            weight, came = lax.optimization_barrier((weight, came))
            across = exchange(weight, 16)
        if bit == 8:
            grad_other, came = lax.optimization_barrier((exchange(grad_full, 1), came))
        upper = (index & bit) != 0
        left, right = jnp.where(upper, came, total), jnp.where(upper, total, came)
        right_a, right_b = halves(right)
        step = mul(right_a, left)
        total = jnp.concatenate(
            [step[:, :, :WIDTH], step[:, :, WIDTH:] + right_b.astype(F32)], axis=2
        ).astype(BF16)
        came_a, came_b = halves(came)
        if not levels:
            levels.append((bit, left[:, :, :WIDTH], None))
            before, state = jnp.where(upper, came_a, diagonal), jnp.where(upper, came_b, 0.0)
            state = state.astype(F32)
            after = jnp.where(upper, diagonal, came_a)
        else:
            levels.append((bit, left[:, :, :WIDTH], after))
            step = mul(before, came)
            before = jnp.where(upper, step[:, :, :WIDTH].astype(BF16), before)
            state = jnp.where(upper, state + step[:, :, WIDTH:], state)
            after = jnp.where(upper, after, mul(came_a, after).astype(BF16))
    far = send(total[:, :, WIDTH:], 16)
    kept_grad, given_grad = head_gradient(place, grad_full, grad_other, weight, across)
    kept_grad, given_grad, far = lax.optimization_barrier((kept_grad, given_grad, far))
    head_grad = (kept_grad, exchange(given_grad, 1))
    first = (state + mul(before, far)).astype(BF16)
    second = (mul(even_a, first) + even_b.astype(F32)).astype(BF16)
    kept = jnp.where(core == 0, first, second)
    given = jnp.where(core == 0, second, first)
    state_in = jnp.concatenate([kept, exchange(given, 1)], axis=0)
    weights = (weight, across)
    return weights, grad_full, grad_other, head_grad, state_in, (even_a, odd_a, levels, after)


def backward_states(mine, theirs, index, core, saved, gate, last):
    even_a, odd_a, levels, after = saved
    theirs = exchange(theirs, 1)
    even = jnp.where(core == 0, mine, theirs)
    odd = jnp.where(core == 0, theirs, mine)
    total = (even.astype(F32) + mul_t(even_a, odd)).astype(BF16)
    for bit, left_a, window in levels:
        came = exchange(total, bit)
        upper = (index & bit) != 0
        if window is None:
            gate, came = lax.optimization_barrier((gate, came))
            second = jnp.where(upper, 0.0, came.astype(F32))
        else:
            second = jnp.where(upper, second, second + mul_t(window, came))
        left, right = jnp.where(upper, came, total), jnp.where(upper, total, came)
        total = (left.astype(F32) + mul_t(left_a, right)).astype(BF16)
    second = second + mul_t(after, send(total, -16))
    second = second.astype(BF16)
    first = (odd.astype(F32) + mul_t(odd_a, second)).astype(BF16)
    kept = jnp.where(core == 0, first, second)
    given = jnp.where(core == 0, second, first)
    last, given = lax.optimization_barrier((last, given))
    return gate, last, jnp.concatenate([kept, exchange(given, 1)], axis=0)


def local(queries, keys, values, beta_logit, out_weight, out_grad):
    index = lax.axis_index("ctx")
    core = index & 1
    place = jnp.stack([core, index >> 4]).astype(jnp.int32)
    rings = [[(half * 8 + z) * 2 + c for z in range(8)] for half in range(2) for c in range(2)]
    operands = (queries, keys, values, beta_logit)
    theirs, *filled = prepare(place, *operands, False)
    mine, reads, wy, qt, local_out = prepare(place, *operands, True, filled)
    weight = lax.all_gather(out_weight, "ctx", axis=0, axis_index_groups=rings)
    grad_full = lax.all_to_all(
        jnp.broadcast_to(out_grad[None], (8, WIDTH, 512)), "tp", 0, 0, tiled=True
    )
    weights, grad_full, grad_other, head_grad, state, saved = forward_states(
        place, mine, theirs, index, core, grad_full, weight
    )
    heads, head_grad, own, own_theirs = head_outputs(place, qt, local_out, state, *head_grad)
    heads_other = exchange(heads, 1)
    terms = weight_terms(place, grad_full, grad_other, heads, heads_other)
    ring_sum = lax.psum_scatter(
        terms, "ctx", scatter_dimension=0, axis_index_groups=rings
    ).reshape(2, WIDTH, 512)
    parts = mixed_parts(place, heads, heads_other, *weights)
    parts, ring_sum, end = backward_states(own, own_theirs, index, core, saved, parts, ring_sum)
    weight_grad = ring_sum[0].astype(F32) + exchange(ring_sum[1], 16).astype(F32)
    parts = lax.all_to_all(parts, "tp", 0, 0, tiled=True)
    sums = jnp.sum(parts.astype(F32), axis=0).astype(BF16)
    kept, came = sums[:WIDTH], exchange(sums[WIDTH:], 1)
    first, second = jnp.where(core == 0, kept, came), jnp.where(core == 0, came, kept)
    mixed = jnp.concatenate(
        [first[:, :WIDTH], second[:, :WIDTH], first[:, WIDTH:], second[:, WIDTH:]], axis=1
    )
    query_grad, key_grad, value_grad, logit_grad = pull(
        place, queries, keys, beta_logit, reads, wy, state, end, head_grad
    )
    return mixed, query_grad, key_grad, value_grad, logit_grad, weight_grad


def solution(mesh):
    placed = P("ctx", "tp")
    return jax.shard_map(
        local,
        mesh=mesh,
        in_specs=(placed, placed, placed, P("tp", "ctx"), placed, placed),
        out_specs=(placed, placed, placed, placed, P("tp", "ctx"), placed),
        check_vma=False,
    )
```

```python
import functools
import math

import jax
import jax.numpy as jnp
from jax import lax
from jax.experimental import pallas as pl
from jax.experimental.pallas import tpu as pltpu
from jax.sharding import PartitionSpec as P

F32 = jnp.float32
BF16 = jnp.bfloat16
WIDTH = 128
VMEM = 62 << 20
PAIRS = 2 * WIDTH


def send(block, distance):
    devices = range(lax.axis_size("ctx"))
    route = [(i - distance, i) for i in devices if i - distance in devices]
    return lax.ppermute(block, "ctx", route)


def exchange(block, bit):
    route = [(i, i ^ bit) for i in range(lax.axis_size("ctx"))]
    return lax.ppermute(block, "ctx", route)


def split(x):
    high = x.astype(BF16)
    return high, (x - high.astype(F32)).astype(BF16)


def dot(a, b, ca=1, cb=0, passes=3):
    dims = (((ca,), (cb,)), ((), ()))
    mul = functools.partial(lax.dot_general, dimension_numbers=dims, preferred_element_type=F32)
    if passes == 1:
        return mul(a.astype(BF16), b.astype(BF16))
    if b.dtype == BF16:
        a_high, a_low = split(a)
        return mul(a_high, b) + mul(a_low, b)
    a_high, a_low = split(a)
    b_high, b_low = split(b)
    return mul(a_high, b_high) + (mul(a_low, b_high) + mul(a_high, b_low))


def inverse_norm(x):
    return lax.rsqrt(jnp.sum(x * x, axis=-1, keepdims=True) + 1e-06)


def order_of(shape, dim):
    p = lax.broadcasted_iota(jnp.int32, shape, dim)
    return 2 * (p & (WIDTH - 1)) + (p >> 7)


def column_of(row):
    shape = (PAIRS, PAIRS)
    time = lax.broadcasted_iota(jnp.int32, shape, 1)
    return jnp.sum(jnp.where(time == order_of(shape, 0), row, 0.0), axis=1, keepdims=True)


def row_of(column):
    shape = (PAIRS, PAIRS)
    time = lax.broadcasted_iota(jnp.int32, shape, 1)
    return jnp.sum(jnp.where(time == order_of(shape, 0), column, 0.0), axis=0, keepdims=True)


def visible_mask():
    shape = (WIDTH, PAIRS)
    token = lax.broadcasted_iota(jnp.int32, shape, 0)
    return (lax.broadcasted_iota(jnp.int32, shape, 1) & (WIDTH - 1)) <= token


def stacked(ref, i):
    start = i * PAIRS
    parts = [ref[:, start : start + WIDTH], ref[:, start + WIDTH : start + PAIRS]]
    return jnp.concatenate(parts, axis=0).astype(F32)


def prepare_kernel(mine, *refs):
    place, q_ref, k_ref, v_ref, logit_ref = refs[:5]
    first = 2 * (place[0] if mine else 1 - place[0])
    ab_ref, m_ref, wy_ref, qt_ref, local_ref = refs[-5:]
    two = range(2)
    shape = (PAIRS, PAIRS)
    row, col = order_of(shape, 0), order_of(shape, 1)
    identity = jnp.where(row == col, 1.0, 0.0).astype(F32)
    query = [q_ref[:, i * WIDTH : (i + 1) * WIDTH].astype(F32) for i in two]
    query = [x * inverse_norm(x) for x in query]
    key = [stacked(k_ref, i) for i in two]
    key = [x * inverse_norm(x) for x in key]
    strength = [2.0 / (1.0 + jnp.exp(-column_of(logit_ref[pl.ds(first + i, 1), :]))) for i in two]
    coupling = [jnp.where(col < row, strength[i] * dot(key[i], key[i], 1, 1), 0.0) for i in two]
    inverse = [identity - jnp.where((row >> 1) == (col >> 1), coupling[i], 0.0) for i in two]
    for level in range(1, 8):
        join = ((row >> (level + 1)) == (col >> (level + 1))) & ((row >> level) != (col >> level))
        edge = [jnp.where(join, coupling[i], 0.0) for i in two]
        step = [dot(inverse[i], edge[i], passes=1) for i in two]
        inverse = [inverse[i] - dot(step[i], inverse[i], passes=1) for i in two]
    rest = [identity - inverse[i] - dot(coupling[i], inverse[i]) for i in two]
    inverse = [inverse[i] + dot(inverse[i], rest[i], passes=1) for i in two]
    scores = [jnp.where(visible_mask(), dot(query[i], key[i], 1, 1), 0.0) for i in two]
    scaled = [strength[i] * jnp.concatenate([key[i], stacked(v_ref, i)], axis=1) for i in two]
    reads = [
        jnp.concatenate([dot(scores[i], inverse[i]), dot(key[i], inverse[i], 0, 0)], axis=0)
        for i in two
    ]
    product = [dot(reads[i], scaled[i]) for i in two]
    eye = identity[:WIDTH, :WIDTH]
    for i in two:
        ab_ref[i, :, :WIDTH] = (eye - product[i][WIDTH:, :WIDTH]).astype(BF16)
        ab_ref[i, :, WIDTH:] = product[i][WIDTH:, WIDTH:].astype(BF16)
        qt_ref[i] = query[i] - product[i][:WIDTH, :WIDTH]
        local_ref[i] = product[i][:WIDTH, WIDTH:]
        m_ref[i] = reads[i]
        wy_ref[i] = dot(inverse[i], scaled[i])


def slot(head, place):
    return (head + 2 * place[0]) % 4


def by_pair(*block):
    return pl.BlockSpec((2,) + block, lambda i, place: (i,) + (0,) * len(block))


def by_slot(*block):
    return pl.BlockSpec((2,) + block, lambda i, place: (i ^ place[0],) + (0,) * len(block))


def by_columns(width):
    return pl.BlockSpec((WIDTH, 2 * width), lambda i, place: (0, i))


def whole(*shape):
    return pl.BlockSpec(shape, lambda i, place: (0,) * len(shape))


def call(kernel, steps, in_specs, out_specs, out_shape, flops, moved, scratch=()):
    return pl.pallas_call(
        kernel,
        grid_spec=pltpu.PrefetchScalarGridSpec(
            num_scalar_prefetch=1,
            grid=(steps,),
            in_specs=in_specs,
            out_specs=out_specs,
            scratch_shapes=list(scratch),
        ),
        out_shape=out_shape,
        compiler_params=pltpu.CompilerParams(vmem_limit_bytes=VMEM),
        cost_estimate=pl.CostEstimate(flops=flops, bytes_accessed=moved, transcendentals=0),
    )


def arr(dtype, *shape):
    return jax.ShapeDtypeStruct(shape, dtype)


def prepare(place, queries, keys, values, logits, mine, filled=()):
    def pair(place):
        return place[0] if mine else 1 - place[0]

    def columns(width):
        return pl.BlockSpec((WIDTH, 2 * width), lambda i, place: (0, pair(place)))

    def heads(*block):
        return pl.BlockSpec((2,) + block, lambda i, place: (pair(place),) + (0,) * len(block))

    def stored(n):
        return arr(F32, 4, n, n)

    return pl.pallas_call(
        functools.partial(prepare_kernel, mine),
        grid_spec=pltpu.PrefetchScalarGridSpec(
            num_scalar_prefetch=1,
            grid=(1,),
            in_specs=[
                columns(WIDTH),
                columns(PAIRS),
                columns(PAIRS),
                whole(4, PAIRS),
            ]
            + [pl.BlockSpec(memory_space=pl.ANY)] * len(filled),
            out_specs=[
                pl.BlockSpec((2, WIDTH, PAIRS), lambda i, place: (0, 0, 0)),
                heads(PAIRS, PAIRS),
                heads(PAIRS, PAIRS),
                heads(WIDTH, WIDTH),
                heads(WIDTH, WIDTH),
            ],
        ),
        out_shape=[
            arr(BF16, 2, WIDTH, PAIRS),
            stored(PAIRS),
            stored(PAIRS),
            stored(WIDTH),
            stored(WIDTH),
        ],
        input_output_aliases={5 + i: 1 + i for i in range(len(filled))},
        compiler_params=pltpu.CompilerParams(vmem_limit_bytes=VMEM),
        cost_estimate=pl.CostEstimate(
            flops=(1 if mine else 100) << 20, bytes_accessed=1 << (16 if mine else 24), transcendentals=0
        ),
    )(place, queries, keys, values, logits, *filled)


STEPS = 4
BLOCKS = [(z, row) for z in range(2) for row in range(2)]


def grad_rows(place, refs):
    def block(ref, z):
        return ref[0, :, pl.ds(pl.multiple_of(z * 256 + place[0] * 128, 128), 128)]

    rows = [
        jnp.concatenate([block(refs[2 * core + row], z) for z, row in BLOCKS], axis=1)
        for core in range(2)
    ]
    return jnp.concatenate(rows, axis=0)


def grad_specs():
    def tile(row):
        return pl.BlockSpec(
            (1, WIDTH, 512), lambda step, place: ((row ^ place[1]) * 4 + step, 0, 0)
        )

    return [tile(0), tile(1), tile(0), tile(1)]


def weight_rows(ref):
    return jnp.concatenate([ref[z, row] for z, row in BLOCKS], axis=0)


def weight_tile():
    return pl.BlockSpec((2, 2, WIDTH, 512), lambda step, place: (step, 0, 0, 0))


def heads_kernel(
    place, qt_ref, local_ref, state_ref, kept_ref, came_ref,
    heads_ref, grad_ref, mine_ref, theirs_ref,
):
    grad_ref[...] = kept_ref[...] + came_ref[...]
    for head in range(4):
        columns = slice(head * WIDTH, (head + 1) * WIDTH)
        result = dot(qt_ref[head], state_ref[slot(head, place)]) + local_ref[head]
        heads_ref[:, columns] = result.astype(BF16)
        own = dot(qt_ref[head], grad_ref[:, columns], 0, 0, passes=1).astype(BF16)

        @pl.when(place[0] == head // 2)
        def _():
            mine_ref[head % 2] = own

        @pl.when(place[0] != head // 2)
        def _():
            theirs_ref[head % 2] = own


def head_outputs(place, qt, local, state, kept, came):
    square, pair = whole(4, WIDTH, WIDTH), arr(BF16, 2, WIDTH, WIDTH)
    return call(
        heads_kernel,
        1,
        [square, square, square, whole(WIDTH, 512), whole(WIDTH, 512)],
        [whole(WIDTH, 512), whole(WIDTH, 512), whole(2, WIDTH, WIDTH), whole(2, WIDTH, WIDTH)],
        [arr(BF16, WIDTH, 512), arr(F32, WIDTH, 512), pair, pair],
        2 * 8 * 128**3,
        2 << 20,
    )(place, qt, local, state, kept, came)


def weight_terms_kernel(place, *refs):
    heads_ref, heads_other_ref, out_ref = refs[4:]
    product = lax.dot_general(
        grad_rows(place, refs[:4]),
        jnp.concatenate([heads_ref[...], heads_other_ref[...]], axis=0),
        (((0,), (0,)), ((), ())),
        preferred_element_type=F32,
    )
    product = (product * (1.0 / 64.0)).astype(BF16)
    for z in range(2):
        out_ref[z] = product[z * 256 : z * 256 + 256]


def weight_terms(place, grad_full, grad_other, heads, heads_other):
    return call(
        weight_terms_kernel,
        STEPS,
        grad_specs() + [whole(WIDTH, 512), whole(WIDTH, 512)],
        pl.BlockSpec((2, 256, 512), lambda step, place: (step, 0, 0)),
        arr(BF16, 8, 256, 512),
        2 * 128 * 512 * 4096,
        5 << 20,
    )(place, grad_full, grad_full, grad_other, grad_other, heads, heads_other)


def mixed_kernel(place, heads_ref, heads_other_ref, weight_ref, out_ref):
    step = pl.program_id(0)
    product = lax.dot_general(
        jnp.concatenate([heads_ref[...], heads_other_ref[...]], axis=0),
        weight_rows(weight_ref),
        (((1,), (1,)), ((), ())),
        preferred_element_type=F32,
    ).astype(BF16)
    for i, (z, row) in enumerate(BLOCKS):
        owner = (row ^ place[1]) * 4 + step
        out_ref[owner, :, z * 128 : z * 128 + 128] = product[:, i * WIDTH : (i + 1) * WIDTH]


def mixed_parts(place, heads, heads_other, weight):
    return call(
        mixed_kernel,
        STEPS,
        [whole(WIDTH, 512), whole(WIDTH, 512), weight_tile()],
        whole(8, 256, 256),
        arr(BF16, 8, 256, 256),
        2 * 128 * 512 * 4096,
        3 << 20,
    )(place, heads, heads_other, weight)


def head_grad_kernel(place, *refs):
    step = pl.program_id(0)
    weight_ref, kept_ref, given_ref = refs[4:]
    total = jnp.dot(
        grad_rows(place, refs[:4]),
        weight_rows(weight_ref),
        preferred_element_type=F32,
    )

    @pl.when(step == 0)
    def _():
        kept_ref[...] = total[:WIDTH]
        given_ref[...] = total[WIDTH:]

    @pl.when(step > 0)
    def _():
        kept_ref[...] += total[:WIDTH]
        given_ref[...] += total[WIDTH:]


def head_gradient(place, grad_full, grad_other, weight):
    part = arr(F32, WIDTH, 512)
    return call(
        head_grad_kernel,
        STEPS,
        grad_specs() + [weight_tile()],
        [whole(WIDTH, 512), whole(WIDTH, 512)],
        [part, part],
        2 * 128 * 512 * 4096,
        5 << 20,
    )(place, grad_full, grad_full, grad_other, grad_other, weight)


def pull_kernel(
    place, q_ref, k_ref, logit_ref, m_ref, wy_ref, state_ref, end_ref, grad_ref,
    dq_ref, dk_ref, dv_ref, dlogit_ref,
):
    two = range(2)
    shape = (PAIRS, PAIRS)
    before = order_of(shape, 1) < order_of(shape, 0)
    query = [q_ref[:, i * WIDTH : (i + 1) * WIDTH].astype(F32) for i in two]
    query_scale = [inverse_norm(x) for x in query]
    query = [query[i] * query_scale[i] for i in two]
    key = [stacked(k_ref, i) for i in two]
    key_scale = [inverse_norm(x) for x in key]
    key = [key[i] * key_scale[i] for i in two]
    first = 2 * pl.program_id(0)
    logit = [column_of(logit_ref[pl.ds(first + i, 1), :]) for i in two]
    state = [state_ref[i] for i in two]
    end = [end_ref[i] for i in two]
    grad = [grad_ref[:, i * WIDTH : (i + 1) * WIDTH] for i in two]
    updates = [wy_ref[i, :, WIDTH:] - dot(wy_ref[i, :, :WIDTH], state[i]) for i in two]
    pulled = [dot(m_ref[i], jnp.concatenate([grad[i], end[i].astype(F32)], axis=0), 0, 0) for i in two]
    value_grad = [2.0 / (1.0 + jnp.exp(-logit[i])) * pulled[i] for i in two]
    cross = [
        dot(jnp.concatenate([grad[i], value_grad[i]], axis=0), updates[i], 1, 1) for i in two
    ]
    pairs = [
        jnp.concatenate(
            [
                jnp.where(visible_mask(), cross[i][:WIDTH], 0.0),
                jnp.where(before, -cross[i][WIDTH:], 0.0),
            ],
            axis=0,
        )
        for i in two
    ]
    forward = [dot(pairs[i], key[i]) for i in two]
    backward = [dot(pairs[i], jnp.concatenate([query[i], key[i]], axis=0), 0, 0) for i in two]
    by_state = [
        dot(jnp.concatenate([grad[i], -value_grad[i]], axis=0), state[i], 1, 1, passes=1)
        for i in two
    ]
    by_end = [dot(updates[i], end[i], 1, 1, passes=1) for i in two]
    for i in two:
        start = i * PAIRS
        dv_ref[:, start : start + WIDTH] = value_grad[i][:WIDTH].astype(BF16)
        dv_ref[:, start + WIDTH : start + PAIRS] = value_grad[i][WIDTH:].astype(BF16)
        slope = jnp.sum(pulled[i] * updates[i], axis=1, keepdims=True) / (1.0 + jnp.exp(logit[i]))
        dlogit_ref[pl.ds(first + i, 1), :] = row_of(slope)
        query_grad = forward[i][:WIDTH] + by_state[i][:WIDTH]
        query_grad = query_scale[i] * (
            query_grad - query[i] * jnp.sum(query[i] * query_grad, axis=1, keepdims=True)
        )
        dq_ref[:, i * WIDTH : (i + 1) * WIDTH] = query_grad.astype(BF16)
        key_grad = forward[i][WIDTH:] + backward[i] + by_end[i] + by_state[i][WIDTH:]
        key_grad = key_scale[i] * (
            key_grad - key[i] * jnp.sum(key[i] * key_grad, axis=1, keepdims=True)
        )
        dk_ref[:, start : start + WIDTH] = key_grad[:WIDTH].astype(BF16)
        dk_ref[:, start + WIDTH : start + PAIRS] = key_grad[WIDTH:].astype(BF16)


def pull(place, queries, keys, logits, reads, wy, state, end, head_grad):
    return call(
        pull_kernel,
        2,
        [
            by_columns(WIDTH),
            by_columns(PAIRS),
            whole(4, PAIRS),
            by_pair(PAIRS, PAIRS),
            by_pair(PAIRS, PAIRS),
            by_slot(WIDTH, WIDTH),
            by_slot(WIDTH, WIDTH),
            by_columns(WIDTH),
        ],
        [by_columns(WIDTH), by_columns(PAIRS), by_columns(PAIRS), whole(4, PAIRS)],
        [
            arr(BF16, WIDTH, 512),
            arr(BF16, WIDTH, 1024),
            arr(BF16, WIDTH, 1024),
            arr(F32, 4, PAIRS),
        ],
        4 * 14 * 2 * PAIRS**3,
        5 << 20,
    )(place, queries, keys, logits, reads, wy, state, end, head_grad)


def mul(a, b):
    return jnp.einsum("hij,hjk->hik", a, b, preferred_element_type=F32)


def mul_t(a, b):
    return jnp.einsum("hji,hjk->hik", a, b, preferred_element_type=F32)


def halves(x):
    return x[:, :, :WIDTH], x[:, :, WIDTH:]


def forward_states(place, mine, theirs, index, core, grad_full, weight):
    theirs = exchange(theirs, 1)
    even = jnp.where(core == 0, mine, theirs)
    odd = jnp.where(core == 0, theirs, mine)
    even_a, even_b = halves(even)
    odd_a, odd_b = halves(odd)
    joined = mul(odd_a, even)
    chip = jnp.concatenate(
        [joined[:, :, :WIDTH], joined[:, :, WIDTH:] + odd_b.astype(F32)], axis=2
    ).astype(BF16)
    total, levels = chip, []
    diagonal = jnp.broadcast_to(jnp.eye(WIDTH, dtype=BF16), (2, WIDTH, WIDTH))
    for bit in (2, 4, 8):
        came = exchange(total, bit)
        if bit == 8:
            grad_other, came = lax.optimization_barrier((exchange(grad_full, 1), came))
        upper = (index & bit) != 0
        left, right = jnp.where(upper, came, total), jnp.where(upper, total, came)
        right_a, right_b = halves(right)
        step = mul(right_a, left)
        total = jnp.concatenate(
            [step[:, :, :WIDTH], step[:, :, WIDTH:] + right_b.astype(F32)], axis=2
        ).astype(BF16)
        came_a, came_b = halves(came)
        if not levels:
            levels.append((bit, left[:, :, :WIDTH], None))
            before, state = jnp.where(upper, came_a, diagonal), jnp.where(upper, came_b, 0.0)
            state = state.astype(F32)
            after = jnp.where(upper, diagonal, came_a)
        else:
            levels.append((bit, left[:, :, :WIDTH], after))
            step = mul(before, came)
            before = jnp.where(upper, step[:, :, :WIDTH].astype(BF16), before)
            state = jnp.where(upper, state + step[:, :, WIDTH:], state)
            after = jnp.where(upper, after, mul(came_a, after).astype(BF16))
    weight, total = lax.optimization_barrier((weight, total))
    far = send(total[:, :, WIDTH:], 16)
    kept_grad, given_grad = head_gradient(place, grad_full, grad_other, weight)
    kept_grad, given_grad, far = lax.optimization_barrier((kept_grad, given_grad, far))
    head_grad = (kept_grad, exchange(given_grad, 1))
    first = (state + mul(before, far)).astype(BF16)
    second = (mul(even_a, first) + even_b.astype(F32)).astype(BF16)
    kept = jnp.where(core == 0, first, second)
    given = jnp.where(core == 0, second, first)
    state_in = jnp.concatenate([kept, exchange(given, 1)], axis=0)
    return grad_full, grad_other, head_grad, state_in, (even_a, odd_a, levels, after)


def backward_states(mine, theirs, index, core, saved, gate, last):
    even_a, odd_a, levels, after = saved
    theirs = exchange(theirs, 1)
    even = jnp.where(core == 0, mine, theirs)
    odd = jnp.where(core == 0, theirs, mine)
    total = (even.astype(F32) + mul_t(even_a, odd)).astype(BF16)
    for bit, left_a, window in levels:
        came = exchange(total, bit)
        upper = (index & bit) != 0
        if window is None:
            gate, came = lax.optimization_barrier((gate, came))
            second = jnp.where(upper, 0.0, came.astype(F32))
        else:
            second = jnp.where(upper, second, second + mul_t(window, came))
        left, right = jnp.where(upper, came, total), jnp.where(upper, total, came)
        total = (left.astype(F32) + mul_t(left_a, right)).astype(BF16)
    second = second + mul_t(after, send(total, -16))
    second = second.astype(BF16)
    first = (odd.astype(F32) + mul_t(odd_a, second)).astype(BF16)
    kept = jnp.where(core == 0, first, second)
    given = jnp.where(core == 0, second, first)
    last, given = lax.optimization_barrier((last, given))
    return gate, last, jnp.concatenate([kept, exchange(given, 1)], axis=0)


def local(queries, keys, values, beta_logit, out_weight, out_grad):
    index = lax.axis_index("ctx")
    core = index & 1
    place = jnp.stack([core, index >> 4]).astype(jnp.int32)
    rings = [[(half * 8 + z) * 2 + c for z in range(8)] for half in range(2) for c in range(2)]
    operands = (queries, keys, values, beta_logit)
    across = exchange(out_weight, 16)
    theirs, *filled = prepare(place, *operands, False)
    across, theirs = lax.optimization_barrier((across, theirs))
    weight_pair = jnp.stack([out_weight, across])
    weight_pair, *operands = lax.optimization_barrier((weight_pair, *operands))
    mine, reads, wy, qt, local_out = prepare(place, *operands, True, filled)
    weight_mine = lax.all_gather(weight_pair, "ctx", axis=0, axis_index_groups=rings)
    grad_full = lax.all_to_all(
        jnp.broadcast_to(out_grad[None], (8, WIDTH, 512)), "tp", 0, 0, tiled=True
    )
    grad_full, grad_other, head_grad, state, saved = forward_states(
        place, mine, theirs, index, core, grad_full, weight_mine
    )
    heads, head_grad, own, own_theirs = head_outputs(place, qt, local_out, state, *head_grad)
    heads_other = exchange(heads, 1)
    terms = weight_terms(place, grad_full, grad_other, heads, heads_other)
    ring_sum = lax.psum_scatter(
        terms, "ctx", scatter_dimension=0, axis_index_groups=rings
    ).reshape(2, WIDTH, 512)
    parts = mixed_parts(place, heads, heads_other, weight_mine)
    parts, ring_sum, end = backward_states(own, own_theirs, index, core, saved, parts, ring_sum)
    across = exchange(ring_sum[1], 16)
    parts = lax.all_to_all(parts, "tp", 0, 0, tiled=True)
    query_grad, key_grad, value_grad, logit_grad = pull(
        place, queries, keys, beta_logit, reads, wy, state, end, head_grad
    )
    parts, across, query_grad = lax.optimization_barrier((parts, across, query_grad))
    weight_grad = ring_sum[0].astype(F32) + across.astype(F32)
    sums = jnp.sum(parts.astype(F32), axis=0).astype(BF16)
    kept, came = sums[:WIDTH], exchange(sums[WIDTH:], 1)
    first, second = jnp.where(core == 0, kept, came), jnp.where(core == 0, came, kept)
    mixed = jnp.concatenate(
        [first[:, :WIDTH], second[:, :WIDTH], first[:, WIDTH:], second[:, WIDTH:]], axis=1
    )
    return mixed, query_grad, key_grad, value_grad, logit_grad, weight_grad


def solution(mesh):
    placed = P("ctx", "tp")
    return jax.shard_map(
        local,
        mesh=mesh,
        in_specs=(placed, placed, placed, P("tp", "ctx"), placed, placed),
        out_specs=(placed, placed, placed, placed, P("tp", "ctx"), placed),
        check_vma=False,
    )
```

```python
import functools
import math

import jax
import jax.numpy as jnp
from jax import lax
from jax.experimental import pallas as pl
from jax.experimental.pallas import tpu as pltpu
from jax.sharding import PartitionSpec as P

F32 = jnp.float32
BF16 = jnp.bfloat16
WIDTH = 128
VMEM = 62 << 20
PAIRS = 2 * WIDTH


def send(block, distance):
    devices = range(lax.axis_size("ctx"))
    route = [(i - distance, i) for i in devices if i - distance in devices]
    return lax.ppermute(block, "ctx", route)


def exchange(block, bit):
    route = [(i, i ^ bit) for i in range(lax.axis_size("ctx"))]
    return lax.ppermute(block, "ctx", route)


def split(x):
    high = x.astype(BF16)
    return high, (x - high.astype(F32)).astype(BF16)


def dot(a, b, ca=1, cb=0, passes=3):
    dims = (((ca,), (cb,)), ((), ()))
    mul = functools.partial(lax.dot_general, dimension_numbers=dims, preferred_element_type=F32)
    if passes == 1:
        return mul(a.astype(BF16), b.astype(BF16))
    if b.dtype == BF16:
        a_high, a_low = split(a)
        return mul(a_high, b) + mul(a_low, b)
    a_high, a_low = split(a)
    b_high, b_low = split(b)
    return mul(a_high, b_high) + (mul(a_low, b_high) + mul(a_high, b_low))


def inverse_norm(x):
    return lax.rsqrt(jnp.sum(x * x, axis=-1, keepdims=True) + 1e-06)


def order_of(shape, dim):
    p = lax.broadcasted_iota(jnp.int32, shape, dim)
    return 2 * (p & (WIDTH - 1)) + (p >> 7)


def column_of(row):
    shape = (PAIRS, PAIRS)
    time = lax.broadcasted_iota(jnp.int32, shape, 1)
    return jnp.sum(jnp.where(time == order_of(shape, 0), row, 0.0), axis=1, keepdims=True)


def row_of(column):
    shape = (PAIRS, PAIRS)
    time = lax.broadcasted_iota(jnp.int32, shape, 1)
    return jnp.sum(jnp.where(time == order_of(shape, 0), column, 0.0), axis=0, keepdims=True)


def visible_mask():
    shape = (WIDTH, PAIRS)
    token = lax.broadcasted_iota(jnp.int32, shape, 0)
    return (lax.broadcasted_iota(jnp.int32, shape, 1) & (WIDTH - 1)) <= token


def stacked(ref, i):
    start = i * PAIRS
    parts = [ref[:, start : start + WIDTH], ref[:, start + WIDTH : start + PAIRS]]
    return jnp.concatenate(parts, axis=0).astype(F32)


def prepare_kernel(mine, *refs):
    place, q_ref, k_ref, v_ref, logit_ref = refs[:5]
    first = 2 * (place[0] if mine else 1 - place[0])
    ab_ref, m_ref, wy_ref, qt_ref, local_ref = refs[-5:]
    two = range(2)
    shape = (PAIRS, PAIRS)
    row, col = order_of(shape, 0), order_of(shape, 1)
    identity = jnp.where(row == col, 1.0, 0.0).astype(F32)
    query = [q_ref[:, i * WIDTH : (i + 1) * WIDTH].astype(F32) for i in two]
    query = [x * inverse_norm(x) for x in query]
    key = [stacked(k_ref, i) for i in two]
    key = [x * inverse_norm(x) for x in key]
    strength = [2.0 / (1.0 + jnp.exp(-column_of(logit_ref[pl.ds(first + i, 1), :]))) for i in two]
    coupling = [jnp.where(col < row, strength[i] * dot(key[i], key[i], 1, 1), 0.0) for i in two]
    inverse = [identity - jnp.where((row >> 1) == (col >> 1), coupling[i], 0.0) for i in two]
    for level in range(1, 8):
        join = ((row >> (level + 1)) == (col >> (level + 1))) & ((row >> level) != (col >> level))
        edge = [jnp.where(join, coupling[i], 0.0) for i in two]
        step = [dot(inverse[i], edge[i], passes=1) for i in two]
        inverse = [inverse[i] - dot(step[i], inverse[i], passes=1) for i in two]
    rest = [identity - inverse[i] - dot(coupling[i], inverse[i]) for i in two]
    inverse = [inverse[i] + dot(inverse[i], rest[i], passes=1) for i in two]
    scores = [jnp.where(visible_mask(), dot(query[i], key[i], 1, 1), 0.0) for i in two]
    scaled = [strength[i] * jnp.concatenate([key[i], stacked(v_ref, i)], axis=1) for i in two]
    reads = [
        jnp.concatenate([dot(scores[i], inverse[i]), dot(key[i], inverse[i], 0, 0)], axis=0)
        for i in two
    ]
    product = [dot(reads[i], scaled[i]) for i in two]
    eye = identity[:WIDTH, :WIDTH]
    for i in two:
        ab_ref[i, :, :WIDTH] = (eye - product[i][WIDTH:, :WIDTH]).astype(BF16)
        ab_ref[i, :, WIDTH:] = product[i][WIDTH:, WIDTH:].astype(BF16)
        qt_ref[i] = query[i] - product[i][:WIDTH, :WIDTH]
        local_ref[i] = product[i][:WIDTH, WIDTH:]
        m_ref[i] = reads[i]
        wy_ref[i] = dot(inverse[i], scaled[i])


def slot(head, place):
    return (head + 2 * place[0]) % 4


def by_pair(*block):
    return pl.BlockSpec((2,) + block, lambda i, place: (i,) + (0,) * len(block))


def by_slot(*block):
    return pl.BlockSpec((2,) + block, lambda i, place: (i ^ place[0],) + (0,) * len(block))


def by_columns(width):
    return pl.BlockSpec((WIDTH, 2 * width), lambda i, place: (0, i))


def whole(*shape):
    return pl.BlockSpec(shape, lambda i, place: (0,) * len(shape))


def call(kernel, steps, in_specs, out_specs, out_shape, flops, moved, scratch=()):
    return pl.pallas_call(
        kernel,
        grid_spec=pltpu.PrefetchScalarGridSpec(
            num_scalar_prefetch=1,
            grid=(steps,),
            in_specs=in_specs,
            out_specs=out_specs,
            scratch_shapes=list(scratch),
        ),
        out_shape=out_shape,
        compiler_params=pltpu.CompilerParams(vmem_limit_bytes=VMEM),
        cost_estimate=pl.CostEstimate(flops=flops, bytes_accessed=moved, transcendentals=0),
    )


def arr(dtype, *shape):
    return jax.ShapeDtypeStruct(shape, dtype)


def prepare(place, queries, keys, values, logits, mine, filled=()):
    def pair(place):
        return place[0] if mine else 1 - place[0]

    def columns(width):
        return pl.BlockSpec((WIDTH, 2 * width), lambda i, place: (0, pair(place)))

    def heads(*block):
        return pl.BlockSpec((2,) + block, lambda i, place: (pair(place),) + (0,) * len(block))

    def stored(n):
        return arr(F32, 4, n, n)

    return pl.pallas_call(
        functools.partial(prepare_kernel, mine),
        grid_spec=pltpu.PrefetchScalarGridSpec(
            num_scalar_prefetch=1,
            grid=(1,),
            in_specs=[
                columns(WIDTH),
                columns(PAIRS),
                columns(PAIRS),
                whole(4, PAIRS),
            ]
            + [pl.BlockSpec(memory_space=pl.ANY)] * len(filled),
            out_specs=[
                pl.BlockSpec((2, WIDTH, PAIRS), lambda i, place: (0, 0, 0)),
                heads(PAIRS, PAIRS),
                heads(PAIRS, PAIRS),
                heads(WIDTH, WIDTH),
                heads(WIDTH, WIDTH),
            ],
        ),
        out_shape=[
            arr(BF16, 2, WIDTH, PAIRS),
            stored(PAIRS),
            stored(PAIRS),
            stored(WIDTH),
            stored(WIDTH),
        ],
        input_output_aliases={5 + i: 1 + i for i in range(len(filled))},
        compiler_params=pltpu.CompilerParams(vmem_limit_bytes=VMEM),
        cost_estimate=pl.CostEstimate(
            flops=(1 if mine else 100) << 20, bytes_accessed=1 << (16 if mine else 24), transcendentals=0
        ),
    )(place, queries, keys, values, logits, *filled)


STEPS = 4
BLOCKS = [(z, row) for z in range(2) for row in range(2)]


def grad_rows(place, refs):
    def block(ref, z):
        return ref[0, :, pl.ds(pl.multiple_of(z * 256 + place[0] * 128, 128), 128)]

    rows = [
        jnp.concatenate([block(refs[2 * core + row], z) for z, row in BLOCKS], axis=1)
        for core in range(2)
    ]
    return jnp.concatenate(rows, axis=0)


def grad_specs():
    def tile(row):
        return pl.BlockSpec(
            (1, WIDTH, 512), lambda step, place: ((row ^ place[1]) * 4 + step, 0, 0)
        )

    return [tile(0), tile(1), tile(0), tile(1)]


def weight_rows(ref):
    return jnp.concatenate([ref[z, row] for z, row in BLOCKS], axis=0)


def weight_tile():
    return pl.BlockSpec((2, 2, WIDTH, 512), lambda step, place: (step, 0, 0, 0))


def heads_kernel(
    place, qt_ref, local_ref, state_ref, kept_ref, came_ref,
    heads_ref, grad_ref, mine_ref, theirs_ref,
):
    grad_ref[...] = kept_ref[...] + came_ref[...]
    for head in range(4):
        columns = slice(head * WIDTH, (head + 1) * WIDTH)
        result = dot(qt_ref[head], state_ref[slot(head, place)]) + local_ref[head]
        heads_ref[:, columns] = result.astype(BF16)
        own = dot(qt_ref[head], grad_ref[:, columns], 0, 0, passes=1).astype(BF16)

        @pl.when(place[0] == head // 2)
        def _():
            mine_ref[head % 2] = own

        @pl.when(place[0] != head // 2)
        def _():
            theirs_ref[head % 2] = own


def head_outputs(place, qt, local, state, kept, came):
    square, pair = whole(4, WIDTH, WIDTH), arr(BF16, 2, WIDTH, WIDTH)
    return call(
        heads_kernel,
        1,
        [square, square, square, whole(WIDTH, 512), whole(WIDTH, 512)],
        [whole(WIDTH, 512), whole(WIDTH, 512), whole(2, WIDTH, WIDTH), whole(2, WIDTH, WIDTH)],
        [arr(BF16, WIDTH, 512), arr(F32, WIDTH, 512), pair, pair],
        2 * 8 * 128**3,
        2 << 20,
    )(place, qt, local, state, kept, came)


def weight_terms_kernel(place, *refs):
    heads_ref, heads_other_ref, out_ref = refs[4:]
    product = lax.dot_general(
        grad_rows(place, refs[:4]),
        jnp.concatenate([heads_ref[...], heads_other_ref[...]], axis=0),
        (((0,), (0,)), ((), ())),
        preferred_element_type=F32,
    )
    product = (product * (1.0 / 64.0)).astype(BF16)
    for z in range(2):
        out_ref[z] = product[z * 256 : z * 256 + 256]


def weight_terms(place, grad_full, grad_other, heads, heads_other):
    return call(
        weight_terms_kernel,
        STEPS,
        grad_specs() + [whole(WIDTH, 512), whole(WIDTH, 512)],
        pl.BlockSpec((2, 256, 512), lambda step, place: (step, 0, 0)),
        arr(BF16, 8, 256, 512),
        2 * 128 * 512 * 4096,
        5 << 20,
    )(place, grad_full, grad_full, grad_other, grad_other, heads, heads_other)


def mixed_kernel(place, heads_ref, heads_other_ref, weight_ref, out_ref):
    step = pl.program_id(0)
    product = lax.dot_general(
        jnp.concatenate([heads_ref[...], heads_other_ref[...]], axis=0),
        weight_rows(weight_ref),
        (((1,), (1,)), ((), ())),
        preferred_element_type=F32,
    ).astype(BF16)
    for i, (z, row) in enumerate(BLOCKS):
        owner = (row ^ place[1]) * 4 + step
        out_ref[owner, :, z * 128 : z * 128 + 128] = product[:, i * WIDTH : (i + 1) * WIDTH]


def mixed_parts(place, heads, heads_other, weight):
    return call(
        mixed_kernel,
        STEPS,
        [whole(WIDTH, 512), whole(WIDTH, 512), weight_tile()],
        whole(8, 256, 256),
        arr(BF16, 8, 256, 256),
        2 * 128 * 512 * 4096,
        3 << 20,
    )(place, heads, heads_other, weight)


def head_grad_kernel(place, *refs):
    step = pl.program_id(0)
    weight_ref, kept_ref, given_ref = refs[4:]
    total = jnp.dot(
        grad_rows(place, refs[:4]),
        weight_rows(weight_ref),
        preferred_element_type=F32,
    )

    @pl.when(step == 0)
    def _():
        kept_ref[...] = total[:WIDTH]
        given_ref[...] = total[WIDTH:]

    @pl.when(step > 0)
    def _():
        kept_ref[...] += total[:WIDTH]
        given_ref[...] += total[WIDTH:]


def head_gradient(place, grad_full, grad_other, weight):
    part = arr(F32, WIDTH, 512)
    return call(
        head_grad_kernel,
        STEPS,
        grad_specs() + [weight_tile()],
        [whole(WIDTH, 512), whole(WIDTH, 512)],
        [part, part],
        2 * 128 * 512 * 4096,
        5 << 20,
    )(place, grad_full, grad_full, grad_other, grad_other, weight)


def pull_kernel(
    place, q_ref, k_ref, logit_ref, m_ref, wy_ref, state_ref, end_ref, grad_ref,
    dq_ref, dk_ref, dv_ref, dlogit_ref,
):
    two = range(2)
    shape = (PAIRS, PAIRS)
    before = order_of(shape, 1) < order_of(shape, 0)
    query = [q_ref[:, i * WIDTH : (i + 1) * WIDTH].astype(F32) for i in two]
    query_scale = [inverse_norm(x) for x in query]
    query = [query[i] * query_scale[i] for i in two]
    key = [stacked(k_ref, i) for i in two]
    key_scale = [inverse_norm(x) for x in key]
    key = [key[i] * key_scale[i] for i in two]
    first = 2 * pl.program_id(0)
    logit = [column_of(logit_ref[pl.ds(first + i, 1), :]) for i in two]
    state = [state_ref[i] for i in two]
    end = [end_ref[i] for i in two]
    grad = [grad_ref[:, i * WIDTH : (i + 1) * WIDTH] for i in two]
    updates = [wy_ref[i, :, WIDTH:] - dot(wy_ref[i, :, :WIDTH], state[i]) for i in two]
    pulled = [dot(m_ref[i], jnp.concatenate([grad[i], end[i].astype(F32)], axis=0), 0, 0) for i in two]
    value_grad = [2.0 / (1.0 + jnp.exp(-logit[i])) * pulled[i] for i in two]
    cross = [
        dot(jnp.concatenate([grad[i], value_grad[i]], axis=0), updates[i], 1, 1) for i in two
    ]
    pairs = [
        jnp.concatenate(
            [
                jnp.where(visible_mask(), cross[i][:WIDTH], 0.0),
                jnp.where(before, -cross[i][WIDTH:], 0.0),
            ],
            axis=0,
        )
        for i in two
    ]
    forward = [dot(pairs[i], key[i]) for i in two]
    backward = [dot(pairs[i], jnp.concatenate([query[i], key[i]], axis=0), 0, 0) for i in two]
    by_state = [
        dot(jnp.concatenate([grad[i], -value_grad[i]], axis=0), state[i], 1, 1, passes=1)
        for i in two
    ]
    by_end = [dot(updates[i], end[i], 1, 1, passes=1) for i in two]
    for i in two:
        start = i * PAIRS
        dv_ref[:, start : start + WIDTH] = value_grad[i][:WIDTH].astype(BF16)
        dv_ref[:, start + WIDTH : start + PAIRS] = value_grad[i][WIDTH:].astype(BF16)
        slope = jnp.sum(pulled[i] * updates[i], axis=1, keepdims=True) / (1.0 + jnp.exp(logit[i]))
        dlogit_ref[pl.ds(first + i, 1), :] = row_of(slope)
        query_grad = forward[i][:WIDTH] + by_state[i][:WIDTH]
        query_grad = query_scale[i] * (
            query_grad - query[i] * jnp.sum(query[i] * query_grad, axis=1, keepdims=True)
        )
        dq_ref[:, i * WIDTH : (i + 1) * WIDTH] = query_grad.astype(BF16)
        key_grad = forward[i][WIDTH:] + backward[i] + by_end[i] + by_state[i][WIDTH:]
        key_grad = key_scale[i] * (
            key_grad - key[i] * jnp.sum(key[i] * key_grad, axis=1, keepdims=True)
        )
        dk_ref[:, start : start + WIDTH] = key_grad[:WIDTH].astype(BF16)
        dk_ref[:, start + WIDTH : start + PAIRS] = key_grad[WIDTH:].astype(BF16)


def pull(place, queries, keys, logits, reads, wy, state, end, head_grad):
    return call(
        pull_kernel,
        2,
        [
            by_columns(WIDTH),
            by_columns(PAIRS),
            whole(4, PAIRS),
            by_pair(PAIRS, PAIRS),
            by_pair(PAIRS, PAIRS),
            by_slot(WIDTH, WIDTH),
            by_slot(WIDTH, WIDTH),
            by_columns(WIDTH),
        ],
        [by_columns(WIDTH), by_columns(PAIRS), by_columns(PAIRS), whole(4, PAIRS)],
        [
            arr(BF16, WIDTH, 512),
            arr(BF16, WIDTH, 1024),
            arr(BF16, WIDTH, 1024),
            arr(F32, 4, PAIRS),
        ],
        4 * 14 * 2 * PAIRS**3,
        5 << 20,
    )(place, queries, keys, logits, reads, wy, state, end, head_grad)


def mul(a, b):
    return jnp.einsum("hij,hjk->hik", a, b, preferred_element_type=F32)


def mul_t(a, b):
    return jnp.einsum("hji,hjk->hik", a, b, preferred_element_type=F32)


def halves(x):
    return x[:, :, :WIDTH], x[:, :, WIDTH:]


def forward_states(place, mine, theirs, index, core, grad_full, weight):
    theirs = exchange(theirs, 1)
    even = jnp.where(core == 0, mine, theirs)
    odd = jnp.where(core == 0, theirs, mine)
    even_a, even_b = halves(even)
    odd_a, odd_b = halves(odd)
    joined = mul(odd_a, even)
    chip = jnp.concatenate(
        [joined[:, :, :WIDTH], joined[:, :, WIDTH:] + odd_b.astype(F32)], axis=2
    ).astype(BF16)
    total, levels = chip, []
    diagonal = jnp.broadcast_to(jnp.eye(WIDTH, dtype=BF16), (2, WIDTH, WIDTH))
    for bit in (2, 4, 8):
        came = exchange(total, bit)
        if bit == 8:
            grad_other, came = lax.optimization_barrier((exchange(grad_full, 1), came))
        upper = (index & bit) != 0
        left, right = jnp.where(upper, came, total), jnp.where(upper, total, came)
        right_a, right_b = halves(right)
        step = mul(right_a, left)
        total = jnp.concatenate(
            [step[:, :, :WIDTH], step[:, :, WIDTH:] + right_b.astype(F32)], axis=2
        ).astype(BF16)
        came_a, came_b = halves(came)
        if not levels:
            levels.append((bit, left[:, :, :WIDTH], None))
            before, state = jnp.where(upper, came_a, diagonal), jnp.where(upper, came_b, 0.0)
            state = state.astype(F32)
            after = jnp.where(upper, diagonal, came_a)
        else:
            levels.append((bit, left[:, :, :WIDTH], after))
            step = mul(before, came)
            before = jnp.where(upper, step[:, :, :WIDTH].astype(BF16), before)
            state = jnp.where(upper, state + step[:, :, WIDTH:], state)
            after = jnp.where(upper, after, mul(came_a, after).astype(BF16))
    weight, total = lax.optimization_barrier((weight, total))
    far = send(total[:, :, WIDTH:], 16)
    kept_grad, given_grad = head_gradient(place, grad_full, grad_other, weight)
    kept_grad, given_grad, far = lax.optimization_barrier((kept_grad, given_grad, far))
    head_grad = (kept_grad, exchange(given_grad, 1))
    first = (state + mul(before, far)).astype(BF16)
    second = (mul(even_a, first) + even_b.astype(F32)).astype(BF16)
    kept = jnp.where(core == 0, first, second)
    given = jnp.where(core == 0, second, first)
    state_in = jnp.concatenate([kept, exchange(given, 1)], axis=0)
    return grad_full, grad_other, head_grad, state_in, (even_a, odd_a, levels, after)


def backward_states(mine, theirs, index, core, saved, gate, last):
    even_a, odd_a, levels, after = saved
    theirs = exchange(theirs, 1)
    even = jnp.where(core == 0, mine, theirs)
    odd = jnp.where(core == 0, theirs, mine)
    total = (even.astype(F32) + mul_t(even_a, odd)).astype(BF16)
    for bit, left_a, window in levels:
        came = exchange(total, bit)
        upper = (index & bit) != 0
        if window is None:
            gate, came = lax.optimization_barrier((gate, came))
            second = jnp.where(upper, 0.0, came.astype(F32))
        else:
            second = jnp.where(upper, second, second + mul_t(window, came))
        left, right = jnp.where(upper, came, total), jnp.where(upper, total, came)
        total = (left.astype(F32) + mul_t(left_a, right)).astype(BF16)
    second = second + mul_t(after, send(total, -16))
    second = second.astype(BF16)
    first = (odd.astype(F32) + mul_t(odd_a, second)).astype(BF16)
    kept = jnp.where(core == 0, first, second)
    given = jnp.where(core == 0, second, first)
    end = jnp.concatenate([kept, exchange(given, 1)], axis=0)
    last, end = lax.optimization_barrier((last, end))
    return gate, last, end


def local(queries, keys, values, beta_logit, out_weight, out_grad):
    index = lax.axis_index("ctx")
    core = index & 1
    place = jnp.stack([core, index >> 4]).astype(jnp.int32)
    rings = [[(half * 8 + z) * 2 + c for z in range(8)] for half in range(2) for c in range(2)]
    operands = (queries, keys, values, beta_logit)
    across = exchange(out_weight, 16)
    theirs, *filled = prepare(place, *operands, False)
    across, theirs = lax.optimization_barrier((across, theirs))
    weight_pair = jnp.stack([out_weight, across])
    weight_pair, *operands = lax.optimization_barrier((weight_pair, *operands))
    mine, reads, wy, qt, local_out = prepare(place, *operands, True, filled)
    weight_mine = lax.all_gather(weight_pair, "ctx", axis=0, axis_index_groups=rings)
    grad_full = lax.all_to_all(
        jnp.broadcast_to(out_grad[None], (8, WIDTH, 512)), "tp", 0, 0, tiled=True
    )
    grad_full, grad_other, head_grad, state, saved = forward_states(
        place, mine, theirs, index, core, grad_full, weight_mine
    )
    heads, head_grad, own, own_theirs = head_outputs(place, qt, local_out, state, *head_grad)
    heads_other = exchange(heads, 1)
    terms = weight_terms(place, grad_full, grad_other, heads, heads_other)
    ring_sum = lax.psum_scatter(
        terms, "ctx", scatter_dimension=0, axis_index_groups=rings
    ).reshape(2, WIDTH, 512)
    parts = mixed_parts(place, heads, heads_other, weight_mine)
    parts, ring_sum, end = backward_states(own, own_theirs, index, core, saved, parts, ring_sum)
    across = exchange(ring_sum[1], 16)
    parts = lax.all_to_all(parts, "tp", 0, 0, tiled=True)
    query_grad, key_grad, value_grad, logit_grad = pull(
        place, queries, keys, beta_logit, reads, wy, state, end, head_grad
    )
    parts, across, query_grad = lax.optimization_barrier((parts, across, query_grad))
    weight_grad = ring_sum[0].astype(F32) + across.astype(F32)
    sums = jnp.sum(parts.astype(F32), axis=0).astype(BF16)
    kept, came = sums[:WIDTH], exchange(sums[WIDTH:], 1)
    first, second = jnp.where(core == 0, kept, came), jnp.where(core == 0, came, kept)
    mixed = jnp.concatenate(
        [first[:, :WIDTH], second[:, :WIDTH], first[:, WIDTH:], second[:, WIDTH:]], axis=1
    )
    return mixed, query_grad, key_grad, value_grad, logit_grad, weight_grad


def solution(mesh):
    placed = P("ctx", "tp")
    return jax.shard_map(
        local,
        mesh=mesh,
        in_specs=(placed, placed, placed, P("tp", "ctx"), placed, placed),
        out_specs=(placed, placed, placed, placed, P("tp", "ctx"), placed),
        check_vma=False,
    )
```
